128 devices in a mesh: rep: 16 (over y, z_hi, core), shard: 8 (over z_lo, x).
Axes of the slice: x: 4, y: 4, z: 4 (z_hi: 2, z_lo: 2; z = z_hi * 2 + z_lo), core: 2. Of those that a mesh axis runs over, the one named last changes fastest.
Arguments:
- tokens: bfloat16 [32, 1024, 768], P(None, ('rep', 'shard')), may hold values from -6 to 6
- out_grad: bfloat16 [32, 1024, 768], P(None, ('rep', 'shard')), may hold values from -6 to 6
- lengths: int32 [32], replicated, may hold values from 256 to 1024, as said below
- ln1_gain: bfloat16 [768], P('shard'), may hold values from 0.5 to 1.5
- ln1_bias: bfloat16 [768], P('shard'), may hold values from -3 to 3
- w_qkv: bfloat16 [768, 2304], P('shard'), may hold values from -0.21875 to 0.21875
- q_bias: bfloat16 [768], P('shard'), may hold values from -3 to 3
- v_bias: bfloat16 [768], P('shard'), may hold values from -0.59765625 to 0.59765625
- w_proj: bfloat16 [768, 768], P('shard'), may hold values from -3 to 3
- proj_bias: bfloat16 [768], P('shard'), may hold values from -4 to 4
- ln2_gain: bfloat16 [768], P('shard'), may hold values from 0.5 to 1.5
- ln2_bias: bfloat16 [768], P('shard'), may hold values from -3 to 3
- w_fc: bfloat16 [768, 3072], P('shard'), may hold values from -0.21875 to 0.21875
- fc_bias: bfloat16 [3072], P('shard'), may hold values from -3 to 3
- w_out: bfloat16 [3072, 768], P('shard'), may hold values from -0.625 to 0.625
- out_bias: bfloat16 [768], P('shard'), may hold values from -4 to 4
Outputs:
- block_out: bfloat16 [32, 1024, 768], P(None, ('rep', 'shard'))
- in_grad: bfloat16 [32, 1024, 768], P(None, ('rep', 'shard'))
- grad_ln1_gain: float32 [768], P('shard')
- grad_ln1_bias: float32 [768], P('shard')
- grad_w_qkv: float32 [768, 2304], P('shard')
- grad_q_bias: float32 [768], P('shard')
- grad_v_bias: float32 [768], P('shard')
- grad_w_proj: float32 [768, 768], P('shard')
- grad_proj_bias: float32 [768], P('shard')
- grad_ln2_gain: float32 [768], P('shard')
- grad_ln2_bias: float32 [768], P('shard')
- grad_w_fc: float32 [768, 3072], P('shard')
- grad_fc_bias: float32 [3072], P('shard')
- grad_w_out: float32 [3072, 768], P('shard')
- grad_out_bias: float32 [768], P('shard')
The draws below stay inside these ranges and needn't reach their ends.
Inputs may be any that keep to these rules, and one draw needn't show every extreme that they name: `lengths`: at least one sequence has all 1024 positions live.
All inputs are finite; a program needn't handle non-finite values.
Results may differ from the reference program's by a relative error of at most 0.025.
Values may be sent and summed in bfloat16 or wider, within the bound.
A program may use at most 128 MiB of HBM per device.

```python
import math
import jax
import jax.numpy as jnp
from jax import lax

D = 768
HEADS = 12
FF = 3072
LAYERS = 12
SLOT = 1024
NSEQ = 32


def draw_lengths(key, part):
    length_key = jax.random.fold_in(key, 11)
    chosen_key = jax.random.fold_in(key, 23)
    values = jax.random.randint(length_key, (NSEQ,), SLOT // 4, SLOT + 1, dtype=jnp.int32)
    chosen = jax.random.randint(chosen_key, (), 0, NSEQ, dtype=jnp.int32)
    return values.at[chosen].set(SLOT)


def level_of(rng, extent, shards, smallest, top_value):
    level = 1.0
    for axis_at, blocks in shards:
        draws = jax.random.uniform(jax.random.fold_in(jax.random.fold_in(rng, 6), axis_at), (blocks,), jnp.float32, smallest / len(shards), top_value / len(shards))
        level = level * jnp.repeat(jnp.exp(draws), extent[axis_at] // blocks).reshape((-1,) + (1,) * (len(extent) - 1 - axis_at))
    return level


def normal_values(rng, dims, scale, limit, shards=(), kind=jnp.bfloat16):
    array = jax.random.normal(rng, dims, jnp.float32) * scale
    if len(shards) > 0:
        array = level_of(rng, dims, shards, -0.22, 0.18) * array
    return jnp.clip(array, min=-limit, max=limit).astype(kind)


def setup_inputs(seed: int = 0) -> dict:
    key_of = jax.random.split(jax.random.key(seed), 17)
    tokens = normal_values(key_of[0], (NSEQ, SLOT, D), 1.0, 6.0, ((1, 128),))
    out_grad = normal_values(key_of[1], (NSEQ, SLOT, D), 1.0, 6.0, ((1, 128),))
    lengths = draw_lengths(jax.random.fold_in(key_of[16], 71), 0)
    ln1_gain = jnp.clip(1.0 + 0.1 * jax.random.normal(key_of[3], (D,), jnp.float32), 0.5, 1.5).astype(jnp.bfloat16)
    ln1_bias = normal_values(key_of[4], (D,), 0.5, 3.0, ((0, 8),))
    w_qkv = normal_values(key_of[5], (D, 3 * D), D ** -0.5, 0.21875, ((0, 8),))
    q_bias = normal_values(key_of[6], (D,), 0.5, 3.0, ((0, 8),))
    v_bias = normal_values(key_of[7], (D,), 0.1, 0.59765625, ((0, 8),))
    w_proj = normal_values(key_of[8], (D, D), 4 ** -0.5, 3.0, ((0, 8),))
    proj_bias = normal_values(key_of[9], (D,), 1.0, 4.0, ((0, 8),))
    ln2_gain = jnp.clip(1.0 + 0.1 * jax.random.normal(key_of[10], (D,), jnp.float32), 0.5, 1.5).astype(jnp.bfloat16)
    ln2_bias = normal_values(key_of[11], (D,), 0.5, 3.0, ((0, 8),))
    w_fc = normal_values(key_of[12], (D, FF), D ** -0.5, 0.21875, ((0, 8),))
    fc_bias = normal_values(key_of[13], (FF,), 0.5, 3.0, ((0, 8),))
    w_out = normal_values(key_of[14], (FF, D), (FF // 32) ** -0.5, 0.625, ((0, 8),))
    out_bias = normal_values(key_of[15], (D,), 1.0, 4.0, ((0, 8),))
    return {"tokens": tokens, "out_grad": out_grad, "lengths": lengths, "ln1_gain": ln1_gain, "ln1_bias": ln1_bias, "w_qkv": w_qkv, "q_bias": q_bias, "v_bias": v_bias, "w_proj": w_proj, "proj_bias": proj_bias, "ln2_gain": ln2_gain, "ln2_bias": ln2_bias, "w_fc": w_fc, "fc_bias": fc_bias, "w_out": w_out, "out_bias": out_bias}


@jax.custom_vjp
def low(v):
    return lax.optimization_barrier(v.astype(jnp.bfloat16)).astype(jnp.float32)

@jax.custom_vjp
def low_back(v):
    return v

def low_keep(v):
    return (low(v), None)

def low_pass(kept, grad):
    return (grad,)

def back_keep(v):
    return (v, None)

def back_low(kept, grad):
    return (low(grad),)
low.defvjp(low_keep, low_pass)
low_back.defvjp(back_keep, back_low)
EPSILON = 1e-05
MASKED = -1e+30

def layer_norm(values, gain, shift):
    centered = values - lax.optimization_barrier(jnp.mean(values, axis=-1, keepdims=True))
    spread = lax.optimization_barrier(jnp.mean(centered * centered, axis=-1, keepdims=True))
    return centered * lax.rsqrt(spread + EPSILON) * gain + shift

def product(left, right):
    return jnp.dot(left, right, precision=lax.Precision.HIGHEST)

def sequence_block(x_seq, length, params):
    ln1_gain, ln1_bias, w_qkv, q_bias, v_bias, w_proj, proj_bias, ln2_gain, ln2_bias, w_fc, fc_bias, w_out, out_bias = params
    head_dim = D // HEADS
    score_scale = 1.0 / math.sqrt(head_dim)
    branch_scale = 1.0 / math.sqrt(LAYERS)
    first_in = low(layer_norm(x_seq, ln1_gain, ln1_bias))
    projected = product(first_in, w_qkv)
    queries = low_back(low(projected[:, :D] + q_bias))
    key_rows = low_back(low(projected[:, D:2 * D]))
    value_rows = low_back(low(projected[:, 2 * D:] + v_bias))
    q_heads = queries.reshape(SLOT, HEADS, head_dim)
    k_heads = key_rows.reshape(SLOT, HEADS, head_dim)
    v_heads = value_rows.reshape(SLOT, HEADS, head_dim)
    raw_scores = jnp.einsum('qhd,khd->hqk', q_heads, k_heads, precision=lax.Precision.HIGHEST) * score_scale
    scores = low_back(raw_scores)
    positions = jnp.arange(SLOT)
    visible = (positions[None, :] <= positions[:, None]) & (positions[None, :] < length)
    attn_probs = jax.nn.softmax(jnp.where(visible[None], scores, MASKED), axis=-1)
    attn_mix = jnp.einsum('hqk,khd->qhd', low(attn_probs), v_heads, precision=lax.Precision.HIGHEST).reshape(SLOT, D)
    mixed_low = low_back(low(attn_mix))
    attn_out = low_back(product(mixed_low, w_proj) + proj_bias)
    resid = x_seq + branch_scale * attn_out
    second_in = low(layer_norm(resid, ln2_gain, ln2_bias))
    up_rows = low_back(product(second_in, w_fc) + fc_bias)
    hidden = low(jax.nn.gelu(up_rows, approximate=True))
    mlp_out = low_back(product(hidden, w_out) + out_bias)
    return resid + branch_scale * mlp_out

def reference(tokens, out_grad, lengths, ln1_gain, ln1_bias, w_qkv, q_bias, v_bias, w_proj, proj_bias, ln2_gain, ln2_bias, w_fc, fc_bias, w_out, out_bias):
    params = (ln1_gain.astype(jnp.float32), ln1_bias.astype(jnp.float32), w_qkv.astype(jnp.float32), q_bias.astype(jnp.float32), v_bias.astype(jnp.float32), w_proj.astype(jnp.float32), proj_bias.astype(jnp.float32), ln2_gain.astype(jnp.float32), ln2_bias.astype(jnp.float32), w_fc.astype(jnp.float32), fc_bias.astype(jnp.float32), w_out.astype(jnp.float32), out_bias.astype(jnp.float32))

    def forward(x_all, weights):

        def one_sequence(inputs):
            return sequence_block(inputs[0], inputs[1], weights)
        return lax.map(jax.checkpoint(one_sequence), (x_all, lengths))
    block_rows, pullback = jax.vjp(forward, tokens.astype(jnp.float32), params)
    grad_x, grad_params = pullback(out_grad.astype(jnp.float32))
    grad_ln1_gain, grad_ln1_bias, grad_w_qkv, grad_q_bias, grad_v_bias, grad_w_proj, grad_proj_bias, grad_ln2_gain, grad_ln2_bias, grad_w_fc, grad_fc_bias, grad_w_out, grad_out_bias = grad_params
    return (block_rows.astype(jnp.bfloat16), grad_x.astype(jnp.bfloat16), grad_ln1_gain, grad_ln1_bias, grad_w_qkv, grad_q_bias, grad_v_bias, grad_w_proj, grad_proj_bias, grad_ln2_gain, grad_ln2_bias, grad_w_fc, grad_fc_bias, grad_w_out, grad_out_bias)
```

```python
import functools
import math

import jax
import jax.numpy as jnp
from jax import lax
from jax.experimental import pallas as pl
from jax.experimental.pallas import tpu as pltpu
from jax.sharding import PartitionSpec as P

HEADS = 12
LAYERS = 12
EPSILON = 1e-05
MASKED = -1e30
MESH = pl.DeviceIdType.MESH
BF = jnp.bfloat16
F32 = jnp.float32
ALPHA = 1.0 / math.sqrt(LAYERS)
ROOT = math.sqrt(2.0 / math.pi)
CUBE = 0.044715
NT = (((1,), (1,)), ((), ()))
PAIR = (0, 2, 3, 5)
SINGLE = (1, 1, 4, 4)


def mm(a, b):
    return jnp.dot(a, b, preferred_element_type=F32)


def mm_nt(a, b):
    return lax.dot_general(a, b, NT, preferred_element_type=F32)


def mean(v):
    return jnp.mean(v, axis=-1, keepdims=True)


def normalize(v):
    centered = v - mean(v)
    rstd = lax.rsqrt(mean(centered * centered) + EPSILON)
    return centered * rstd, rstd


def norm_back(n, rstd, r):
    return (r - mean(r) - n * mean(r * n)) * rstd


def column_sum(v):
    return jnp.sum(v, axis=0, keepdims=True)


def roll_half(v):
    return pltpu.roll(v, 64, 1)


def place(x, y, z, c):
    return (y * 4 + (z // 2) * 2 + c, lax.rem(z, 2) * 4 + x)


def remote(src, dst, send, recv, device):
    return pltpu.make_async_remote_copy(
        src_ref=src, dst_ref=dst, send_sem=send, recv_sem=recv, device_id=device, device_id_type=MESH
    )


def arrived(ref, sem):
    pltpu.make_async_copy(ref, ref, sem).wait()


def block_kernel(
    tok, cot, lens, smi, wq_s, wp_s, wf_s, wo_s,
    bo, ig, gw, sgo,
    wq, wp, wf, wo, gall, r0, r2, r3, pmat, qh, kh, vh, goh, kt, vt, msg, rcv, osnd, orcv, grcv, tmp,
    yv, acc1, acc2, smr, sm, fbs, fbg, sg, sgr, a1v, a2v, gmv, lt1, lt2, ov, g3, hv,
    ag_s, ag_r, ag_l, sm_s, sm_r, aa_s, aa_r, c_s, c_r, d_s, d_r, fin_s, fin_r, t_s, t_r,
):
    rep, sh = lax.axis_index("rep"), lax.axis_index("shard")
    me = rep * 8 + sh
    x, zl, y, c = lax.rem(sh, 4), sh // 4, rep // 4, lax.rem(rep, 2)
    z = lax.rem(rep // 2, 2) * 2 + zl
    sibling = place(x, y, z, 1 - c)

    def ring(v, k):
        return lax.rem(v + k + 4, 4)

    def along(dim, value):
        return place(*[value if d == dim else v for d, v in enumerate((x, y, z))], c)

    own = (x, y, z)

    barrier = pltpu.get_barrier_semaphore()

    def greet(step, carry):
        peer = lax.rem(me + step, 128)
        pl.semaphore_signal(
            barrier, inc=1, device_id=(peer // 8, lax.rem(peer, 8)), device_id_type=MESH
        )
        return carry

    lax.fori_loop(1, 128, greet, 0)
    pl.semaphore_wait(barrier, 127)

    def rows16(start, size):
        return pl.ds(pl.multiple_of(start, 16), size)

    def gathered(m, s, core, h):
        if m == 0:
            return wq.at[rows16(s * 96 + core * 48, 48), pl.ds(h * 1152, 1152)]
        if m == 1:
            return wp.at[rows16(s * 96 + core * 48, 48), pl.ds(h * 384, 384)]
        if m == 2:
            return wf.at[pl.ds(h * 4, 4), pl.ds(s * 6 + core * 3, 3)]
        return wo.at[s, pl.ds(h * 24 + core * 12, 12)]

    def shard_of(m, core, h):
        if m == 0:
            return wq_s.at[rows16(core * 48, 48), pl.ds(h * 1152, 1152)]
        if m == 1:
            return wp_s.at[rows16(core * 48, 48), pl.ds(h * 384, 384)]
        if m == 2:
            return wf_s.at[pl.ds(h * 4, 4), pl.ds(core * 3, 3)]
        return wo_s.at[pl.ds(h * 24 + core * 12, 12)]

    def from_x(k):
        return zl * 4 + ring(x, -k)

    def from_z(j):
        return (1 - zl) * 4 + ring(x, -j)

    def own_copies(m):
        return [
            pltpu.make_async_copy(
                shard_of(m, core, h), gathered(m, sh, core, h), ag_l.at[m, core * 2 + h]
            )
            for core in (0, 1)
            for h in (0, 1)
        ]

    def beside(h):
        return along(2, ring(z, 1 - 2 * h))

    def gather_start(m):
        for copy in own_copies(m):
            copy.start()
        for h in (0, 1):
            remote(
                shard_of(m, c, h), gathered(m, sh, c, h), ag_s.at[m, 6 + h], ag_r.at[m, 6 + h], beside(h)
            ).start()
            for k in (1, 3, 2):
                i = (k - 1) * 2 + h
                remote(
                    shard_of(m, c, h), gathered(m, sh, c, h), ag_s.at[m, i], ag_r.at[m, i],
                    along(0, ring(x, k)),
                ).start()

    def gather_relay_x(m):
        for k in (1, 3, 2):
            for h in (0, 1):
                i = (k - 1) * 2 + h
                piece = gathered(m, from_x(k), c, h)
                arrived(piece, ag_r.at[m, i])
                i = 6 + 2 * k + h
                remote(piece, piece, ag_s.at[m, i], ag_r.at[m, i], beside(h)).start()
                i = 14 + (k - 1) * 2 + h
                remote(piece, piece, ag_s.at[m, i], ag_r.at[m, i], sibling).start()

    def gather_relay_z(m):
        for j in (0, 1, 3, 2):
            for h in (0, 1):
                piece = gathered(m, from_z(j), c, h)
                arrived(piece, ag_r.at[m, 6 + 2 * j + h])
                i = 20 + 2 * j + h
                remote(piece, piece, ag_s.at[m, i], ag_r.at[m, i], sibling).start()

    def gather_finish(m):
        for copy in own_copies(m):
            copy.wait()
        for h in (0, 1):
            for k in (1, 2, 3):
                arrived(gathered(m, from_x(k), 1 - c, h), ag_r.at[m, 14 + (k - 1) * 2 + h])
            for j in range(4):
                arrived(gathered(m, from_z(j), 1 - c, h), ag_r.at[m, 20 + 2 * j + h])

    def gather_drain(m):
        for h in (0, 1):
            for i in range(0, 28, 2):
                arrived(shard_of(m, 0, h), ag_s.at[m, i + h])

    def exchange_start(src, dst, i):
        def send(step, carry):
            peer = lax.rem(me + step, 128)
            remote(
                src.at[peer], dst.at[me], aa_s.at[i], aa_r.at[i], (peer // 8, lax.rem(peer, 8))
            ).start()
            return carry

        lax.fori_loop(1, 128, send, 0)
        dst[pl.ds(me, 1)] = src[pl.ds(me, 1)]

    def exchange_wait(dst, i):
        most = dst.at[pl.ds(0, 127)]
        arrived(most, aa_r.at[i])

    def exchange_drain(src, i):
        most = src.at[pl.ds(0, 127)]
        arrived(most, aa_s.at[i])

    lane = lax.broadcasted_iota(jnp.int32, (1, 128), 1)
    low = lane < 64
    half = lax.rem(me, 2)
    here = (lane >= half * 64) & (lane < half * 64 + 64)

    def lanes(i, count=1):
        return pl.ds(i * 128, count * 128)

    def put_groups(dst, b, per_group):
        stacked = jnp.stack([g.reshape(32, 8, 128) for g in per_group], axis=1)
        dst[:, :, b * 128 : (b + 1) * 128] = stacked.reshape(128, 8, 128).astype(BF)

    def get_groups(src, b):
        v = src[:, :, b * 128 : (b + 1) * 128].astype(F32).reshape(32, 4, 8, 128)
        return [v[:, g].reshape(256, 128) for g in range(4)]

    def put_positions(dst, b, v):
        dst[:, :, b * 128 : (b + 1) * 128] = v.reshape(128, 8, 128).astype(BF)

    def get_positions(src, b):
        return src[:, :, b * 128 : (b + 1) * 128].astype(F32).reshape(1024, 128)

    for k in range(1, 8):
        remote(
            smi, smr.at[sh], sm_s.at[k - 1], sm_r.at[k - 1], (rep, lax.rem(sh + k, 8))
        ).start()
    smr[pl.ds(sh, 1)] = smi[...].reshape(1, 16, 768)
    for m in range(4):
        gather_start(m)
    for k in range(1, 8):
        arrived(smr.at[lax.rem(sh + 8 - k, 8)], sm_r.at[k - 1])
    sm[...] = jnp.sum(smr[...].astype(F32), axis=0)
    for q in range(8):
        fbs[q] = jnp.broadcast_to(sm[8 + q // 2 : 9 + q // 2, (q % 2) * 384 : (q % 2) * 384 + 384], (8, 384))
    x_in = tok[...].astype(F32).reshape(256, 768)
    n1, rstd1 = normalize(x_in)
    a1 = n1 * sm[0:1, :] + sm[1:2, :]
    a1v[...] = a1.astype(BF)
    gather_relay_x(0)
    gather_relay_z(0)
    gather_finish(0)

    for b in range(9):
        v = mm(a1v[...], wq[:, b * 256 : (b + 1) * 256])
        if b < 3:
            v = v + sm[2:3, b * 256 : (b + 1) * 256]
        if b >= 6:
            v = v + sm[3:4, (b - 6) * 256 : (b - 5) * 256]
        tmp[pl.ds(b * 512, 256)] = v[:, :128]
        tmp[pl.ds(b * 512 + 256, 256)] = v[:, 128:]

    def natural(which, b):
        return tmp[pl.ds((which * 6 + b) * 256, 256)]

    for which in range(3):
        put_groups(msg, which, [natural(which, PAIR[g]) for g in range(4)])
    packed = []
    for g in range(4):
        qb, kb = natural(0, SINGLE[g]), natural(1, SINGLE[g])
        packed.append(
            jnp.where(low, qb, roll_half(kb)) if g % 2 == 0 else jnp.where(low, roll_half(qb), kb)
        )
    put_groups(msg, 3, packed)
    put_groups(msg, 4, [natural(2, SINGLE[g]) for g in range(4)])
    exchange_start(msg, rcv, 0)
    for m in range(1, 4):
        gather_relay_x(m)
        gather_relay_z(m)
    exchange_wait(rcv, 0)

    q01, k01, v01, qks, vs = [get_positions(rcv, b) for b in range(5)]
    zero = jnp.zeros((1024, 128), F32)
    for h, (qq, kk, vv, mask, vmask) in enumerate(
        (
            (q01, k01, v01, low, low),
            (q01, k01, v01, ~low, ~low),
            (qks, roll_half(qks), vs, low, here),
        )
    ):
        qh[h] = jnp.where(mask, qq * 0.125, zero).astype(BF)
        kk = jnp.where(mask, kk, zero)
        kh[h] = kk.astype(BF)
        kt[h] = jnp.transpose(kk).astype(BF)
        vv = jnp.where(vmask, vv, zero)
        vh[h] = vv.astype(BF)
        vt[h] = jnp.transpose(vv).astype(BF)
    length = lens[me // 4]
    offsets = (0, 256, 768, 1536)
    tmp[pl.ds(0, 2048)] = jnp.zeros((2048, 128), F32)

    def attend(h, carry):
        for i in range(4):
            n = (i + 1) * 256
            s = mm_nt(kh[h, :n, :], qh[h, i * 256 : n, :])
            key = lax.broadcasted_iota(jnp.int32, (n, 256), 0)
            limit = lax.broadcasted_iota(jnp.int32, (1, 256), 1) + (i * 256 + 1)
            s = jnp.where(key < jnp.minimum(limit, length), s, MASKED)
            e = jnp.exp(s - jnp.max(s, axis=0, keepdims=True))
            p = (e * (1.0 / jnp.sum(e, axis=0, keepdims=True))).astype(BF)
            pmat[h, offsets[i] : offsets[i] + n, :] = p
            o = jnp.transpose(mm(vt[h, :, :n], p))
            tmp[pl.ds((h // 2) * 1024 + i * 256, 256)] += o
        return carry

    lax.fori_loop(0, 3, attend, 0)
    put_positions(osnd, 0, tmp[pl.ds(0, 1024)])
    put_positions(osnd, 1, tmp[pl.ds(1024, 1024)])
    exchange_start(osnd, orcv, 1)
    for m in range(1, 4):
        gather_finish(m)
    exchange_wait(orcv, 1)

    pairs, singles = get_groups(orcv, 0), get_groups(orcv, 1)
    blocks = [None] * 6
    for g in range(4):
        blocks[PAIR[g]] = pairs[g]
    blocks[1], blocks[4] = singles[0] + singles[1], singles[2] + singles[3]
    for b in range(6):
        ov[:, b * 128 : (b + 1) * 128] = blocks[b].astype(BF)
    x_in = tok[...].astype(F32).reshape(256, 768)
    g_in = cot[...].astype(F32).reshape(256, 768)
    y_mid = x_in + ALPHA * (mm(ov[...], wp[...]) + sm[4:5, :])
    yv[...] = y_mid
    n2, rstd2 = normalize(y_mid)
    a2 = n2 * sm[5:6, :] + sm[6:7, :]
    a2v[...] = a2.astype(BF)
    gm = (ALPHA * g_in).astype(BF)
    gmv[...] = gm
    gm = gm.astype(F32)
    sg[7:8, :] = column_sum(gm)
    lt1[...] = jnp.transpose(a2v[...].astype(F32)).astype(BF)
    lt2[...] = jnp.transpose(gm).astype(BF)
    acc1[...] = jnp.zeros((256, 768), F32)
    acc2[...] = jnp.zeros((256, 768), F32)

    def color(k, ux, uy, uz):
        order = ((ux, uy, uz), (uy, uz, ux), (uz, ux, uy))[k]
        return order[0], order[1] * 4 + order[2]

    def put_columns(m, q, v):
        uy, zq = lax.rem(q, 4), q // 4
        for s in range(8):
            for core in range(2):
                for k in range(3):
                    r = s * 96 + core * 48 + k * 16
                    a, u = color(k, s % 4, uy, zq * 2 + s // 4)
                    gall[core, m * 12 + k * 4 + a, u] = v[r : r + 16]

    def put_rows(m, q, v):
        ux, zq = lax.rem(q, 4), q // 4
        for core in range(2):
            for e in range(8):
                for k in range(3):
                    r = core * 384 + e * 48 + k * 16
                    a, u = color(k, ux, e % 4, (e // 4) * 2 + zq)
                    gall[core, m * 12 + k * 4 + a, u] = v[r : r + 16]

    def feed(q, carry):
        w1 = wf[q].reshape(768, 384)
        w2a, w2b = wo[q, 0:24].reshape(384, 384), wo[q, 24:48].reshape(384, 384)
        u = mm(a2v[...], w1) + fbs[q, 0:1, :]
        uu = u * u
        t = jnp.tanh(ROOT * (u + CUBE * (u * uu)))
        hidden = (0.5 * u * (1.0 + t)).astype(BF)
        slope = 0.5 * (1.0 + t) + 0.5 * u * (1.0 - t * t) * (ROOT * (1.0 + (3.0 * CUBE) * uu))
        hv[0] = hidden
        acc1[:, 0:384] += mm(hidden, w2a)
        acc1[:, 384:768] += mm(hidden, w2b)
        gh = mm_nt(gmv[:, 0:384], w2a) + mm_nt(gmv[:, 384:768], w2b)
        gu = (gh * slope).astype(BF)
        hv[1] = gu
        fbg[q] = jnp.broadcast_to(column_sum(gu.astype(F32)), (8, 384))
        acc2[...] += mm_nt(gu, w1)
        put_columns(1, q, mm(lt1[...], hv[1]).astype(BF))
        put_rows(2, q, mm(lt2[...], hv[0]).astype(BF))
        return carry

    lax.fori_loop(0, 8, feed, 0)
    block = yv[...] + ALPHA * (acc1[...] + sm[7:8, :])
    bo[...] = block.reshape(32, 8, 768).astype(BF)
    for q in range(8):
        sg[8 + q // 2 : 9 + q // 2, (q % 2) * 384 : (q % 2) * 384 + 384] = fbg[q, 0:1, :]
    sg[12:16, :] = jnp.zeros((4, 768), F32)
    n2, rstd2 = normalize(yv[...])
    ga2 = acc2[...]
    sg[5:6, :] = column_sum(ga2 * n2)
    sg[6:7, :] = column_sum(ga2)
    gyy = cot[...].astype(F32).reshape(256, 768) + norm_back(n2, rstd2, ga2 * sm[5:6, :])
    acc1[...] = gyy
    ga = (ALPHA * gyy).astype(BF)
    a2v[...] = ga
    sg[4:5, :] = column_sum(ga.astype(F32))
    lt1[...] = jnp.transpose(ov[...].astype(F32)).astype(BF)
    for q in (6, 7):
        put_columns(0, q, mm(lt1[...], a2v[:, (q - 6) * 384 : (q - 5) * 384]).astype(BF))
    go = mm_nt(a2v[...], wp[...])
    exchange_drain(osnd, 1)
    for m in range(4):
        gather_drain(m)
    put_groups(osnd, 0, [go[:, PAIR[g] * 128 : PAIR[g] * 128 + 128] for g in range(4)])
    put_groups(osnd, 1, [go[:, SINGLE[g] * 128 : SINGLE[g] * 128 + 128] for g in range(4)])
    exchange_start(osnd, grcv, 2)
    lt1[...] = jnp.transpose(a1v[...].astype(F32)).astype(BF)
    exchange_wait(grcv, 2)

    go01, gos = get_positions(grcv, 0), get_positions(grcv, 1)
    goh[0] = jnp.where(low, go01, zero).astype(BF)
    goh[1] = jnp.where(low, zero, go01).astype(BF)
    goh[2] = jnp.where(here, gos, zero).astype(BF)
    tmp[...] = jnp.zeros((6144, 128), F32)

    def attend_back(h, carry):
        base = (h // 2) * 1024
        for i in range(4):
            n = (i + 1) * 256
            g_rows = goh[h, i * 256 : n, :]
            p = pmat[h, offsets[i] : offsets[i] + n, :]
            pf = p.astype(F32)
            gp = mm_nt(vh[h, :n, :], g_rows)
            inner = jnp.sum(pf * gp, axis=0, keepdims=True)
            gs = (pf * (gp - inner)).astype(BF)
            tmp[pl.ds(base + i * 256, 256)] += jnp.transpose(mm(kt[h, :, :n], gs)) * 0.125
            tmp[pl.ds(2048 + base, n)] += mm(gs, qh[h, i * 256 : n, :])
            tmp[pl.ds(4096 + base, n)] += mm(p, g_rows)
        return carry

    lax.fori_loop(0, 3, attend_back, 0)
    exchange_drain(msg, 0)
    for b in range(3):
        put_positions(msg, b, tmp[pl.ds(b * 2048, 1024)])
    put_positions(msg, 3, tmp[pl.ds(1024, 1024)] + roll_half(tmp[pl.ds(3072, 1024)]))
    put_positions(msg, 4, tmp[pl.ds(5120, 1024)])
    exchange_start(msg, rcv, 3)
    exchange_wait(rcv, 3)

    got = [get_groups(rcv, b) for b in range(5)]
    for which in range(3):
        blocks = [None] * 6
        for g in range(4):
            blocks[PAIR[g]] = got[which][g]
        for b, e, o in ((1, 0, 1), (4, 2, 3)):
            if which == 0:
                blocks[b] = jnp.where(low, got[3][e], roll_half(got[3][o]))
            elif which == 1:
                blocks[b] = jnp.where(low, roll_half(got[3][e]), got[3][o])
            else:
                blocks[b] = got[4][e] + got[4][o]
        for b in range(6):
            at = which * 768 + b * 128
            g3[:, at : at + 128] = blocks[b].astype(BF)
            if which != 1:
                row = 2 if which == 0 else 3
                sg[row : row + 1, b * 128 : b * 128 + 128] = column_sum(blocks[b])

    def qkv_grad(q, carry):
        cols = g3[:, pl.ds(pl.multiple_of(q * 384, 128), 384)]
        put_columns(0, q, mm(lt1[...], cols).astype(BF))
        return carry

    lax.fori_loop(0, 6, qkv_grad, 0)
    ga1 = mm_nt(g3[...], wq[...])
    n1, rstd1 = normalize(tok[...].astype(F32).reshape(256, 768))
    sg[0:1, :] = column_sum(ga1 * n1)
    sg[1:2, :] = column_sum(ga1)
    gx = acc1[...] + norm_back(n1, rstd1, ga1 * sm[0:1, :])
    ig[...] = gx.reshape(32, 8, 768).astype(BF)

    def block0(m, k, a):
        if m == 0:
            i = k * 4 + a
            return wo.at[i // 3, pl.ds(lax.rem(i, 3) * 16, 16)]
        return r0.at[(m - 1) * 12 + k * 4 + a]

    def block1(m, k, off):
        i = k * 3 + off - 1
        if m == 0:
            return wo.at[4 + i // 3, pl.ds((i % 3) * 16, 16)]
        return wf.at[(m - 1) * 4 + i // 3, pl.ds((i % 3) * 16, 16)]

    def core_start(m):
        for off in (1, 2, 3, 0):
            for k in range(3):
                a = ring(own[k], off)
                i = (m * 3 + k) * 4 + off
                remote(
                    gall.at[1 - c, m * 12 + k * 4 + a], block0(m, k, a), c_s.at[i], c_r.at[i], sibling
                ).start()

    def stage1_start(m):
        for off in (1, 2, 3):
            for k in range(3):
                a = ring(own[k], off)
                i = (m * 3 + k) * 4 + off
                arrived(block0(m, k, a), c_r.at[i])
                mine = gall.at[c, m * 12 + k * 4 + a]
                mine[...] = (mine[...].astype(F32) + block0(m, k, a)[...].astype(F32)).astype(BF)
                i = (m * 3 + k) * 3 + off - 1
                remote(
                    mine, block1(m, k, off), d_s.at[0, i], d_r.at[0, i], along(k, a)
                ).start()

    def stage2_start(m):
        for k in range(3):
            a = own[k]
            arrived(block0(m, k, a), c_r.at[(m * 3 + k) * 4])
            mine = gall.at[c, m * 12 + k * 4 + a]
            total = mine[...].astype(F32) + block0(m, k, a)[...].astype(F32)
            for off in (1, 2, 3):
                i = (m * 3 + k) * 3 + off - 1
                arrived(block1(m, k, off), d_r.at[0, i])
                total = total + block1(m, k, off)[...].astype(F32)
            mine[...] = total.astype(BF)
            dim = (k + 1) % 3
            for off in (1, 2, 3):
                i = (m * 3 + k) * 3 + off - 1
                b = ring(own[dim], off)
                remote(
                    mine.at[pl.ds(b * 4, 4)], r2.at[i], d_s.at[1, i], d_r.at[1, i], along(dim, b)
                ).start()

    def stage3_start(m):
        for k in range(3):
            mine = gall.at[c, m * 12 + k * 4 + own[k], pl.ds(own[(k + 1) % 3] * 4, 4)]
            total = mine[...].astype(F32)
            for off in (1, 2, 3):
                i = (m * 3 + k) * 3 + off - 1
                arrived(r2.at[i], d_r.at[1, i])
                total = total + r2[i].astype(F32)
            mine[...] = total.astype(BF)
            dim = (k + 2) % 3
            for off in (1, 2, 3):
                i = (m * 3 + k) * 3 + off - 1
                e = ring(own[dim], off)
                remote(mine.at[e], r3.at[i], d_s.at[2, i], d_r.at[2, i], along(dim, e)).start()

    def share_start(m):
        for k in range(3):
            u = own[(k + 1) % 3] * 4 + own[(k + 2) % 3]
            total = gall[c, m * 12 + k * 4 + own[k], u].astype(F32)
            for off in (1, 2, 3):
                i = (m * 3 + k) * 3 + off - 1
                arrived(r3.at[i], d_r.at[2, i])
                total = total + r3[i].astype(F32)
            gw[m, rep, k] = total.astype(BF)
        for k in range(1, 16):
            remote(
                gw.at[m, rep], gw.at[m, rep], fin_s.at[m, k - 1], fin_r.at[m, k - 1],
                (lax.rem(rep + k, 16), sh),
            ).start()

    def share_finish(m):
        for k in range(1, 16):
            arrived(gw.at[m, lax.rem(rep + 16 - k, 16)], fin_r.at[m, k - 1])

    def sums_drain(m):
        for k in range(3):
            for off in range(4):
                arrived(r0.at[0], c_s.at[(m * 3 + k) * 4 + off])
            for off in range(3):
                i = (m * 3 + k) * 3 + off
                arrived(r0.at[0], d_s.at[0, i])
                arrived(r2.at[0], d_s.at[1, i])
                arrived(r3.at[0], d_s.at[2, i])
        for k in range(15):
            arrived(gw.at[m, 0], fin_s.at[m, k])

    def vectors_start(stage):
        if stage == 0:
            remote(sg, sgr.at[12], t_s.at[9], t_r.at[9], sibling).start()
            return
        dim = stage - 1
        slot = dim * 4 + own[dim]
        sgr[pl.ds(slot, 1)] = sg[...].reshape(1, 16, 768)
        for off in (1, 2, 3):
            i = dim * 3 + off - 1
            remote(
                sgr.at[slot], sgr.at[slot], t_s.at[i], t_r.at[i], along(dim, ring(own[dim], off))
            ).start()

    def vectors_finish(stage):
        if stage == 0:
            arrived(sgr.at[12], t_r.at[9])
            arrived(sg, t_s.at[9])
            sg[...] = sg[...] + sgr[12]
            return
        dim = stage - 1
        for off in (1, 2, 3):
            i = dim * 3 + off - 1
            arrived(sgr.at[dim * 4 + ring(own[dim], -off)], t_r.at[i])
        sg[...] = (sgr[dim * 4] + sgr[dim * 4 + 1]) + (sgr[dim * 4 + 2] + sgr[dim * 4 + 3])

    for m in (0, 1, 2):
        core_start(m)
    vectors_start(0)
    for m in (0, 1, 2):
        stage1_start(m)
    vectors_finish(0)
    vectors_start(1)
    for m in (0, 1, 2):
        stage2_start(m)
    vectors_finish(1)
    vectors_start(2)
    for m in (0, 1, 2):
        stage3_start(m)
    vectors_finish(2)
    vectors_start(3)
    for m in (0, 1, 2):
        share_start(m)
    vectors_finish(3)
    sgo[...] = sg[...]
    for m in (0, 1, 2):
        share_finish(m)

    for k in range(7):
        arrived(smi, sm_s.at[k])
    exchange_drain(osnd, 2)
    exchange_drain(msg, 3)
    for m in range(3):
        sums_drain(m)
    for i in range(9):
        arrived(sgr.at[0], t_s.at[i])


def block_step(tok, cot, lens, smi, wq_s, wp_s, wf_s, wo_s):
    vmem = pl.BlockSpec(memory_space=pltpu.VMEM)
    smem = pl.BlockSpec(memory_space=pltpu.SMEM)
    anywhere = pl.BlockSpec(memory_space=pl.ANY)
    V, D = pltpu.VMEM, pltpu.SemaphoreType.DMA
    return pl.pallas_call(
        block_kernel,
        name="block",
        out_shape=(
            jax.ShapeDtypeStruct((32, 8, 768), BF),
            jax.ShapeDtypeStruct((32, 8, 768), BF),
            jax.ShapeDtypeStruct((3, 16, 3, 16, 384), BF),
            jax.ShapeDtypeStruct((16, 768), F32),
        ),
        in_specs=[vmem, vmem, smem, vmem, anywhere, anywhere, anywhere, anywhere],
        out_specs=(vmem, vmem, vmem, vmem),
        scratch_shapes=[
            V((768, 2304), BF),
            V((768, 768), BF),
            V((8, 48, 16, 384), BF),
            V((8, 48, 16, 384), BF),
            V((2, 36, 16, 16, 384), BF),
            V((24, 16, 16, 384), BF),
            V((27, 4, 16, 384), BF),
            V((27, 16, 384), BF),
            V((3, 2560, 256), BF),
            V((3, 1024, 128), BF),
            V((3, 1024, 128), BF),
            V((3, 1024, 128), BF),
            V((3, 1024, 128), BF),
            V((3, 128, 1024), BF),
            V((3, 128, 1024), BF),
            V((128, 8, 640), BF),
            V((128, 8, 640), BF),
            V((128, 8, 256), BF),
            V((128, 8, 256), BF),
            V((128, 8, 256), BF),
            V((6144, 128), F32),
            V((256, 768), F32),
            V((256, 768), F32),
            V((256, 768), F32),
            V((8, 16, 768), BF),
            V((16, 768), F32),
            V((8, 8, 384), F32),
            V((8, 8, 384), F32),
            V((16, 768), F32),
            V((13, 16, 768), F32),
            V((256, 768), BF),
            V((256, 768), BF),
            V((256, 768), BF),
            V((768, 256), BF),
            V((768, 256), BF),
            V((256, 768), BF),
            V((256, 2304), BF),
            V((2, 256, 384), BF),
            D((4, 28)), D((4, 28)), D((4, 4)),
            D((7,)), D((7,)),
            D((4,)), D((4,)),
            D((36,)), D((36,)),
            D((3, 27)), D((3, 27)),
            D((3, 15)), D((3, 15)),
            D((10,)), D((10,)),
        ],
        compiler_params=pltpu.CompilerParams(
            collective_id=0, has_side_effects=True, vmem_limit_bytes=64 * 2**20
        ),
    )(tok, cot, lens, smi, wq_s, wp_s, wf_s, wo_s)


def per_device(
    tokens,
    out_grad,
    lengths,
    ln1_gain,
    ln1_bias,
    w_qkv,
    q_bias,
    v_bias,
    w_proj,
    proj_bias,
    ln2_gain,
    ln2_bias,
    w_fc,
    fc_bias,
    w_out,
    out_bias,
):
    sh = lax.axis_index("shard")
    vectors = jnp.stack(
        [ln1_gain, ln1_bias, q_bias, v_bias, proj_bias, ln2_gain, ln2_bias, out_bias]
    )
    column = lax.broadcasted_iota(jnp.int32, (8, 768), 1)
    vectors = jnp.where(column // 96 == sh, jnp.tile(vectors, (1, 8)), jnp.zeros((), BF))
    place384 = lax.broadcasted_iota(jnp.int32, (8, 768), 0) * 2 + column // 384
    wide = jnp.where(place384 == sh, jnp.tile(fc_bias[None, :], (8, 2)), jnp.zeros((), BF))
    smi = jnp.concatenate([vectors, wide], axis=0)
    wf_s = w_fc.reshape(6, 16, 8, 384).transpose(2, 0, 1, 3)
    wo_s = w_out.reshape(24, 16, 2, 384).transpose(2, 0, 1, 3).reshape(48, 16, 384)
    block, in_grad, gw, sg = block_step(tokens, out_grad, lengths, smi, w_qkv, w_proj, wf_s, wo_s)
    gw = gw.reshape(3, 4, 2, 2, 3, 16, 384)
    wide = gw[:2].transpose(0, 3, 4, 5, 2, 1, 6).reshape(2, 96, 3072).astype(F32)
    tall = gw[2].transpose(2, 1, 0, 3, 4, 5).reshape(768, 384).astype(F32)
    rows = lax.dynamic_slice(sg[:8], (0, sh * 96), (8, 96))
    d_fb = lax.dynamic_slice(sg[8:12].reshape(3072), (sh * 384,), (384,))
    return (
        block,
        in_grad,
        rows[0],
        rows[1],
        wide[0, :, :2304],
        rows[2],
        rows[3],
        wide[0, :, 2304:],
        rows[4],
        rows[5],
        rows[6],
        wide[1],
        d_fb,
        tall.T,
        rows[7],
    )


def solution(mesh):
    pieces = P(None, ("rep", "shard"), None)
    row, table = P("shard"), P("shard", None)
    kinds = (row, row, table, row, row, table, row, row, row, table, row, table, row)
    return jax.shard_map(
        per_device,
        mesh=mesh,
        in_specs=(pieces, pieces, P(), *kinds),
        out_specs=(pieces, pieces, *kinds),
        check_vma=False,
    )
```

```python
import functools
import math

import jax
import jax.numpy as jnp
from jax import lax
from jax.experimental import pallas as pl
from jax.experimental.pallas import tpu as pltpu
from jax.sharding import PartitionSpec as P

HEADS = 12
LAYERS = 12
EPSILON = 1e-05
MASKED = -1e30
MESH = pl.DeviceIdType.MESH
BF = jnp.bfloat16
F32 = jnp.float32
ALPHA = 1.0 / math.sqrt(LAYERS)
ROOT = math.sqrt(2.0 / math.pi)
CUBE = 0.044715
NT = (((1,), (1,)), ((), ()))
PAIR = (0, 2, 3, 5)
SINGLE = (1, 1, 4, 4)


def mm(a, b):
    return jnp.dot(a, b, preferred_element_type=F32)


def mm_nt(a, b):
    return lax.dot_general(a, b, NT, preferred_element_type=F32)


def mean(v):
    return jnp.mean(v, axis=-1, keepdims=True)


def normalize(v):
    centered = v - mean(v)
    rstd = lax.rsqrt(mean(centered * centered) + EPSILON)
    return centered * rstd, rstd


def norm_back(n, rstd, r):
    return (r - mean(r) - n * mean(r * n)) * rstd


def column_sum(v):
    return jnp.sum(v, axis=0, keepdims=True)


def roll_half(v):
    return pltpu.roll(v, 64, 1)


def place(x, y, z, c):
    return (y * 4 + (z // 2) * 2 + c, lax.rem(z, 2) * 4 + x)


def remote(src, dst, send, recv, device):
    return pltpu.make_async_remote_copy(
        src_ref=src, dst_ref=dst, send_sem=send, recv_sem=recv, device_id=device, device_id_type=MESH
    )


def arrived(ref, sem):
    pltpu.make_async_copy(ref, ref, sem).wait()


def block_kernel(
    tok, cot, lens, smi, wq_s, wp_s, wf_s, wo_s,
    bo, ig, gq_o, gp_o, gf_o, go_t, sgo, fbo,
    wq, wp, wf, wo, gw, gall, r0, r2, r3, pmat, qh, kh, vh, goh, turned, msg, rcv, osnd, orcv, grcv, tmp,
    yv, acc1, acc2, smr, sm, fbs, fbg, sg, sgr, a1v, a2v, gmv, lt1, lt2, ov, g3, hv,
    ag_s, ag_r, ag_l, sm_s, sm_r, aa_s, aa_r, c_s, c_r, d_s, d_r, fin_s, fin_r, t_s, t_r,
):
    rep, sh = lax.axis_index("rep"), lax.axis_index("shard")
    me = rep * 8 + sh
    x, zl, y, c = lax.rem(sh, 4), sh // 4, rep // 4, lax.rem(rep, 2)
    z = lax.rem(rep // 2, 2) * 2 + zl
    sibling = place(x, y, z, 1 - c)

    def ring(v, k):
        return lax.rem(v + k + 4, 4)

    def along(dim, value):
        return place(*[value if d == dim else v for d, v in enumerate((x, y, z))], c)

    own = (x, y, z)

    barrier = pltpu.get_barrier_semaphore()

    def greet(step, carry):
        peer = lax.rem(me + step, 128)
        pl.semaphore_signal(
            barrier, inc=1, device_id=(peer // 8, lax.rem(peer, 8)), device_id_type=MESH
        )
        return carry

    lax.fori_loop(1, 128, greet, 0)
    pl.semaphore_wait(barrier, 127)

    def rows16(start, size):
        return pl.ds(pl.multiple_of(start, 16), size)

    def gathered(m, s, core, h):
        if m == 0:
            return wq.at[rows16(s * 96 + core * 48, 48), pl.ds(h * 1152, 1152)]
        if m == 1:
            return wp.at[rows16(s * 96 + core * 48, 48), pl.ds(h * 384, 384)]
        if m == 2:
            return wf.at[pl.ds(h * 4, 4), pl.ds(s * 6 + core * 3, 3)]
        return wo.at[s, pl.ds(h * 24 + core * 12, 12)]

    def shard_of(m, core, h):
        if m == 0:
            return wq_s.at[rows16(core * 48, 48), pl.ds(h * 1152, 1152)]
        if m == 1:
            return wp_s.at[rows16(core * 48, 48), pl.ds(h * 384, 384)]
        return gathered(m, sh, core, h)

    def from_x(k):
        return zl * 4 + ring(x, -k)

    def from_z(j):
        return (1 - zl) * 4 + ring(x, -j)

    def own_copies(m):
        if m == 2:
            return [
                pltpu.make_async_copy(
                    wf_s.at[:, :, pl.ds(q * 384, 384)], wf.at[q, pl.ds(sh * 6, 6)], ag_l.at[m, q]
                )
                for q in range(8)
            ]
        if m == 3:
            return [
                pltpu.make_async_copy(
                    wo_s.at[:, :, pl.ds(h * 384, 384)], wo.at[sh, pl.ds(h * 24, 24)], ag_l.at[m, h]
                )
                for h in (0, 1)
            ]
        return [
            pltpu.make_async_copy(
                shard_of(m, core, h), gathered(m, sh, core, h), ag_l.at[m, core * 2 + h]
            )
            for core in (0, 1)
            for h in (0, 1)
        ]

    def beside(h):
        return along(2, ring(z, 1 - 2 * h))

    def gather_start(m):
        for copy in own_copies(m):
            copy.start()
        if m >= 2:
            for copy in own_copies(m):
                copy.wait()
        for h in (0, 1):
            remote(
                shard_of(m, c, h), gathered(m, sh, c, h), ag_s.at[m, 6 + h], ag_r.at[m, 6 + h], beside(h)
            ).start()
            for k in (1, 3, 2):
                i = (k - 1) * 2 + h
                remote(
                    shard_of(m, c, h), gathered(m, sh, c, h), ag_s.at[m, i], ag_r.at[m, i],
                    along(0, ring(x, k)),
                ).start()

    def gather_relay_x(m):
        for k in (1, 3, 2):
            for h in (0, 1):
                i = (k - 1) * 2 + h
                piece = gathered(m, from_x(k), c, h)
                arrived(piece, ag_r.at[m, i])
                i = 6 + 2 * k + h
                remote(piece, piece, ag_s.at[m, i], ag_r.at[m, i], beside(h)).start()
                i = 14 + (k - 1) * 2 + h
                remote(piece, piece, ag_s.at[m, i], ag_r.at[m, i], sibling).start()

    def gather_relay_z(m):
        for j in (0, 1, 3, 2):
            for h in (0, 1):
                piece = gathered(m, from_z(j), c, h)
                arrived(piece, ag_r.at[m, 6 + 2 * j + h])
                i = 20 + 2 * j + h
                remote(piece, piece, ag_s.at[m, i], ag_r.at[m, i], sibling).start()

    def gather_finish(m):
        if m < 2:
            for copy in own_copies(m):
                copy.wait()
        for h in (0, 1):
            for k in (1, 2, 3):
                arrived(gathered(m, from_x(k), 1 - c, h), ag_r.at[m, 14 + (k - 1) * 2 + h])
            for j in range(4):
                arrived(gathered(m, from_z(j), 1 - c, h), ag_r.at[m, 20 + 2 * j + h])

    def gather_drain(m):
        for h in (0, 1):
            for i in range(0, 28, 2):
                arrived(gathered(m, 0, 0, h), ag_s.at[m, i + h])

    def exchange_start(src, dst, i):
        def send(step, carry):
            peer = lax.rem(me + step, 128)
            remote(
                src.at[peer], dst.at[me], aa_s.at[i], aa_r.at[i], (peer // 8, lax.rem(peer, 8))
            ).start()
            return carry

        lax.fori_loop(1, 128, send, 0)
        dst[pl.ds(me, 1)] = src[pl.ds(me, 1)]

    def exchange_wait(dst, i):
        most = dst.at[pl.ds(0, 127)]
        arrived(most, aa_r.at[i])

    def exchange_drain(src, i):
        most = src.at[pl.ds(0, 127)]
        arrived(most, aa_s.at[i])

    lane = lax.broadcasted_iota(jnp.int32, (1, 128), 1)
    low = lane < 64
    half = lax.rem(me, 2)
    here = (lane >= half * 64) & (lane < half * 64 + 64)

    def lanes(i, count=1):
        return pl.ds(i * 128, count * 128)

    def put_groups(dst, b, per_group):
        stacked = jnp.stack([g.reshape(32, 8, 128) for g in per_group], axis=1)
        dst[:, :, b * 128 : (b + 1) * 128] = stacked.reshape(128, 8, 128).astype(BF)

    def get_groups(src, b):
        v = src[:, :, b * 128 : (b + 1) * 128].astype(F32).reshape(32, 4, 8, 128)
        return [v[:, g].reshape(256, 128) for g in range(4)]

    def put_positions(dst, b, v):
        dst[:, :, b * 128 : (b + 1) * 128] = v.reshape(128, 8, 128).astype(BF)

    def get_positions(src, b):
        return src[:, :, b * 128 : (b + 1) * 128].astype(F32).reshape(1024, 128)

    def block0(m, k, a):
        if m == 0:
            i = k * 4 + a
            return wo.at[i // 3, pl.ds(lax.rem(i, 3) * 16, 16)]
        return r0.at[(m - 1) * 12 + k * 4 + a]

    def block1(m, k, off):
        i = k * 3 + off - 1
        if m == 0:
            return wo.at[4 + i // 3, pl.ds((i % 3) * 16, 16)]
        return wf.at[(m - 1) * 4 + i // 3, pl.ds((i % 3) * 16, 16)]

    def core_start(m):
        for off in (1, 2, 3, 0):
            for k in range(3):
                a = ring(own[k], off)
                i = (m * 3 + k) * 4 + off
                remote(
                    gall.at[1 - c, m * 12 + k * 4 + a], block0(m, k, a), c_s.at[i], c_r.at[i], sibling
                ).start()

    def stage1_start(m):
        for off in (1, 2, 3):
            for k in range(3):
                a = ring(own[k], off)
                i = (m * 3 + k) * 4 + off
                arrived(block0(m, k, a), c_r.at[i])
                mine = gall.at[c, m * 12 + k * 4 + a]
                mine[...] = (mine[...].astype(F32) + block0(m, k, a)[...].astype(F32)).astype(BF)
                i = (m * 3 + k) * 3 + off - 1
                remote(
                    mine, block1(m, k, off), d_s.at[0, i], d_r.at[0, i], along(k, a)
                ).start()

    def stage2_start(m):
        for k in range(3):
            a = own[k]
            arrived(block0(m, k, a), c_r.at[(m * 3 + k) * 4])
            mine = gall.at[c, m * 12 + k * 4 + a]
            total = mine[...].astype(F32) + block0(m, k, a)[...].astype(F32)
            for off in (1, 2, 3):
                i = (m * 3 + k) * 3 + off - 1
                arrived(block1(m, k, off), d_r.at[0, i])
                total = total + block1(m, k, off)[...].astype(F32)
            mine[...] = total.astype(BF)
            dim = (k + 1) % 3
            for off in (1, 2, 3):
                i = (m * 3 + k) * 3 + off - 1
                b = ring(own[dim], off)
                remote(
                    mine.at[pl.ds(b * 4, 4)], r2.at[i], d_s.at[1, i], d_r.at[1, i], along(dim, b)
                ).start()

    def stage3_start(m):
        for k in range(3):
            mine = gall.at[c, m * 12 + k * 4 + own[k], pl.ds(own[(k + 1) % 3] * 4, 4)]
            total = mine[...].astype(F32)
            for off in (1, 2, 3):
                i = (m * 3 + k) * 3 + off - 1
                arrived(r2.at[i], d_r.at[1, i])
                total = total + r2[i].astype(F32)
            mine[...] = total.astype(BF)
            dim = (k + 2) % 3
            for off in (1, 2, 3):
                i = (m * 3 + k) * 3 + off - 1
                e = ring(own[dim], off)
                remote(mine.at[e], r3.at[i], d_s.at[2, i], d_r.at[2, i], along(dim, e)).start()

    def share_start(m):
        for k in range(3):
            u = own[(k + 1) % 3] * 4 + own[(k + 2) % 3]
            total = gall[c, m * 12 + k * 4 + own[k], u].astype(F32)
            for off in (1, 2, 3):
                i = (m * 3 + k) * 3 + off - 1
                arrived(r3.at[i], d_r.at[2, i])
                total = total + r3[i].astype(F32)
            gw[m, rep, k] = total.astype(BF)
        for k in range(1, 16):
            remote(
                gw.at[m, rep], gw.at[m, rep], fin_s.at[m, k - 1], fin_r.at[m, k - 1],
                (lax.rem(rep + k, 16), sh),
            ).start()

    def share_finish(m):
        for k in range(1, 16):
            arrived(gw.at[m, lax.rem(rep + 16 - k, 16)], fin_r.at[m, k - 1])

    def assemble(m):
        for r in range(16):
            e, core = (r // 2 % 2) * 4 + r // 4, r % 2
            v = gw[m, r].reshape(48, 384)
            if m == 2:
                go_t[core * 384 + e * 48 : core * 384 + e * 48 + 48, :] = v
                continue
            at = core * 48
            if m == 1:
                gf_o[at : at + 48, e * 384 : e * 384 + 384] = v
            elif e < 6:
                gq_o[at : at + 48, e * 384 : e * 384 + 384] = v
            else:
                gp_o[at : at + 48, (e - 6) * 384 : (e - 6) * 384 + 384] = v

    def sums_drain(m):
        for k in range(3):
            for off in range(4):
                arrived(r0.at[0], c_s.at[(m * 3 + k) * 4 + off])
            for off in range(3):
                i = (m * 3 + k) * 3 + off
                arrived(r0.at[0], d_s.at[0, i])
                arrived(r2.at[0], d_s.at[1, i])
                arrived(r3.at[0], d_s.at[2, i])
        for k in range(15):
            arrived(gw.at[m, 0], fin_s.at[m, k])

    def vectors_start(stage):
        if stage == 0:
            remote(sg, sgr.at[12], t_s.at[9], t_r.at[9], sibling).start()
            return
        dim = stage - 1
        slot = dim * 4 + own[dim]
        sgr[pl.ds(slot, 1)] = sg[...].reshape(1, 16, 768)
        for off in (1, 2, 3):
            i = dim * 3 + off - 1
            remote(
                sgr.at[slot], sgr.at[slot], t_s.at[i], t_r.at[i], along(dim, ring(own[dim], off))
            ).start()

    def vectors_finish(stage):
        if stage == 0:
            arrived(sgr.at[12], t_r.at[9])
            arrived(sg, t_s.at[9])
            sg[...] = sg[...] + sgr[12]
            return
        dim = stage - 1
        for off in (1, 2, 3):
            i = dim * 3 + off - 1
            arrived(sgr.at[dim * 4 + ring(own[dim], -off)], t_r.at[i])
        sg[...] = (sgr[dim * 4] + sgr[dim * 4 + 1]) + (sgr[dim * 4 + 2] + sgr[dim * 4 + 3])

    for k in range(1, 8):
        remote(
            smi, smr.at[sh], sm_s.at[k - 1], sm_r.at[k - 1], (rep, lax.rem(sh + k, 8))
        ).start()
    smr[pl.ds(sh, 1)] = smi[...].reshape(1, 16, 768)
    gather_start(0)
    for k in range(1, 8):
        arrived(smr.at[lax.rem(sh + 8 - k, 8)], sm_r.at[k - 1])
    sm[...] = jnp.sum(smr[...].astype(F32), axis=0)
    for q in range(8):
        fbs[q] = jnp.broadcast_to(sm[8 + q // 2 : 9 + q // 2, (q % 2) * 384 : (q % 2) * 384 + 384], (8, 384))
    x_in = tok[...].astype(F32).reshape(256, 768)
    n1, rstd1 = normalize(x_in)
    a1 = n1 * sm[0:1, :] + sm[1:2, :]
    a1v[...] = a1.astype(BF)
    gather_relay_x(0)
    for m in range(1, 4):
        gather_start(m)
    gather_relay_z(0)
    gather_finish(0)

    for b in range(9):
        v = mm(a1v[...], wq[:, b * 256 : (b + 1) * 256])
        if b < 3:
            v = v + sm[2:3, b * 256 : (b + 1) * 256]
        if b >= 6:
            v = v + sm[3:4, (b - 6) * 256 : (b - 5) * 256]
        tmp[pl.ds(b * 512, 256)] = v[:, :128]
        tmp[pl.ds(b * 512 + 256, 256)] = v[:, 128:]

    def natural(which, b):
        return tmp[pl.ds((which * 6 + b) * 256, 256)]

    for which in range(3):
        put_groups(msg, which, [natural(which, PAIR[g]) for g in range(4)])
    packed = []
    for g in range(4):
        qb, kb = natural(0, SINGLE[g]), natural(1, SINGLE[g])
        packed.append(
            jnp.where(low, qb, roll_half(kb)) if g % 2 == 0 else jnp.where(low, roll_half(qb), kb)
        )
    put_groups(msg, 3, packed)
    put_groups(msg, 4, [natural(2, SINGLE[g]) for g in range(4)])
    exchange_start(msg, rcv, 0)
    for m in range(1, 4):
        gather_relay_x(m)
    exchange_wait(rcv, 0)

    q01, k01, v01, qks, vs = [get_positions(rcv, b) for b in range(5)]
    zero = jnp.zeros((1024, 128), F32)
    for h, (qq, kk, vv, mask, vmask) in enumerate(
        (
            (q01, k01, v01, low, low),
            (q01, k01, v01, ~low, ~low),
            (qks, roll_half(qks), vs, low, here),
        )
    ):
        qh[h] = jnp.where(mask, qq * 0.125, zero).astype(BF)
        kk = jnp.where(mask, kk, zero)
        kh[h] = kk.astype(BF)
        vv = jnp.where(vmask, vv, zero)
        vh[h] = vv.astype(BF)
        turned[h] = jnp.transpose(vv).astype(BF)
    length = lens[me // 4]
    offsets = (0, 256, 768, 1536)
    tmp[pl.ds(0, 2048)] = jnp.zeros((2048, 128), F32)

    def attend(h, carry):
        for i in range(4):
            n = (i + 1) * 256
            s = mm_nt(kh[h, :n, :], qh[h, i * 256 : n, :])
            key = lax.broadcasted_iota(jnp.int32, (n, 256), 0)
            limit = lax.broadcasted_iota(jnp.int32, (1, 256), 1) + (i * 256 + 1)
            s = jnp.where(key < jnp.minimum(limit, length), s, MASKED)
            e = jnp.exp(s - jnp.max(s, axis=0, keepdims=True))
            p = (e * (1.0 / jnp.sum(e, axis=0, keepdims=True))).astype(BF)
            pmat[h, offsets[i] : offsets[i] + n, :] = p
            o = jnp.transpose(mm(turned[h, :, :n], p))
            tmp[pl.ds((h // 2) * 1024 + i * 256, 256)] += o
        return carry

    lax.fori_loop(0, 3, attend, 0)
    put_positions(osnd, 0, tmp[pl.ds(0, 1024)])
    put_positions(osnd, 1, tmp[pl.ds(1024, 1024)])
    exchange_start(osnd, orcv, 1)
    for h in range(3):
        turned[h] = jnp.transpose(kh[h].astype(F32)).astype(BF)
    for m in range(1, 4):
        gather_relay_z(m)
    for m in range(1, 4):
        gather_finish(m)
    exchange_wait(orcv, 1)

    pairs, singles = get_groups(orcv, 0), get_groups(orcv, 1)
    blocks = [None] * 6
    for g in range(4):
        blocks[PAIR[g]] = pairs[g]
    blocks[1], blocks[4] = singles[0] + singles[1], singles[2] + singles[3]
    for b in range(6):
        ov[:, b * 128 : (b + 1) * 128] = blocks[b].astype(BF)
    x_in = tok[...].astype(F32).reshape(256, 768)
    g_in = cot[...].astype(F32).reshape(256, 768)
    y_mid = x_in + ALPHA * (mm(ov[...], wp[...]) + sm[4:5, :])
    yv[...] = y_mid
    n2, rstd2 = normalize(y_mid)
    a2 = n2 * sm[5:6, :] + sm[6:7, :]
    a2v[...] = a2.astype(BF)
    gm = (ALPHA * g_in).astype(BF)
    gmv[...] = gm
    gm = gm.astype(F32)
    sg[7:8, :] = column_sum(gm)
    lt1[...] = jnp.transpose(a2v[...].astype(F32)).astype(BF)
    lt2[...] = jnp.transpose(gm).astype(BF)
    acc1[...] = jnp.zeros((256, 768), F32)
    acc2[...] = jnp.zeros((256, 768), F32)

    def color(k, ux, uy, uz):
        order = ((ux, uy, uz), (uy, uz, ux), (uz, ux, uy))[k]
        return order[0], order[1] * 4 + order[2]

    def put_columns(m, q, v):
        uy, zq = lax.rem(q, 4), q // 4
        for s in range(8):
            for core in range(2):
                for k in range(3):
                    r = s * 96 + core * 48 + k * 16
                    a, u = color(k, s % 4, uy, zq * 2 + s // 4)
                    gall[core, m * 12 + k * 4 + a, u] = v[r : r + 16]

    def put_rows(m, q, v):
        ux, zq = lax.rem(q, 4), q // 4
        for core in range(2):
            for e in range(8):
                for k in range(3):
                    r = core * 384 + e * 48 + k * 16
                    a, u = color(k, ux, e % 4, (e // 4) * 2 + zq)
                    gall[core, m * 12 + k * 4 + a, u] = v[r : r + 16]

    def feed(q, carry):
        w1 = wf[q].reshape(768, 384)
        w2a, w2b = wo[q, 0:24].reshape(384, 384), wo[q, 24:48].reshape(384, 384)
        u = mm(a2v[...], w1) + fbs[q, 0:1, :]
        uu = u * u
        t = jnp.tanh(ROOT * (u + CUBE * (u * uu)))
        hidden = (0.5 * u * (1.0 + t)).astype(BF)
        slope = 0.5 * (1.0 + t) + 0.5 * u * (1.0 - t * t) * (ROOT * (1.0 + (3.0 * CUBE) * uu))
        hv[0] = hidden
        acc1[:, 0:384] += mm(hidden, w2a)
        acc1[:, 384:768] += mm(hidden, w2b)
        gh = mm_nt(gmv[:, 0:384], w2a) + mm_nt(gmv[:, 384:768], w2b)
        gu = (gh * slope).astype(BF)
        hv[1] = gu
        fbg[q] = jnp.broadcast_to(column_sum(gu.astype(F32)), (8, 384))
        acc2[...] += mm_nt(gu, w1)
        put_columns(1, q, mm(lt1[...], hv[1]).astype(BF))
        put_rows(2, q, mm(lt2[...], hv[0]).astype(BF))
        return carry

    lax.fori_loop(0, 8, feed, 0)
    core_start(1)
    core_start(2)
    block = yv[...] + ALPHA * (acc1[...] + sm[7:8, :])
    bo[...] = block.reshape(32, 8, 768).astype(BF)
    for q in range(8):
        sg[8 + q // 2 : 9 + q // 2, (q % 2) * 384 : (q % 2) * 384 + 384] = fbg[q, 0:1, :]
    sg[12:16, :] = jnp.zeros((4, 768), F32)
    n2, rstd2 = normalize(yv[...])
    ga2 = acc2[...]
    sg[5:6, :] = column_sum(ga2 * n2)
    sg[6:7, :] = column_sum(ga2)
    gyy = cot[...].astype(F32).reshape(256, 768) + norm_back(n2, rstd2, ga2 * sm[5:6, :])
    acc1[...] = gyy
    ga = (ALPHA * gyy).astype(BF)
    a2v[...] = ga
    sg[4:5, :] = column_sum(ga.astype(F32))
    lt1[...] = jnp.transpose(ov[...].astype(F32)).astype(BF)
    for q in (6, 7):
        put_columns(0, q, mm(lt1[...], a2v[:, (q - 6) * 384 : (q - 5) * 384]).astype(BF))
    go = mm_nt(a2v[...], wp[...])
    exchange_drain(osnd, 1)
    for m in range(4):
        gather_drain(m)
    put_groups(osnd, 0, [go[:, PAIR[g] * 128 : PAIR[g] * 128 + 128] for g in range(4)])
    put_groups(osnd, 1, [go[:, SINGLE[g] * 128 : SINGLE[g] * 128 + 128] for g in range(4)])
    exchange_start(osnd, grcv, 2)
    lt1[...] = jnp.transpose(a1v[...].astype(F32)).astype(BF)
    exchange_wait(grcv, 2)

    for m in (1, 2):
        stage1_start(m)
    go01, gos = get_positions(grcv, 0), get_positions(grcv, 1)
    goh[0] = jnp.where(low, go01, zero).astype(BF)
    goh[1] = jnp.where(low, zero, go01).astype(BF)
    goh[2] = jnp.where(here, gos, zero).astype(BF)
    tmp[...] = jnp.zeros((6144, 128), F32)

    def attend_back(h, carry):
        base = (h // 2) * 1024
        for i in range(4):
            n = (i + 1) * 256
            g_rows = goh[h, i * 256 : n, :]
            p = pmat[h, offsets[i] : offsets[i] + n, :]
            pf = p.astype(F32)
            gp = mm_nt(vh[h, :n, :], g_rows)
            inner = jnp.sum(pf * gp, axis=0, keepdims=True)
            gs = (pf * (gp - inner)).astype(BF)
            tmp[pl.ds(base + i * 256, 256)] += jnp.transpose(mm(turned[h, :, :n], gs)) * 0.125
            tmp[pl.ds(2048 + base, n)] += mm(gs, qh[h, i * 256 : n, :])
            tmp[pl.ds(4096 + base, n)] += mm(p, g_rows)
        return carry

    lax.fori_loop(0, 3, attend_back, 0)
    exchange_drain(msg, 0)
    for b in range(3):
        put_positions(msg, b, tmp[pl.ds(b * 2048, 1024)])
    put_positions(msg, 3, tmp[pl.ds(1024, 1024)] + roll_half(tmp[pl.ds(3072, 1024)]))
    put_positions(msg, 4, tmp[pl.ds(5120, 1024)])
    exchange_start(msg, rcv, 3)
    for m in (1, 2):
        stage2_start(m)
    for m in (1, 2):
        stage3_start(m)
    exchange_wait(rcv, 3)

    for m in (1, 2):
        share_start(m)
    got = [get_groups(rcv, b) for b in range(5)]
    for which in range(3):
        blocks = [None] * 6
        for g in range(4):
            blocks[PAIR[g]] = got[which][g]
        for b, e, o in ((1, 0, 1), (4, 2, 3)):
            if which == 0:
                blocks[b] = jnp.where(low, got[3][e], roll_half(got[3][o]))
            elif which == 1:
                blocks[b] = jnp.where(low, roll_half(got[3][e]), got[3][o])
            else:
                blocks[b] = got[4][e] + got[4][o]
        for b in range(6):
            at = which * 768 + b * 128
            g3[:, at : at + 128] = blocks[b].astype(BF)
            if which != 1:
                row = 2 if which == 0 else 3
                sg[row : row + 1, b * 128 : b * 128 + 128] = column_sum(blocks[b])

    def qkv_grad(q, carry):
        cols = g3[:, pl.ds(pl.multiple_of(q * 384, 128), 384)]
        put_columns(0, q, mm(lt1[...], cols).astype(BF))
        return carry

    lax.fori_loop(0, 6, qkv_grad, 0)
    core_start(0)
    ga1 = mm_nt(g3[...], wq[...])
    n1, rstd1 = normalize(tok[...].astype(F32).reshape(256, 768))
    sg[0:1, :] = column_sum(ga1 * n1)
    sg[1:2, :] = column_sum(ga1)
    gx = acc1[...] + norm_back(n1, rstd1, ga1 * sm[0:1, :])
    ig[...] = gx.reshape(32, 8, 768).astype(BF)

    vectors_start(0)
    stage1_start(0)
    vectors_finish(0)
    vectors_start(1)
    for m in (1, 2):
        share_finish(m)
        assemble(m)
    stage2_start(0)
    vectors_finish(1)
    vectors_start(2)
    stage3_start(0)
    vectors_finish(2)
    vectors_start(3)
    share_start(0)
    vectors_finish(3)
    lead = pltpu.roll(sg[0:8, :], lax.rem(8 - sh, 8) * 96, 1)
    sgo[...] = lead[:, 0:128]
    wide = column_sum(
        jnp.where(lax.broadcasted_iota(jnp.int32, (4, 768), 0) == sh // 2, sg[8:12, :], 0.0)
    )
    fbo[...] = jnp.where(lax.rem(sh, 2) == 0, wide[:, 0:384], wide[:, 384:768])
    share_finish(0)
    assemble(0)

    for k in range(7):
        arrived(smi, sm_s.at[k])
    exchange_drain(osnd, 2)
    exchange_drain(msg, 3)
    for m in range(3):
        sums_drain(m)
    for i in range(9):
        arrived(sgr.at[0], t_s.at[i])


def block_step(tok, cot, lens, smi, wq_s, wp_s, wf_s, wo_s):
    vmem = pl.BlockSpec(memory_space=pltpu.VMEM)
    smem = pl.BlockSpec(memory_space=pltpu.SMEM)
    anywhere = pl.BlockSpec(memory_space=pl.ANY)
    V, D = pltpu.VMEM, pltpu.SemaphoreType.DMA
    return pl.pallas_call(
        block_kernel,
        name="block",
        out_shape=(
            jax.ShapeDtypeStruct((32, 8, 768), BF),
            jax.ShapeDtypeStruct((32, 8, 768), BF),
            jax.ShapeDtypeStruct((96, 2304), BF),
            jax.ShapeDtypeStruct((96, 768), BF),
            jax.ShapeDtypeStruct((96, 3072), BF),
            jax.ShapeDtypeStruct((768, 384), BF),
            jax.ShapeDtypeStruct((8, 128), F32),
            jax.ShapeDtypeStruct((1, 384), F32),
        ),
        in_specs=[vmem, vmem, smem, vmem, anywhere, anywhere, anywhere, anywhere],
        out_specs=(vmem,) * 8,
        scratch_shapes=[
            V((768, 2304), BF),
            V((768, 768), BF),
            V((8, 48, 16, 384), BF),
            V((8, 48, 16, 384), BF),
            V((3, 16, 3, 16, 384), BF),
            V((2, 36, 16, 16, 384), BF),
            V((24, 16, 16, 384), BF),
            V((27, 4, 16, 384), BF),
            V((27, 16, 384), BF),
            V((3, 2560, 256), BF),
            V((3, 1024, 128), BF),
            V((3, 1024, 128), BF),
            V((3, 1024, 128), BF),
            V((3, 1024, 128), BF),
            V((3, 128, 1024), BF),
            V((128, 8, 640), BF),
            V((128, 8, 640), BF),
            V((128, 8, 256), BF),
            V((128, 8, 256), BF),
            V((128, 8, 256), BF),
            V((6144, 128), F32),
            V((256, 768), F32),
            V((256, 768), F32),
            V((256, 768), F32),
            V((8, 16, 768), BF),
            V((16, 768), F32),
            V((8, 8, 384), F32),
            V((8, 8, 384), F32),
            V((16, 768), F32),
            V((13, 16, 768), F32),
            V((256, 768), BF),
            V((256, 768), BF),
            V((256, 768), BF),
            V((768, 256), BF),
            V((768, 256), BF),
            V((256, 768), BF),
            V((256, 2304), BF),
            V((2, 256, 384), BF),
            D((4, 28)), D((4, 28)), D((4, 8)),
            D((7,)), D((7,)),
            D((4,)), D((4,)),
            D((36,)), D((36,)),
            D((3, 27)), D((3, 27)),
            D((3, 15)), D((3, 15)),
            D((10,)), D((10,)),
        ],
        compiler_params=pltpu.CompilerParams(
            collective_id=0, has_side_effects=True, vmem_limit_bytes=64 * 2**20
        ),
    )(tok, cot, lens, smi, wq_s, wp_s, wf_s, wo_s)


def per_device(
    tokens,
    out_grad,
    lengths,
    ln1_gain,
    ln1_bias,
    w_qkv,
    q_bias,
    v_bias,
    w_proj,
    proj_bias,
    ln2_gain,
    ln2_bias,
    w_fc,
    fc_bias,
    w_out,
    out_bias,
):
    sh = lax.axis_index("shard")
    vectors = jnp.stack(
        [ln1_gain, ln1_bias, q_bias, v_bias, proj_bias, ln2_gain, ln2_bias, out_bias]
    )
    column = lax.broadcasted_iota(jnp.int32, (8, 768), 1)
    vectors = jnp.where(column // 96 == sh, jnp.tile(vectors, (1, 8)), jnp.zeros((), BF))
    place384 = lax.broadcasted_iota(jnp.int32, (8, 768), 0) * 2 + column // 384
    wide = jnp.where(place384 == sh, jnp.tile(fc_bias[None, :], (8, 2)), jnp.zeros((), BF))
    smi = jnp.concatenate([vectors, wide], axis=0)
    wf_s = w_fc.reshape(6, 16, 3072)
    wo_s = w_out.reshape(24, 16, 768)
    block, in_grad, gq, gp, gf, gt, rows, d_fb = block_step(
        tokens, out_grad, lengths, smi, w_qkv, w_proj, wf_s, wo_s
    )
    rows = rows[:, :96]
    return (
        block,
        in_grad,
        rows[0],
        rows[1],
        gq.astype(F32),
        rows[2],
        rows[3],
        gp.astype(F32),
        rows[4],
        rows[5],
        rows[6],
        gf.astype(F32),
        d_fb[0],
        gt.astype(F32).T,
        rows[7],
    )


def solution(mesh):
    pieces = P(None, ("rep", "shard"), None)
    row, table = P("shard"), P("shard", None)
    kinds = (row, row, table, row, row, table, row, row, row, table, row, table, row)
    return jax.shard_map(
        per_device,
        mesh=mesh,
        in_specs=(pieces, pieces, P(), *kinds),
        out_specs=(pieces, pieces, *kinds),
        check_vma=False,
    )
```

```python
import functools
import math

import jax
import jax.numpy as jnp
from jax import lax
from jax.experimental import pallas as pl
from jax.experimental.pallas import tpu as pltpu
from jax.sharding import PartitionSpec as P

HEADS = 12
LAYERS = 12
EPSILON = 1e-05
MASKED = -1e30
MESH = pl.DeviceIdType.MESH
BF = jnp.bfloat16
F32 = jnp.float32
ALPHA = 1.0 / math.sqrt(LAYERS)
ROOT = math.sqrt(2.0 / math.pi)
CUBE = 0.044715
NT = (((1,), (1,)), ((), ()))
PAIR = (0, 2, 3, 5)
SINGLE = (1, 1, 4, 4)


def mm(a, b):
    return jnp.dot(a, b, preferred_element_type=F32)


def mm_nt(a, b):
    return lax.dot_general(a, b, NT, preferred_element_type=F32)


def mean(v):
    return jnp.mean(v, axis=-1, keepdims=True)


def normalize(v):
    centered = v - mean(v)
    rstd = lax.rsqrt(mean(centered * centered) + EPSILON)
    return centered * rstd, rstd


def norm_back(n, rstd, r):
    return (r - mean(r) - n * mean(r * n)) * rstd


def column_sum(v):
    return jnp.sum(v, axis=0, keepdims=True)


def roll_half(v):
    return pltpu.roll(v, 64, 1)


def place(x, y, z, c):
    return (y * 4 + (z // 2) * 2 + c, lax.rem(z, 2) * 4 + x)


def remote(src, dst, send, recv, device):
    return pltpu.make_async_remote_copy(
        src_ref=src, dst_ref=dst, send_sem=send, recv_sem=recv, device_id=device, device_id_type=MESH
    )


def arrived(ref, sem):
    pltpu.make_async_copy(ref, ref, sem).wait()


def block_kernel(
    tok, cot, lens, smi, wq_s, wp_s, wf_s, wo_s,
    bo, ig, gq_o, gf_o, go_t, sgo, fbo,
    wq, wp, wf, wo, gall, r0, r2, r3, pmat, qh, kh, vh, goh, turned, msg, rcv, osnd, orcv, grcv, tmp,
    yv, acc1, acc2, smr, sm, fbs, fbg, sg, sgr, a1v, a2v, gmv, lt1, lt2, ov, g3, hv,
    ag_s, ag_r, ag_l, sm_s, sm_r, aa_s, aa_r, c_s, c_r, d_s, d_r, fin_s, fin_r, t_s, t_r,
):
    rep, sh = lax.axis_index("rep"), lax.axis_index("shard")
    me = rep * 8 + sh
    x, zl, y, c = lax.rem(sh, 4), sh // 4, rep // 4, lax.rem(rep, 2)
    z = lax.rem(rep // 2, 2) * 2 + zl
    sibling = place(x, y, z, 1 - c)

    def ring(v, k):
        return lax.rem(v + k + 4, 4)

    def along(dim, value):
        return place(*[value if d == dim else v for d, v in enumerate((x, y, z))], c)

    own = (x, y, z)

    barrier = pltpu.get_barrier_semaphore()

    def greet(step, carry):
        peer = lax.rem(me + step, 128)
        pl.semaphore_signal(
            barrier, inc=1, device_id=(peer // 8, lax.rem(peer, 8)), device_id_type=MESH
        )
        return carry

    lax.fori_loop(1, 128, greet, 0)
    pl.semaphore_wait(barrier, 127)

    def rows16(start, size):
        return pl.ds(pl.multiple_of(start, 16), size)

    def gathered(m, s, core, h):
        if m == 0:
            return wq.at[rows16(s * 96 + core * 48, 48), pl.ds(h * 1152, 1152)]
        if m == 1:
            return wp.at[rows16(s * 96 + core * 48, 48), pl.ds(h * 384, 384)]
        if m == 2:
            return wf.at[pl.ds(h * 4, 4), pl.ds(s * 6 + core * 3, 3)]
        return wo.at[s, pl.ds(h * 24 + core * 12, 12)]

    def shard_of(m, core, h):
        if m == 0:
            return wq_s.at[rows16(core * 48, 48), pl.ds(h * 1152, 1152)]
        if m == 1:
            return wp_s.at[rows16(core * 48, 48), pl.ds(h * 384, 384)]
        return gathered(m, sh, core, h)

    def from_x(k):
        return zl * 4 + ring(x, -k)

    def from_z(j):
        return (1 - zl) * 4 + ring(x, -j)

    def own_copies(m):
        if m == 2:
            return [
                pltpu.make_async_copy(
                    wf_s.at[:, :, pl.ds(q * 384, 384)], wf.at[q, pl.ds(sh * 6, 6)], ag_l.at[m, q]
                )
                for q in range(8)
            ]
        if m == 3:
            return [
                pltpu.make_async_copy(
                    wo_s.at[:, :, pl.ds(h * 384, 384)], wo.at[sh, pl.ds(h * 24, 24)], ag_l.at[m, h]
                )
                for h in (0, 1)
            ]
        return [
            pltpu.make_async_copy(
                shard_of(m, core, h), gathered(m, sh, core, h), ag_l.at[m, core * 2 + h]
            )
            for core in (0, 1)
            for h in (0, 1)
        ]

    def beside(h):
        return along(2, ring(z, 1 - 2 * h))

    def gather_start(m):
        for copy in own_copies(m):
            copy.start()
        if m >= 2:
            for copy in own_copies(m):
                copy.wait()
        for h in (0, 1):
            remote(
                shard_of(m, c, h), gathered(m, sh, c, h), ag_s.at[m, 6 + h], ag_r.at[m, 6 + h], beside(h)
            ).start()
            for k in (1, 3):
                i = (k - 1) * 2 + h
                remote(
                    shard_of(m, c, h), gathered(m, sh, c, h), ag_s.at[m, i], ag_r.at[m, i],
                    along(0, ring(x, k)),
                ).start()

    def gather_relay_x(m):
        for k, h in ((1, 0), (3, 1), (1, 1), (3, 0), (2, 0), (2, 1)):
            i = (k - 1) * 2 + h
            piece = gathered(m, from_x(k), c, h)
            arrived(piece, ag_r.at[m, i])
            if (k, h) in ((1, 0), (3, 1)):
                remote(
                    piece, piece, ag_s.at[m, 2 + h], ag_r.at[m, 2 + h], along(0, ring(x, 1 - 2 * h))
                ).start()
            i = 6 + 2 * k + h
            remote(piece, piece, ag_s.at[m, i], ag_r.at[m, i], beside(h)).start()
            i = 14 + (k - 1) * 2 + h
            remote(piece, piece, ag_s.at[m, i], ag_r.at[m, i], sibling).start()

    def gather_relay_z(m):
        for j in (0, 1, 3, 2):
            for h in (0, 1):
                piece = gathered(m, from_z(j), c, h)
                arrived(piece, ag_r.at[m, 6 + 2 * j + h])
                i = 20 + 2 * j + h
                remote(piece, piece, ag_s.at[m, i], ag_r.at[m, i], sibling).start()

    def gather_finish(m):
        if m < 2:
            for copy in own_copies(m):
                copy.wait()
        for h in (0, 1):
            for k in (1, 2, 3):
                arrived(gathered(m, from_x(k), 1 - c, h), ag_r.at[m, 14 + (k - 1) * 2 + h])
            for j in range(4):
                arrived(gathered(m, from_z(j), 1 - c, h), ag_r.at[m, 20 + 2 * j + h])

    def gather_drain(m):
        for h in (0, 1):
            for i in range(0, 28, 2):
                arrived(gathered(m, 0, 0, h), ag_s.at[m, i + h])

    def exchange_start(src, dst, i):
        def send(step, carry):
            peer = lax.rem(me + step, 128)
            remote(
                src.at[peer], dst.at[me], aa_s.at[i], aa_r.at[i], (peer // 8, lax.rem(peer, 8))
            ).start()
            return carry

        lax.fori_loop(1, 128, send, 0)
        dst[pl.ds(me, 1)] = src[pl.ds(me, 1)]

    def exchange_wait(dst, i):
        most = dst.at[pl.ds(0, 127)]
        arrived(most, aa_r.at[i])

    def exchange_drain(src, i):
        most = src.at[pl.ds(0, 127)]
        arrived(most, aa_s.at[i])

    lane = lax.broadcasted_iota(jnp.int32, (1, 128), 1)
    low = lane < 64
    half = lax.rem(me, 2)
    here = (lane >= half * 64) & (lane < half * 64 + 64)

    def lanes(i, count=1):
        return pl.ds(i * 128, count * 128)

    def put_groups(dst, b, per_group):
        stacked = jnp.stack([g.reshape(32, 8, 128) for g in per_group], axis=1)
        dst[:, :, b * 128 : (b + 1) * 128] = stacked.reshape(128, 8, 128).astype(BF)

    def get_groups(src, b):
        v = src[:, :, b * 128 : (b + 1) * 128].astype(F32).reshape(32, 4, 8, 128)
        return [v[:, g].reshape(256, 128) for g in range(4)]

    def put_positions(dst, b, v):
        dst[:, :, b * 128 : (b + 1) * 128] = v.reshape(128, 8, 128).astype(BF)

    def get_positions(src, b):
        return src[:, :, b * 128 : (b + 1) * 128].astype(F32).reshape(1024, 128)

    def block0(m, k, a):
        if m == 0:
            i = k * 4 + a
            return wo.at[i // 3, pl.ds(lax.rem(i, 3) * 16, 16)]
        return r0.at[(m - 1) * 12 + k * 4 + a]

    def block1(m, k, off):
        i = k * 3 + off - 1
        if m == 0:
            return wo.at[4 + i // 3, pl.ds((i % 3) * 16, 16)]
        return wf.at[(m - 1) * 4 + i // 3, pl.ds((i % 3) * 16, 16)]

    def core_start(m):
        for off in (1, 2, 3, 0):
            for k in range(3):
                a = ring(own[k], off)
                i = (m * 3 + k) * 4 + off
                remote(
                    gall.at[1 - c, m * 12 + k * 4 + a], block0(m, k, a), c_s.at[i], c_r.at[i], sibling
                ).start()

    def stage1_start(m):
        for off in (1, 2, 3):
            for k in range(3):
                a = ring(own[k], off)
                i = (m * 3 + k) * 4 + off
                arrived(block0(m, k, a), c_r.at[i])
                mine = gall.at[c, m * 12 + k * 4 + a]
                mine[...] = (mine[...].astype(F32) + block0(m, k, a)[...].astype(F32)).astype(BF)
                i = (m * 3 + k) * 3 + off - 1
                remote(
                    mine, block1(m, k, off), d_s.at[0, i], d_r.at[0, i], along(k, a)
                ).start()

    def stage2_start(m):
        for k in range(3):
            a = own[k]
            arrived(block0(m, k, a), c_r.at[(m * 3 + k) * 4])
            mine = gall.at[c, m * 12 + k * 4 + a]
            total = mine[...].astype(F32) + block0(m, k, a)[...].astype(F32)
            for off in (1, 2, 3):
                i = (m * 3 + k) * 3 + off - 1
                arrived(block1(m, k, off), d_r.at[0, i])
                total = total + block1(m, k, off)[...].astype(F32)
            mine[...] = total.astype(BF)
            dim = (k + 1) % 3
            for off in (1, 2, 3):
                i = (m * 3 + k) * 3 + off - 1
                b = ring(own[dim], off)
                remote(
                    mine.at[pl.ds(b * 4, 4)], r2.at[i], d_s.at[1, i], d_r.at[1, i], along(dim, b)
                ).start()

    def stage3_start(m):
        for k in range(3):
            mine = gall.at[c, m * 12 + k * 4 + own[k], pl.ds(own[(k + 1) % 3] * 4, 4)]
            total = mine[...].astype(F32)
            for off in (1, 2, 3):
                i = (m * 3 + k) * 3 + off - 1
                arrived(r2.at[i], d_r.at[1, i])
                total = total + r2[i].astype(F32)
            mine[...] = total.astype(BF)
            dim = (k + 2) % 3
            for off in (1, 2, 3):
                i = (m * 3 + k) * 3 + off - 1
                e = ring(own[dim], off)
                remote(mine.at[e], r3.at[i], d_s.at[2, i], d_r.at[2, i], along(dim, e)).start()

    def region(m, r):
        part, core = lax.rem(r // 2, 2) * 4 + r // 4, lax.rem(r, 2)
        if m == 2:
            return go_t.at[rows16(core * 384 + part * 48, 48)]
        out = gf_o if m == 1 else gq_o
        return out.at[rows16(core * 48, 48), pl.ds(pl.multiple_of(part * 384, 128), 384)]

    def share_start(m):
        for k in range(3):
            u = own[(k + 1) % 3] * 4 + own[(k + 2) % 3]
            total = gall[c, m * 12 + k * 4 + own[k], u].astype(F32)
            for off in (1, 2, 3):
                i = (m * 3 + k) * 3 + off - 1
                arrived(r3.at[i], d_r.at[2, i])
                total = total + r3[i].astype(F32)
            region(m, rep).at[pl.ds(k * 16, 16), :][...] = total.astype(BF)
        mine = region(m, rep)
        for k in range(1, 16):
            remote(
                mine, mine, fin_s.at[m, k - 1], fin_r.at[m, k - 1], (lax.rem(rep + k, 16), sh)
            ).start()

    def share_finish(m):
        for k in range(1, 16):
            arrived(region(m, lax.rem(rep + 16 - k, 16)), fin_r.at[m, k - 1])

    def sums_drain(m):
        for k in range(3):
            for off in range(4):
                arrived(r0.at[0], c_s.at[(m * 3 + k) * 4 + off])
            for off in range(3):
                i = (m * 3 + k) * 3 + off
                arrived(r0.at[0], d_s.at[0, i])
                arrived(r2.at[0], d_s.at[1, i])
                arrived(r3.at[0], d_s.at[2, i])
        for k in range(15):
            arrived(region(m, rep), fin_s.at[m, k])

    def vectors_start(stage):
        if stage == 0:
            remote(sg, sgr.at[12], t_s.at[9], t_r.at[9], sibling).start()
            return
        dim = stage - 1
        slot = dim * 4 + own[dim]
        sgr[pl.ds(slot, 1)] = sg[...].reshape(1, 16, 768)
        for off in (1, 2, 3):
            i = dim * 3 + off - 1
            remote(
                sgr.at[slot], sgr.at[slot], t_s.at[i], t_r.at[i], along(dim, ring(own[dim], off))
            ).start()

    def vectors_finish(stage):
        if stage == 0:
            arrived(sgr.at[12], t_r.at[9])
            arrived(sg, t_s.at[9])
            sg[...] = sg[...] + sgr[12]
            return
        dim = stage - 1
        for off in (1, 2, 3):
            i = dim * 3 + off - 1
            arrived(sgr.at[dim * 4 + ring(own[dim], -off)], t_r.at[i])
        sg[...] = (sgr[dim * 4] + sgr[dim * 4 + 1]) + (sgr[dim * 4 + 2] + sgr[dim * 4 + 3])

    gather_start(0)
    for k in range(1, 8):
        remote(
            smi, smr.at[sh], sm_s.at[k - 1], sm_r.at[k - 1], (rep, lax.rem(sh + k, 8))
        ).start()
    smr[pl.ds(sh, 1)] = smi[...].reshape(1, 16, 768)
    for k in range(1, 8):
        arrived(smr.at[lax.rem(sh + 8 - k, 8)], sm_r.at[k - 1])
    sm[...] = jnp.sum(smr[...].astype(F32), axis=0)
    for q in range(4):
        fbs[q] = jnp.broadcast_to(sm[8 + q : 9 + q, :], (8, 768))
    x_in = tok[...].astype(F32).reshape(256, 768)
    n1, rstd1 = normalize(x_in)
    a1 = n1 * sm[0:1, :] + sm[1:2, :]
    a1v[...] = a1.astype(BF)
    gather_relay_x(0)
    for m in range(1, 4):
        gather_start(m)
    gather_relay_z(0)
    gather_finish(0)

    for b in range(9):
        v = mm(a1v[...], wq[:, b * 256 : (b + 1) * 256])
        if b < 3:
            v = v + sm[2:3, b * 256 : (b + 1) * 256]
        if b >= 6:
            v = v + sm[3:4, (b - 6) * 256 : (b - 5) * 256]
        tmp[pl.ds(b * 512, 256)] = v[:, :128]
        tmp[pl.ds(b * 512 + 256, 256)] = v[:, 128:]

    def natural(which, b):
        return tmp[pl.ds((which * 6 + b) * 256, 256)]

    for which in range(3):
        put_groups(msg, which, [natural(which, PAIR[g]) for g in range(4)])
    packed = []
    for g in range(4):
        qb, kb = natural(0, SINGLE[g]), natural(1, SINGLE[g])
        packed.append(
            jnp.where(low, qb, roll_half(kb)) if g % 2 == 0 else jnp.where(low, roll_half(qb), kb)
        )
    put_groups(msg, 3, packed)
    put_groups(msg, 4, [natural(2, SINGLE[g]) for g in range(4)])
    exchange_start(msg, rcv, 0)
    for m in (1, 2):
        gather_relay_x(m)
    exchange_wait(rcv, 0)

    q01, k01, v01, qks, vs = [get_positions(rcv, b) for b in range(5)]
    zero = jnp.zeros((1024, 128), F32)
    for h, (qq, kk, vv, mask, vmask) in enumerate(
        (
            (q01, k01, v01, low, low),
            (q01, k01, v01, ~low, ~low),
            (qks, roll_half(qks), vs, low, here),
        )
    ):
        qh[h] = jnp.where(mask, qq * 0.125, zero).astype(BF)
        kk = jnp.where(mask, kk, zero)
        kh[h] = kk.astype(BF)
        vv = jnp.where(vmask, vv, zero)
        vh[h] = vv.astype(BF)
        turned[h] = jnp.transpose(vv).astype(BF)
    length = lens[me // 4]
    offsets = (0, 256, 768, 1536)
    tmp[pl.ds(0, 2048)] = jnp.zeros((2048, 128), F32)

    def attend(h, carry):
        for i in range(4):
            n = (i + 1) * 256
            s = mm_nt(kh[h, :n, :], qh[h, i * 256 : n, :])
            key = lax.broadcasted_iota(jnp.int32, (n, 256), 0)
            limit = lax.broadcasted_iota(jnp.int32, (1, 256), 1) + (i * 256 + 1)
            s = jnp.where(key < jnp.minimum(limit, length), s, MASKED)
            e = jnp.exp(s - jnp.max(s, axis=0, keepdims=True))
            p = (e * (1.0 / jnp.sum(e, axis=0, keepdims=True))).astype(BF)
            pmat[h, offsets[i] : offsets[i] + n, :] = p
            o = jnp.transpose(mm(turned[h, :, :n], p))
            tmp[pl.ds((h // 2) * 1024 + i * 256, 256)] += o
        return carry

    lax.fori_loop(0, 3, attend, 0)
    put_positions(osnd, 0, tmp[pl.ds(0, 1024)])
    put_positions(osnd, 1, tmp[pl.ds(1024, 1024)])
    exchange_start(osnd, orcv, 1)
    gather_relay_x(3)
    for h in range(3):
        turned[h] = jnp.transpose(kh[h].astype(F32)).astype(BF)
    for m in range(1, 4):
        gather_relay_z(m)
    for m in range(1, 4):
        gather_finish(m)
    exchange_wait(orcv, 1)

    pairs, singles = get_groups(orcv, 0), get_groups(orcv, 1)
    blocks = [None] * 6
    for g in range(4):
        blocks[PAIR[g]] = pairs[g]
    blocks[1], blocks[4] = singles[0] + singles[1], singles[2] + singles[3]
    for b in range(6):
        ov[:, b * 128 : (b + 1) * 128] = blocks[b].astype(BF)
    x_in = tok[...].astype(F32).reshape(256, 768)
    g_in = cot[...].astype(F32).reshape(256, 768)
    y_mid = x_in + ALPHA * (mm(ov[...], wp[...]) + sm[4:5, :])
    yv[...] = y_mid
    n2, rstd2 = normalize(y_mid)
    a2 = n2 * sm[5:6, :] + sm[6:7, :]
    a2v[...] = a2.astype(BF)
    gm = (ALPHA * g_in).astype(BF)
    gmv[...] = gm
    gm = gm.astype(F32)
    sg[7:8, :] = column_sum(gm)
    lt1[...] = jnp.transpose(a2v[...].astype(F32)).astype(BF)
    lt2[...] = jnp.transpose(gm).astype(BF)
    acc1[...] = jnp.zeros((256, 768), F32)
    acc2[...] = jnp.zeros((256, 768), F32)

    def color(k, ux, uy, uz):
        order = ((ux, uy, uz), (uy, uz, ux), (uz, ux, uy))[k]
        return order[0], order[1] * 4 + order[2]

    def put_columns(m, q, v, first, shards):
        uy, zq = lax.rem(q, 4), q // 4
        for s in range(first, first + shards):
            for core in range(2):
                for k in range(3):
                    r = (s - first) * 96 + core * 48 + k * 16
                    a, u = color(k, s % 4, uy, zq * 2 + s // 4)
                    gall[core, m * 12 + k * 4 + a, u] = v[r : r + 16]

    def put_rows(m, q, v, core):
        ux, zq = lax.rem(q, 4), q // 4
        for e in range(8):
            for k in range(3):
                r = e * 48 + k * 16
                a, u = color(k, ux, e % 4, (e // 4) * 2 + zq)
                gall[core, m * 12 + k * 4 + a, u] = v[r : r + 16]

    def feed(p, carry):
        left, right = 2 * p, 2 * p + 1
        w1 = jnp.concatenate([wf[q].reshape(768, 384) for q in (left, right)], axis=1)
        w2 = jnp.concatenate(
            [
                jnp.concatenate([wo[q, h * 24 : h * 24 + 24].reshape(384, 384) for h in (0, 1)], axis=1)
                for q in (left, right)
            ],
            axis=0,
        )
        u = mm(a2v[...], w1) + fbs[p, 0:1, :]
        uu = u * u
        t = jnp.tanh(ROOT * (u + CUBE * (u * uu)))
        hv[0] = (0.5 * u * (1.0 + t)).astype(BF)
        slope = 0.5 * (1.0 + t) + 0.5 * u * (1.0 - t * t) * (ROOT * (1.0 + (3.0 * CUBE) * uu))
        gu = (mm_nt(gmv[...], w2) * slope).astype(BF)
        hv[1] = gu
        fbg[p] = jnp.broadcast_to(column_sum(gu.astype(F32)), (8, 768))
        acc1[...] += mm(hv[0], w2)
        acc2[...] += mm_nt(hv[1], w1)
        for half in (0, 1):
            v = mm(lt1[half * 384 : half * 384 + 384, :], hv[1]).astype(BF)
            put_columns(1, left, v[:, 0:384], half * 4, 4)
            put_columns(1, right, v[:, 384:768], half * 4, 4)
            v = mm(lt2[half * 384 : half * 384 + 384, :], hv[0]).astype(BF)
            put_rows(2, left, v[:, 0:384], half)
            put_rows(2, right, v[:, 384:768], half)
        return carry

    lax.fori_loop(0, 4, feed, 0)
    core_start(1)
    core_start(2)
    block = yv[...] + ALPHA * (acc1[...] + sm[7:8, :])
    bo[...] = block.reshape(32, 8, 768).astype(BF)
    for q in range(4):
        sg[8 + q : 9 + q, :] = fbg[q, 0:1, :]
    sg[12:16, :] = jnp.zeros((4, 768), F32)
    n2, rstd2 = normalize(yv[...])
    ga2 = acc2[...]
    sg[5:6, :] = column_sum(ga2 * n2)
    sg[6:7, :] = column_sum(ga2)
    gyy = cot[...].astype(F32).reshape(256, 768) + norm_back(n2, rstd2, ga2 * sm[5:6, :])
    acc1[...] = gyy
    ga = (ALPHA * gyy).astype(BF)
    a2v[...] = ga
    sg[4:5, :] = column_sum(ga.astype(F32))
    lt1[...] = jnp.transpose(ov[...].astype(F32)).astype(BF)
    for half in (0, 1):
        v = mm(lt1[half * 384 : half * 384 + 384, :], a2v[...]).astype(BF)
        put_columns(0, 6, v[:, 0:384], half * 4, 4)
        put_columns(0, 7, v[:, 384:768], half * 4, 4)
    go = mm_nt(a2v[...], wp[...])
    exchange_drain(osnd, 1)
    for m in range(4):
        gather_drain(m)
    put_groups(osnd, 0, [go[:, PAIR[g] * 128 : PAIR[g] * 128 + 128] for g in range(4)])
    put_groups(osnd, 1, [go[:, SINGLE[g] * 128 : SINGLE[g] * 128 + 128] for g in range(4)])
    exchange_start(osnd, grcv, 2)
    lt1[...] = jnp.transpose(a1v[...].astype(F32)).astype(BF)
    exchange_wait(grcv, 2)

    for m in (1, 2):
        stage1_start(m)
    go01, gos = get_positions(grcv, 0), get_positions(grcv, 1)
    goh[0] = jnp.where(low, go01, zero).astype(BF)
    goh[1] = jnp.where(low, zero, go01).astype(BF)
    goh[2] = jnp.where(here, gos, zero).astype(BF)
    tmp[...] = jnp.zeros((6144, 128), F32)

    def attend_back(h, carry):
        base = (h // 2) * 1024
        for i in range(4):
            n = (i + 1) * 256
            g_rows = goh[h, i * 256 : n, :]
            p = pmat[h, offsets[i] : offsets[i] + n, :]
            pf = p.astype(F32)
            gp = mm_nt(vh[h, :n, :], g_rows)
            inner = jnp.sum(pf * gp, axis=0, keepdims=True)
            gs = (pf * (gp - inner)).astype(BF)
            tmp[pl.ds(base + i * 256, 256)] += jnp.transpose(mm(turned[h, :, :n], gs)) * 0.125
            tmp[pl.ds(2048 + base, n)] += mm(gs, qh[h, i * 256 : n, :])
            tmp[pl.ds(4096 + base, n)] += mm(p, g_rows)
        return carry

    lax.fori_loop(0, 3, attend_back, 0)
    exchange_drain(msg, 0)
    for b in range(3):
        put_positions(msg, b, tmp[pl.ds(b * 2048, 1024)])
    put_positions(msg, 3, tmp[pl.ds(1024, 1024)] + roll_half(tmp[pl.ds(3072, 1024)]))
    put_positions(msg, 4, tmp[pl.ds(5120, 1024)])
    exchange_start(msg, rcv, 3)
    exchange_wait(rcv, 3)

    got = [get_groups(rcv, b) for b in range(5)]
    for which in range(3):
        blocks = [None] * 6
        for g in range(4):
            blocks[PAIR[g]] = got[which][g]
        for b, e, o in ((1, 0, 1), (4, 2, 3)):
            if which == 0:
                blocks[b] = jnp.where(low, got[3][e], roll_half(got[3][o]))
            elif which == 1:
                blocks[b] = jnp.where(low, roll_half(got[3][e]), got[3][o])
            else:
                blocks[b] = got[4][e] + got[4][o]
        for b in range(6):
            at = which * 768 + b * 128
            g3[:, at : at + 128] = blocks[b].astype(BF)
            if which != 1:
                row = 2 if which == 0 else 3
                sg[row : row + 1, b * 128 : b * 128 + 128] = column_sum(blocks[b])

    def qkv_grad(p, carry):
        cols = g3[:, pl.ds(pl.multiple_of(p * 768, 128), 768)]
        for half in (0, 1):
            v = mm(lt1[half * 384 : half * 384 + 384, :], cols).astype(BF)
            put_columns(0, 2 * p, v[:, 0:384], half * 4, 4)
            put_columns(0, 2 * p + 1, v[:, 384:768], half * 4, 4)
        return carry

    lax.fori_loop(0, 3, qkv_grad, 0)
    core_start(0)
    for m in (1, 2):
        stage2_start(m)
    ga1 = mm_nt(g3[...], wq[...])
    n1, rstd1 = normalize(tok[...].astype(F32).reshape(256, 768))
    sg[0:1, :] = column_sum(ga1 * n1)
    sg[1:2, :] = column_sum(ga1)
    gx = acc1[...] + norm_back(n1, rstd1, ga1 * sm[0:1, :])
    ig[...] = gx.reshape(32, 8, 768).astype(BF)

    vectors_start(0)
    stage1_start(0)
    vectors_finish(0)
    vectors_start(1)
    for m in (1, 2):
        stage3_start(m)
    stage2_start(0)
    vectors_finish(1)
    vectors_start(2)
    for m in (1, 2):
        share_start(m)
    stage3_start(0)
    vectors_finish(2)
    vectors_start(3)
    share_start(0)
    vectors_finish(3)
    lead = pltpu.roll(sg[0:8, :], lax.rem(8 - sh, 8) * 96, 1)
    sgo[...] = lead[:, 0:128]
    wide = column_sum(
        jnp.where(lax.broadcasted_iota(jnp.int32, (4, 768), 0) == sh // 2, sg[8:12, :], 0.0)
    )
    fbo[...] = jnp.where(lax.rem(sh, 2) == 0, wide[:, 0:384], wide[:, 384:768])
    for m in range(3):
        share_finish(m)

    for k in range(7):
        arrived(smi, sm_s.at[k])
    exchange_drain(osnd, 2)
    exchange_drain(msg, 3)
    for m in range(3):
        sums_drain(m)
    for i in range(9):
        arrived(sgr.at[0], t_s.at[i])


def block_step(tok, cot, lens, smi, wq_s, wp_s, wf_s, wo_s):
    vmem = pl.BlockSpec(memory_space=pltpu.VMEM)
    smem = pl.BlockSpec(memory_space=pltpu.SMEM)
    anywhere = pl.BlockSpec(memory_space=pl.ANY)
    V, D = pltpu.VMEM, pltpu.SemaphoreType.DMA
    return pl.pallas_call(
        block_kernel,
        name="block",
        out_shape=(
            jax.ShapeDtypeStruct((32, 8, 768), BF),
            jax.ShapeDtypeStruct((32, 8, 768), BF),
            jax.ShapeDtypeStruct((96, 3072), BF),
            jax.ShapeDtypeStruct((96, 3072), BF),
            jax.ShapeDtypeStruct((768, 384), BF),
            jax.ShapeDtypeStruct((8, 128), F32),
            jax.ShapeDtypeStruct((1, 384), F32),
        ),
        in_specs=[vmem, vmem, smem, vmem, anywhere, anywhere, anywhere, anywhere],
        out_specs=(vmem,) * 7,
        scratch_shapes=[
            V((768, 2304), BF),
            V((768, 768), BF),
            V((8, 48, 16, 384), BF),
            V((8, 48, 16, 384), BF),
            V((2, 36, 16, 16, 384), BF),
            V((24, 16, 16, 384), BF),
            V((27, 4, 16, 384), BF),
            V((27, 16, 384), BF),
            V((3, 2560, 256), BF),
            V((3, 1024, 128), BF),
            V((3, 1024, 128), BF),
            V((3, 1024, 128), BF),
            V((3, 1024, 128), BF),
            V((3, 128, 1024), BF),
            V((128, 8, 640), BF),
            V((128, 8, 640), BF),
            V((128, 8, 256), BF),
            V((128, 8, 256), BF),
            V((128, 8, 256), BF),
            V((6144, 128), F32),
            V((256, 768), F32),
            V((256, 768), F32),
            V((256, 768), F32),
            V((8, 16, 768), BF),
            V((16, 768), F32),
            V((4, 8, 768), F32),
            V((4, 8, 768), F32),
            V((16, 768), F32),
            V((13, 16, 768), F32),
            V((256, 768), BF),
            V((256, 768), BF),
            V((256, 768), BF),
            V((768, 256), BF),
            V((768, 256), BF),
            V((256, 768), BF),
            V((256, 2304), BF),
            V((2, 256, 768), BF),
            D((4, 28)), D((4, 28)), D((4, 8)),
            D((7,)), D((7,)),
            D((4,)), D((4,)),
            D((36,)), D((36,)),
            D((3, 27)), D((3, 27)),
            D((3, 15)), D((3, 15)),
            D((10,)), D((10,)),
        ],
        compiler_params=pltpu.CompilerParams(
            collective_id=0, has_side_effects=True, vmem_limit_bytes=64 * 2**20
        ),
    )(tok, cot, lens, smi, wq_s, wp_s, wf_s, wo_s)


def per_device(
    tokens,
    out_grad,
    lengths,
    ln1_gain,
    ln1_bias,
    w_qkv,
    q_bias,
    v_bias,
    w_proj,
    proj_bias,
    ln2_gain,
    ln2_bias,
    w_fc,
    fc_bias,
    w_out,
    out_bias,
):
    sh = lax.axis_index("shard")
    vectors = jnp.stack(
        [ln1_gain, ln1_bias, q_bias, v_bias, proj_bias, ln2_gain, ln2_bias, out_bias]
    )
    column = lax.broadcasted_iota(jnp.int32, (8, 768), 1)
    vectors = jnp.where(column // 96 == sh, jnp.tile(vectors, (1, 8)), jnp.zeros((), BF))
    place384 = lax.broadcasted_iota(jnp.int32, (8, 768), 0) * 2 + column // 384
    wide = jnp.where(place384 == sh, jnp.tile(fc_bias[None, :], (8, 2)), jnp.zeros((), BF))
    smi = jnp.concatenate([vectors, wide], axis=0)
    wf_s = w_fc.reshape(6, 16, 3072)
    wo_s = w_out.reshape(24, 16, 768)
    block, in_grad, gq, gf, gt, rows, d_fb = block_step(
        tokens, out_grad, lengths, smi, w_qkv, w_proj, wf_s, wo_s
    )
    rows = rows[:, :96]
    return (
        block,
        in_grad,
        rows[0],
        rows[1],
        gq[:, :2304].astype(F32),
        rows[2],
        rows[3],
        gq[:, 2304:].astype(F32),
        rows[4],
        rows[5],
        rows[6],
        gf.astype(F32),
        d_fb[0],
        gt.astype(F32).T,
        rows[7],
    )


def solution(mesh):
    pieces = P(None, ("rep", "shard"), None)
    row, table = P("shard"), P("shard", None)
    kinds = (row, row, table, row, row, table, row, row, row, table, row, table, row)
    return jax.shard_map(
        per_device,
        mesh=mesh,
        in_specs=(pieces, pieces, P(), *kinds),
        out_specs=(pieces, pieces, *kinds),
        check_vma=False,
    )
```

```python
import functools
import math

import jax
import jax.numpy as jnp
from jax import lax
from jax.experimental import pallas as pl
from jax.experimental.pallas import tpu as pltpu
from jax.sharding import PartitionSpec as P

HEADS = 12
LAYERS = 12
EPSILON = 1e-05
MASKED = -1e30
MESH = pl.DeviceIdType.MESH
BF = jnp.bfloat16
F32 = jnp.float32
ALPHA = 1.0 / math.sqrt(LAYERS)
ROOT = math.sqrt(2.0 / math.pi)
CUBE = 0.044715
NT = (((1,), (1,)), ((), ()))
PAIR = (0, 2, 3, 5)
SINGLE = (1, 1, 4, 4)


def mm(a, b):
    return jnp.dot(a, b, preferred_element_type=F32)


def mm_nt(a, b):
    return lax.dot_general(a, b, NT, preferred_element_type=F32)


def mean(v):
    return jnp.mean(v, axis=-1, keepdims=True)


def normalize(v):
    centered = v - mean(v)
    rstd = lax.rsqrt(mean(centered * centered) + EPSILON)
    return centered * rstd, rstd


def norm_back(n, rstd, r):
    return (r - mean(r) - n * mean(r * n)) * rstd


def column_sum(v):
    return jnp.sum(v, axis=0, keepdims=True)


def roll_half(v):
    return pltpu.roll(v, 64, 1)


def place(x, y, z, c):
    return (y * 4 + (z // 2) * 2 + c, lax.rem(z, 2) * 4 + x)


def remote(src, dst, send, recv, device):
    return pltpu.make_async_remote_copy(
        src_ref=src, dst_ref=dst, send_sem=send, recv_sem=recv, device_id=device, device_id_type=MESH
    )


def arrived(ref, sem):
    pltpu.make_async_copy(ref, ref, sem).wait()


def block_kernel(
    tok, cot, lens, smi, wq_s, wp_s, wf_s, wo_s,
    bo, ig, gq_o, gf_o, go_t, sgo, fbo,
    wq, wp, wf, wo, gall, r0, r2, r3, pmat, qh, kh, vh, goh, turned, msg, rcv, osnd, orcv, grcv, tmp,
    yv, acc1, acc2, smr, sm, fbs, fbg, sg, sgr, a1v, a2v, gmv, lt1, lt2, ov, g3, hv,
    ag_s, ag_r, ag_l, sm_s, sm_r, aa_s, aa_r, c_s, c_r, d_s, d_r, fin_s, fin_r, t_s, t_r,
):
    rep, sh = lax.axis_index("rep"), lax.axis_index("shard")
    me = rep * 8 + sh
    x, zl, y, c = lax.rem(sh, 4), sh // 4, rep // 4, lax.rem(rep, 2)
    z = lax.rem(rep // 2, 2) * 2 + zl
    sibling = place(x, y, z, 1 - c)

    def ring(v, k):
        return lax.rem(v + k + 4, 4)

    def along(dim, value):
        return place(*[value if d == dim else v for d, v in enumerate((x, y, z))], c)

    own = (x, y, z)

    barrier = pltpu.get_barrier_semaphore()

    def greet(step, carry):
        peer = lax.rem(me + step, 128)
        pl.semaphore_signal(
            barrier, inc=1, device_id=(peer // 8, lax.rem(peer, 8)), device_id_type=MESH
        )
        return carry

    lax.fori_loop(1, 128, greet, 0)
    pl.semaphore_wait(barrier, 127)

    def rows16(start, size):
        return pl.ds(pl.multiple_of(start, 16), size)

    def gathered(m, s, core, h):
        if m == 0:
            return wq.at[rows16(s * 96 + core * 48, 48), pl.ds(h * 1152, 1152)]
        if m == 1:
            return wp.at[rows16(s * 96 + core * 48, 48), pl.ds(h * 384, 384)]
        if m == 2:
            return wf.at[pl.ds(h * 4, 4), pl.ds(s * 6 + core * 3, 3)]
        return wo.at[s, pl.ds(h * 24 + core * 12, 12)]

    def shard_of(m, core, h):
        if m == 0:
            return wq_s.at[rows16(core * 48, 48), pl.ds(h * 1152, 1152)]
        if m == 1:
            return wp_s.at[rows16(core * 48, 48), pl.ds(h * 384, 384)]
        return gathered(m, sh, core, h)

    def from_x(k):
        return zl * 4 + ring(x, -k)

    def from_z(j):
        return (1 - zl) * 4 + ring(x, -j)

    def own_copies(m):
        if m == 2:
            return [
                pltpu.make_async_copy(
                    wf_s.at[:, :, pl.ds(q * 384, 384)], wf.at[q, pl.ds(sh * 6, 6)], ag_l.at[m, q]
                )
                for q in range(8)
            ]
        if m == 3:
            return [
                pltpu.make_async_copy(
                    wo_s.at[:, :, pl.ds(h * 384, 384)], wo.at[sh, pl.ds(h * 24, 24)], ag_l.at[m, h]
                )
                for h in (0, 1)
            ]
        return [
            pltpu.make_async_copy(
                shard_of(m, core, h), gathered(m, sh, core, h), ag_l.at[m, core * 2 + h]
            )
            for core in (0, 1)
            for h in (0, 1)
        ]

    def beside(h):
        return along(2, ring(z, 1 - 2 * h))

    def gather_start(m):
        for copy in own_copies(m):
            copy.start()
        if m >= 2:
            for copy in own_copies(m):
                copy.wait()
        for h in (0, 1):
            remote(
                shard_of(m, c, h), gathered(m, sh, c, h), ag_s.at[m, 6 + h], ag_r.at[m, 6 + h], beside(h)
            ).start()
            for k in (1, 3):
                i = (k - 1) * 2 + h
                remote(
                    shard_of(m, c, h), gathered(m, sh, c, h), ag_s.at[m, i], ag_r.at[m, i],
                    along(0, ring(x, k)),
                ).start()

    def gather_relay_x(m):
        for k, h in ((1, 0), (3, 1), (1, 1), (3, 0), (2, 0), (2, 1)):
            i = (k - 1) * 2 + h
            piece = gathered(m, from_x(k), c, h)
            arrived(piece, ag_r.at[m, i])
            if (k, h) in ((1, 0), (3, 1)):
                remote(
                    piece, piece, ag_s.at[m, 2 + h], ag_r.at[m, 2 + h], along(0, ring(x, 1 - 2 * h))
                ).start()
            i = 6 + 2 * k + h
            remote(piece, piece, ag_s.at[m, i], ag_r.at[m, i], beside(h)).start()
            i = 14 + (k - 1) * 2 + h
            remote(piece, piece, ag_s.at[m, i], ag_r.at[m, i], sibling).start()

    def gather_relay_z(m):
        for j in (0, 1, 3, 2):
            for h in (0, 1):
                piece = gathered(m, from_z(j), c, h)
                arrived(piece, ag_r.at[m, 6 + 2 * j + h])
                i = 20 + 2 * j + h
                remote(piece, piece, ag_s.at[m, i], ag_r.at[m, i], sibling).start()

    def gather_finish(m):
        if m < 2:
            for copy in own_copies(m):
                copy.wait()
        for h in (0, 1):
            for k in (1, 2, 3):
                arrived(gathered(m, from_x(k), 1 - c, h), ag_r.at[m, 14 + (k - 1) * 2 + h])
            for j in range(4):
                arrived(gathered(m, from_z(j), 1 - c, h), ag_r.at[m, 20 + 2 * j + h])

    def gather_drain(m):
        for h in (0, 1):
            for i in range(0, 28, 2):
                arrived(gathered(m, 0, 0, h), ag_s.at[m, i + h])

    def exchange_start(src, dst, i):
        def send(step, carry):
            peer = lax.rem(me + step, 128)
            remote(
                src.at[peer], dst.at[me], aa_s.at[i], aa_r.at[i], (peer // 8, lax.rem(peer, 8))
            ).start()
            return carry

        lax.fori_loop(1, 128, send, 0)
        dst[pl.ds(me, 1)] = src[pl.ds(me, 1)]

    def exchange_wait(dst, i):
        most = dst.at[pl.ds(0, 127)]
        arrived(most, aa_r.at[i])

    def exchange_drain(src, i):
        most = src.at[pl.ds(0, 127)]
        arrived(most, aa_s.at[i])

    lane = lax.broadcasted_iota(jnp.int32, (1, 128), 1)
    low = lane < 64
    half = lax.rem(me, 2)
    here = (lane >= half * 64) & (lane < half * 64 + 64)

    def lanes(i, count=1):
        return pl.ds(i * 128, count * 128)

    def put_groups(dst, b, per_group):
        stacked = jnp.stack([g.reshape(32, 8, 128) for g in per_group], axis=1)
        dst[:, :, b * 128 : (b + 1) * 128] = stacked.reshape(128, 8, 128).astype(BF)

    def get_groups(src, b):
        v = src[:, :, b * 128 : (b + 1) * 128].astype(F32).reshape(32, 4, 8, 128)
        return [v[:, g].reshape(256, 128) for g in range(4)]

    def put_positions(dst, b, v):
        dst[:, :, b * 128 : (b + 1) * 128] = v.reshape(128, 8, 128).astype(BF)

    def get_positions(src, b):
        return src[:, :, b * 128 : (b + 1) * 128].astype(F32).reshape(1024, 128)

    def block0(m, k, a):
        if m == 0:
            i = k * 4 + a
            return wo.at[i // 3, pl.ds(lax.rem(i, 3) * 16, 16)]
        return r0.at[(m - 1) * 12 + k * 4 + a]

    def block1(m, k, off):
        i = k * 3 + off - 1
        if m == 0:
            return wo.at[4 + i // 3, pl.ds((i % 3) * 16, 16)]
        return wf.at[(m - 1) * 4 + i // 3, pl.ds((i % 3) * 16, 16)]

    def core_start(m):
        for off in (1, 2, 3, 0):
            for k in range(3):
                a = ring(own[k], off)
                i = (m * 3 + k) * 4 + off
                remote(
                    gall.at[1 - c, m * 12 + k * 4 + a], block0(m, k, a), c_s.at[i], c_r.at[i], sibling
                ).start()

    def stage1_start(m):
        for off in (1, 2, 3):
            for k in range(3):
                a = ring(own[k], off)
                i = (m * 3 + k) * 4 + off
                arrived(block0(m, k, a), c_r.at[i])
                mine = gall.at[c, m * 12 + k * 4 + a]
                mine[...] = mine[...] + block0(m, k, a)[...]
                i = (m * 3 + k) * 3 + off - 1
                remote(
                    mine, block1(m, k, off), d_s.at[0, i], d_r.at[0, i], along(k, a)
                ).start()

    def stage2_start(m):
        for k in range(3):
            a = own[k]
            arrived(block0(m, k, a), c_r.at[(m * 3 + k) * 4])
            mine = gall.at[c, m * 12 + k * 4 + a]
            total = mine[...].astype(F32) + block0(m, k, a)[...].astype(F32)
            for off in (1, 2, 3):
                i = (m * 3 + k) * 3 + off - 1
                arrived(block1(m, k, off), d_r.at[0, i])
                total = total + block1(m, k, off)[...].astype(F32)
            mine[...] = total.astype(BF)
            dim = (k + 1) % 3
            for off in (1, 2, 3):
                i = (m * 3 + k) * 3 + off - 1
                b = ring(own[dim], off)
                remote(
                    mine.at[pl.ds(b * 4, 4)], r2.at[i], d_s.at[1, i], d_r.at[1, i], along(dim, b)
                ).start()

    def stage3_start(m):
        for k in range(3):
            mine = gall.at[c, m * 12 + k * 4 + own[k], pl.ds(own[(k + 1) % 3] * 4, 4)]
            total = mine[...].astype(F32)
            for off in (1, 2, 3):
                i = (m * 3 + k) * 3 + off - 1
                arrived(r2.at[i], d_r.at[1, i])
                total = total + r2[i].astype(F32)
            mine[...] = total.astype(BF)
            dim = (k + 2) % 3
            for off in (1, 2, 3):
                i = (m * 3 + k) * 3 + off - 1
                e = ring(own[dim], off)
                remote(mine.at[e], r3.at[i], d_s.at[2, i], d_r.at[2, i], along(dim, e)).start()

    def region(m, r):
        part, core = lax.rem(r // 2, 2) * 4 + r // 4, lax.rem(r, 2)
        if m == 2:
            return go_t.at[rows16(core * 384 + part * 48, 48)]
        out = gf_o if m == 1 else gq_o
        return out.at[rows16(core * 48, 48), pl.ds(pl.multiple_of(part * 384, 128), 384)]

    def share_start(m):
        for k in range(3):
            u = own[(k + 1) % 3] * 4 + own[(k + 2) % 3]
            total = gall[c, m * 12 + k * 4 + own[k], u].astype(F32)
            for off in (1, 2, 3):
                i = (m * 3 + k) * 3 + off - 1
                arrived(r3.at[i], d_r.at[2, i])
                total = total + r3[i].astype(F32)
            region(m, rep).at[pl.ds(k * 16, 16), :][...] = total.astype(BF)
        mine = region(m, rep)
        for k in range(1, 8):
            peer = lax.rem(rep // 2 + k, 8) * 2 + c
            remote(mine, mine, fin_s.at[m, k - 1], fin_r.at[m, k - 1], (peer, sh)).start()

    def strip(m, core):
        if m == 2:
            return go_t.at[rows16(core * 384, 384)]
        return (gf_o if m == 1 else gq_o).at[rows16(core * 48, 48)]

    def share_relay(m):
        for k in range(1, 8):
            peer = lax.rem(rep // 2 + 8 - k, 8) * 2 + c
            arrived(region(m, peer), fin_r.at[m, k - 1])
        remote(strip(m, c), strip(m, c), fin_s.at[m, 7], fin_r.at[m, 7], sibling).start()

    def share_finish(m):
        arrived(strip(m, 1 - c), fin_r.at[m, 7])

    def sums_drain(m):
        for k in range(3):
            for off in range(4):
                arrived(r0.at[0], c_s.at[(m * 3 + k) * 4 + off])
            for off in range(3):
                i = (m * 3 + k) * 3 + off
                arrived(r0.at[0], d_s.at[0, i])
                arrived(r2.at[0], d_s.at[1, i])
                arrived(r3.at[0], d_s.at[2, i])
        for k in range(7):
            arrived(region(m, rep), fin_s.at[m, k])
        arrived(strip(m, c), fin_s.at[m, 7])

    def vectors_start(stage):
        if stage == 0:
            remote(sg, sgr.at[12], t_s.at[9], t_r.at[9], sibling).start()
            return
        dim = stage - 1
        slot = dim * 4 + own[dim]
        sgr[pl.ds(slot, 1)] = sg[...].reshape(1, 16, 768)
        for off in (1, 2, 3):
            i = dim * 3 + off - 1
            remote(
                sgr.at[slot], sgr.at[slot], t_s.at[i], t_r.at[i], along(dim, ring(own[dim], off))
            ).start()

    def vectors_finish(stage):
        if stage == 0:
            arrived(sgr.at[12], t_r.at[9])
            arrived(sg, t_s.at[9])
            sg[...] = sg[...] + sgr[12]
            return
        dim = stage - 1
        for off in (1, 2, 3):
            i = dim * 3 + off - 1
            arrived(sgr.at[dim * 4 + ring(own[dim], -off)], t_r.at[i])
        sg[...] = (sgr[dim * 4] + sgr[dim * 4 + 1]) + (sgr[dim * 4 + 2] + sgr[dim * 4 + 3])

    gather_start(0)
    for k in range(1, 8):
        remote(
            smi, smr.at[sh], sm_s.at[k - 1], sm_r.at[k - 1], (rep, lax.rem(sh + k, 8))
        ).start()
    smr[pl.ds(sh, 1)] = smi[...].reshape(1, 16, 768)
    for k in range(1, 8):
        arrived(smr.at[lax.rem(sh + 8 - k, 8)], sm_r.at[k - 1])
    sm[...] = jnp.sum(smr[...].astype(F32), axis=0)
    for q in range(4):
        fbs[q] = jnp.broadcast_to(sm[8 + q : 9 + q, :], (8, 768))
    x_in = tok[...].astype(F32).reshape(256, 768)
    n1, rstd1 = normalize(x_in)
    a1 = n1 * sm[0:1, :] + sm[1:2, :]
    a1v[...] = a1.astype(BF)
    gather_relay_x(0)
    for m in range(1, 4):
        gather_start(m)
    gather_relay_z(0)
    gather_finish(0)
    gather_relay_x(1)

    for b in range(9):
        v = mm(a1v[...], wq[:, b * 256 : (b + 1) * 256])
        if b < 3:
            v = v + sm[2:3, b * 256 : (b + 1) * 256]
        if b >= 6:
            v = v + sm[3:4, (b - 6) * 256 : (b - 5) * 256]
        tmp[pl.ds(b * 512, 256)] = v[:, :128]
        tmp[pl.ds(b * 512 + 256, 256)] = v[:, 128:]

    def natural(which, b):
        return tmp[pl.ds((which * 6 + b) * 256, 256)]

    for which in range(3):
        put_groups(msg, which, [natural(which, PAIR[g]) for g in range(4)])
    packed = []
    for g in range(4):
        qb, kb = natural(0, SINGLE[g]), natural(1, SINGLE[g])
        packed.append(
            jnp.where(low, qb, roll_half(kb)) if g % 2 == 0 else jnp.where(low, roll_half(qb), kb)
        )
    put_groups(msg, 3, packed)
    put_groups(msg, 4, [natural(2, SINGLE[g]) for g in range(4)])
    exchange_start(msg, rcv, 0)
    for m in (2, 3):
        gather_relay_x(m)
    exchange_wait(rcv, 0)

    q01, k01, v01, qks, vs = [get_positions(rcv, b) for b in range(5)]
    zero = jnp.zeros((1024, 128), F32)
    for h, (qq, kk, vv, mask, vmask) in enumerate(
        (
            (q01, k01, v01, low, low),
            (q01, k01, v01, ~low, ~low),
            (qks, roll_half(qks), vs, low, here),
        )
    ):
        qh[h] = jnp.where(mask, qq * 0.125, zero).astype(BF)
        kk = jnp.where(mask, kk, zero)
        kh[h] = kk.astype(BF)
        vv = jnp.where(vmask, vv, zero)
        vh[h] = vv.astype(BF)
        turned[h] = jnp.transpose(vv).astype(BF)
    length = lens[me // 4]
    offsets = (0, 256, 768, 1536)
    tmp[pl.ds(0, 2048)] = jnp.zeros((2048, 128), F32)

    def attend(h, carry):
        for i in range(4):
            n = (i + 1) * 256
            s = mm_nt(kh[h, :n, :], qh[h, i * 256 : n, :])
            key = lax.broadcasted_iota(jnp.int32, (n, 256), 0)
            limit = lax.broadcasted_iota(jnp.int32, (1, 256), 1) + (i * 256 + 1)
            s = jnp.where(key < jnp.minimum(limit, length), s, MASKED)
            e = jnp.exp(s - jnp.max(s, axis=0, keepdims=True))
            p = (e * (1.0 / jnp.sum(e, axis=0, keepdims=True))).astype(BF)
            pmat[h, offsets[i] : offsets[i] + n, :] = p
            o = jnp.transpose(mm(turned[h, :, :n], p))
            tmp[pl.ds((h // 2) * 1024 + i * 256, 256)] += o
        return carry

    lax.fori_loop(0, 3, attend, 0)
    put_positions(osnd, 0, tmp[pl.ds(0, 1024)])
    put_positions(osnd, 1, tmp[pl.ds(1024, 1024)])
    exchange_start(osnd, orcv, 1)
    for h in range(3):
        turned[h] = jnp.transpose(kh[h].astype(F32)).astype(BF)
    for m in range(1, 4):
        gather_relay_z(m)
    for m in range(1, 4):
        gather_finish(m)
    exchange_wait(orcv, 1)

    pairs, singles = get_groups(orcv, 0), get_groups(orcv, 1)
    blocks = [None] * 6
    for g in range(4):
        blocks[PAIR[g]] = pairs[g]
    blocks[1], blocks[4] = singles[0] + singles[1], singles[2] + singles[3]
    for b in range(6):
        ov[:, b * 128 : (b + 1) * 128] = blocks[b].astype(BF)
    x_in = tok[...].astype(F32).reshape(256, 768)
    g_in = cot[...].astype(F32).reshape(256, 768)
    y_mid = x_in + ALPHA * (mm(ov[...], wp[...]) + sm[4:5, :])
    yv[...] = y_mid
    n2, rstd2 = normalize(y_mid)
    a2 = n2 * sm[5:6, :] + sm[6:7, :]
    a2v[...] = a2.astype(BF)
    gm = (ALPHA * g_in).astype(BF)
    gmv[...] = gm
    gm = gm.astype(F32)
    sg[7:8, :] = column_sum(gm)
    lt1[...] = jnp.transpose(a2v[...].astype(F32)).astype(BF)
    lt2[...] = jnp.transpose(gm).astype(BF)
    acc1[...] = jnp.zeros((256, 768), F32)
    acc2[...] = jnp.zeros((256, 768), F32)

    def color(k, ux, uy, uz):
        order = ((ux, uy, uz), (uy, uz, ux), (uz, ux, uy))[k]
        return order[0], order[1] * 4 + order[2]

    def put_columns(m, q, v, first, shards):
        uy, zq = lax.rem(q, 4), q // 4
        for s in range(first, first + shards):
            for core in range(2):
                for k in range(3):
                    r = (s - first) * 96 + core * 48 + k * 16
                    a, u = color(k, s % 4, uy, zq * 2 + s // 4)
                    gall[core, m * 12 + k * 4 + a, u] = v[r : r + 16]

    def put_rows(m, q, v, core):
        ux, zq = lax.rem(q, 4), q // 4
        for e in range(8):
            for k in range(3):
                r = e * 48 + k * 16
                a, u = color(k, ux, e % 4, (e // 4) * 2 + zq)
                gall[core, m * 12 + k * 4 + a, u] = v[r : r + 16]

    def feed(p, carry):
        left, right = 2 * p, 2 * p + 1
        w1 = jnp.concatenate([wf[q].reshape(768, 384) for q in (left, right)], axis=1)
        w2 = jnp.concatenate(
            [
                jnp.concatenate([wo[q, h * 24 : h * 24 + 24].reshape(384, 384) for h in (0, 1)], axis=1)
                for q in (left, right)
            ],
            axis=0,
        )
        u = mm(a2v[...], w1) + fbs[p, 0:1, :]
        uu = u * u
        t = jnp.tanh(ROOT * (u + CUBE * (u * uu)))
        hv[0] = (0.5 * u * (1.0 + t)).astype(BF)
        slope = 0.5 * (1.0 + t) + 0.5 * u * (1.0 - t * t) * (ROOT * (1.0 + (3.0 * CUBE) * uu))
        gu = (mm_nt(gmv[...], w2) * slope).astype(BF)
        hv[1] = gu
        fbg[p] = jnp.broadcast_to(column_sum(gu.astype(F32)), (8, 768))
        acc1[...] += mm(hv[0], w2)
        acc2[...] += mm_nt(hv[1], w1)
        for half in (0, 1):
            v = mm(lt1[half * 384 : half * 384 + 384, :], hv[1]).astype(BF)
            put_columns(1, left, v[:, 0:384], half * 4, 4)
            put_columns(1, right, v[:, 384:768], half * 4, 4)
            v = mm(lt2[half * 384 : half * 384 + 384, :], hv[0]).astype(BF)
            put_rows(2, left, v[:, 0:384], half)
            put_rows(2, right, v[:, 384:768], half)
        return carry

    lax.fori_loop(0, 4, feed, 0)
    core_start(1)
    core_start(2)
    block = yv[...] + ALPHA * (acc1[...] + sm[7:8, :])
    bo[...] = block.reshape(32, 8, 768).astype(BF)
    for q in range(4):
        sg[8 + q : 9 + q, :] = fbg[q, 0:1, :]
    sg[12:16, :] = jnp.zeros((4, 768), F32)
    n2, rstd2 = normalize(yv[...])
    ga2 = acc2[...]
    sg[5:6, :] = column_sum(ga2 * n2)
    sg[6:7, :] = column_sum(ga2)
    gyy = cot[...].astype(F32).reshape(256, 768) + norm_back(n2, rstd2, ga2 * sm[5:6, :])
    acc1[...] = gyy
    ga = (ALPHA * gyy).astype(BF)
    a2v[...] = ga
    sg[4:5, :] = column_sum(ga.astype(F32))
    lt1[...] = jnp.transpose(ov[...].astype(F32)).astype(BF)
    for half in (0, 1):
        v = mm(lt1[half * 384 : half * 384 + 384, :], a2v[...]).astype(BF)
        put_columns(0, 6, v[:, 0:384], half * 4, 4)
        put_columns(0, 7, v[:, 384:768], half * 4, 4)
    go = mm_nt(a2v[...], wp[...])
    exchange_drain(osnd, 1)
    for m in range(4):
        gather_drain(m)
    put_groups(osnd, 0, [go[:, PAIR[g] * 128 : PAIR[g] * 128 + 128] for g in range(4)])
    put_groups(osnd, 1, [go[:, SINGLE[g] * 128 : SINGLE[g] * 128 + 128] for g in range(4)])
    exchange_start(osnd, grcv, 2)
    lt1[...] = jnp.transpose(a1v[...].astype(F32)).astype(BF)
    exchange_wait(grcv, 2)

    for m in (1, 2):
        stage1_start(m)
    go01, gos = get_positions(grcv, 0), get_positions(grcv, 1)
    goh[0] = jnp.where(low, go01, zero).astype(BF)
    goh[1] = jnp.where(low, zero, go01).astype(BF)
    goh[2] = jnp.where(here, gos, zero).astype(BF)
    tmp[...] = jnp.zeros((6144, 128), F32)

    def attend_back(h, carry):
        base = (h // 2) * 1024
        for i in range(4):
            n = (i + 1) * 256
            g_rows = goh[h, i * 256 : n, :]
            p = pmat[h, offsets[i] : offsets[i] + n, :]
            pf = p.astype(F32)
            gp = mm_nt(vh[h, :n, :], g_rows)
            inner = jnp.sum(pf * gp, axis=0, keepdims=True)
            gs = (pf * (gp - inner)).astype(BF)
            tmp[pl.ds(base + i * 256, 256)] += jnp.transpose(mm(turned[h, :, :n], gs)) * 0.125
            tmp[pl.ds(2048 + base, n)] += mm(gs, qh[h, i * 256 : n, :])
            tmp[pl.ds(4096 + base, n)] += mm(p, g_rows)
        return carry

    lax.fori_loop(0, 3, attend_back, 0)
    exchange_drain(msg, 0)
    for b in range(3):
        put_positions(msg, b, tmp[pl.ds(b * 2048, 1024)])
    put_positions(msg, 3, tmp[pl.ds(1024, 1024)] + roll_half(tmp[pl.ds(3072, 1024)]))
    put_positions(msg, 4, tmp[pl.ds(5120, 1024)])
    exchange_start(msg, rcv, 3)
    exchange_wait(rcv, 3)

    got = [get_groups(rcv, b) for b in range(5)]
    for which in range(3):
        blocks = [None] * 6
        for g in range(4):
            blocks[PAIR[g]] = got[which][g]
        for b, e, o in ((1, 0, 1), (4, 2, 3)):
            if which == 0:
                blocks[b] = jnp.where(low, got[3][e], roll_half(got[3][o]))
            elif which == 1:
                blocks[b] = jnp.where(low, roll_half(got[3][e]), got[3][o])
            else:
                blocks[b] = got[4][e] + got[4][o]
        for b in range(6):
            at = which * 768 + b * 128
            g3[:, at : at + 128] = blocks[b].astype(BF)
            if which != 1:
                row = 2 if which == 0 else 3
                sg[row : row + 1, b * 128 : b * 128 + 128] = column_sum(blocks[b])

    def qkv_grad(p, carry):
        cols = g3[:, pl.ds(pl.multiple_of(p * 768, 128), 768)]
        for half in (0, 1):
            v = mm(lt1[half * 384 : half * 384 + 384, :], cols).astype(BF)
            put_columns(0, 2 * p, v[:, 0:384], half * 4, 4)
            put_columns(0, 2 * p + 1, v[:, 384:768], half * 4, 4)
        return carry

    lax.fori_loop(0, 3, qkv_grad, 0)
    core_start(0)
    for m in (1, 2):
        stage2_start(m)
    ga1 = mm_nt(g3[...], wq[...])
    n1, rstd1 = normalize(tok[...].astype(F32).reshape(256, 768))
    sg[0:1, :] = column_sum(ga1 * n1)
    sg[1:2, :] = column_sum(ga1)
    gx = acc1[...] + norm_back(n1, rstd1, ga1 * sm[0:1, :])
    ig[...] = gx.reshape(32, 8, 768).astype(BF)

    vectors_start(0)
    for m in (1, 2):
        stage3_start(m)
    stage1_start(0)
    vectors_finish(0)
    vectors_start(1)
    for m in (1, 2):
        share_start(m)
    stage2_start(0)
    vectors_finish(1)
    vectors_start(2)
    for m in (1, 2):
        share_relay(m)
    stage3_start(0)
    vectors_finish(2)
    vectors_start(3)
    share_start(0)
    vectors_finish(3)
    lead = pltpu.roll(sg[0:8, :], lax.rem(8 - sh, 8) * 96, 1)
    sgo[...] = lead[:, 0:128]
    wide = column_sum(
        jnp.where(lax.broadcasted_iota(jnp.int32, (4, 768), 0) == sh // 2, sg[8:12, :], 0.0)
    )
    fbo[...] = jnp.where(lax.rem(sh, 2) == 0, wide[:, 0:384], wide[:, 384:768])
    share_relay(0)
    for m in range(3):
        share_finish(m)

    for k in range(7):
        arrived(smi, sm_s.at[k])
    exchange_drain(osnd, 2)
    exchange_drain(msg, 3)
    for m in range(3):
        sums_drain(m)
    for i in range(9):
        arrived(sgr.at[0], t_s.at[i])


def block_step(tok, cot, lens, smi, wq_s, wp_s, wf_s, wo_s):
    vmem = pl.BlockSpec(memory_space=pltpu.VMEM)
    smem = pl.BlockSpec(memory_space=pltpu.SMEM)
    anywhere = pl.BlockSpec(memory_space=pl.ANY)
    V, D = pltpu.VMEM, pltpu.SemaphoreType.DMA
    return pl.pallas_call(
        block_kernel,
        name="block",
        out_shape=(
            jax.ShapeDtypeStruct((32, 8, 768), BF),
            jax.ShapeDtypeStruct((32, 8, 768), BF),
            jax.ShapeDtypeStruct((96, 3072), BF),
            jax.ShapeDtypeStruct((96, 3072), BF),
            jax.ShapeDtypeStruct((768, 384), BF),
            jax.ShapeDtypeStruct((8, 128), F32),
            jax.ShapeDtypeStruct((1, 384), F32),
        ),
        in_specs=[vmem, vmem, smem, vmem, anywhere, anywhere, anywhere, anywhere],
        out_specs=(vmem,) * 7,
        scratch_shapes=[
            V((768, 2304), BF),
            V((768, 768), BF),
            V((8, 48, 16, 384), BF),
            V((8, 48, 16, 384), BF),
            V((2, 36, 16, 16, 384), BF),
            V((24, 16, 16, 384), BF),
            V((27, 4, 16, 384), BF),
            V((27, 16, 384), BF),
            V((3, 2560, 256), BF),
            V((3, 1024, 128), BF),
            V((3, 1024, 128), BF),
            V((3, 1024, 128), BF),
            V((3, 1024, 128), BF),
            V((3, 128, 1024), BF),
            V((128, 8, 640), BF),
            V((128, 8, 640), BF),
            V((128, 8, 256), BF),
            V((128, 8, 256), BF),
            V((128, 8, 256), BF),
            V((6144, 128), F32),
            V((256, 768), F32),
            V((256, 768), F32),
            V((256, 768), F32),
            V((8, 16, 768), BF),
            V((16, 768), F32),
            V((4, 8, 768), F32),
            V((4, 8, 768), F32),
            V((16, 768), F32),
            V((13, 16, 768), F32),
            V((256, 768), BF),
            V((256, 768), BF),
            V((256, 768), BF),
            V((768, 256), BF),
            V((768, 256), BF),
            V((256, 768), BF),
            V((256, 2304), BF),
            V((2, 256, 768), BF),
            D((4, 28)), D((4, 28)), D((4, 8)),
            D((7,)), D((7,)),
            D((4,)), D((4,)),
            D((36,)), D((36,)),
            D((3, 27)), D((3, 27)),
            D((3, 8)), D((3, 8)),
            D((10,)), D((10,)),
        ],
        compiler_params=pltpu.CompilerParams(
            collective_id=0, has_side_effects=True, vmem_limit_bytes=64 * 2**20
        ),
    )(tok, cot, lens, smi, wq_s, wp_s, wf_s, wo_s)


def per_device(
    tokens,
    out_grad,
    lengths,
    ln1_gain,
    ln1_bias,
    w_qkv,
    q_bias,
    v_bias,
    w_proj,
    proj_bias,
    ln2_gain,
    ln2_bias,
    w_fc,
    fc_bias,
    w_out,
    out_bias,
):
    sh = lax.axis_index("shard")
    vectors = jnp.stack(
        [ln1_gain, ln1_bias, q_bias, v_bias, proj_bias, ln2_gain, ln2_bias, out_bias]
    )
    column = lax.broadcasted_iota(jnp.int32, (8, 768), 1)
    vectors = jnp.where(column // 96 == sh, jnp.tile(vectors, (1, 8)), jnp.zeros((), BF))
    place384 = lax.broadcasted_iota(jnp.int32, (8, 768), 0) * 2 + column // 384
    wide = jnp.where(place384 == sh, jnp.tile(fc_bias[None, :], (8, 2)), jnp.zeros((), BF))
    smi = jnp.concatenate([vectors, wide], axis=0)
    wf_s = w_fc.reshape(6, 16, 3072)
    wo_s = w_out.reshape(24, 16, 768)
    block, in_grad, gq, gf, gt, rows, d_fb = block_step(
        tokens, out_grad, lengths, smi, w_qkv, w_proj, wf_s, wo_s
    )
    rows = rows[:, :96]
    return (
        block,
        in_grad,
        rows[0],
        rows[1],
        gq[:, :2304].astype(F32),
        rows[2],
        rows[3],
        gq[:, 2304:].astype(F32),
        rows[4],
        rows[5],
        rows[6],
        gf.astype(F32),
        d_fb[0],
        gt.astype(F32).T,
        rows[7],
    )


def solution(mesh):
    pieces = P(None, ("rep", "shard"), None)
    row, table = P("shard"), P("shard", None)
    kinds = (row, row, table, row, row, table, row, row, row, table, row, table, row)
    return jax.shard_map(
        per_device,
        mesh=mesh,
        in_specs=(pieces, pieces, P(), *kinds),
        out_specs=(pieces, pieces, *kinds),
        check_vma=False,
    )
```

```python
import functools
import math

import jax
import jax.numpy as jnp
from jax import lax
from jax.experimental import pallas as pl
from jax.experimental.pallas import tpu as pltpu
from jax.sharding import PartitionSpec as P

HEADS = 12
LAYERS = 12
EPSILON = 1e-05
MASKED = -1e30
MESH = pl.DeviceIdType.MESH
BF = jnp.bfloat16
F32 = jnp.float32
ALPHA = 1.0 / math.sqrt(LAYERS)
ROOT = math.sqrt(2.0 / math.pi)
CUBE = 0.044715
NT = (((1,), (1,)), ((), ()))
PAIR = (0, 2, 3, 5)
SINGLE = (1, 1, 4, 4)


def mm(a, b):
    return jnp.dot(a, b, preferred_element_type=F32)


def mm_nt(a, b):
    return lax.dot_general(a, b, NT, preferred_element_type=F32)


def mean(v):
    return jnp.mean(v, axis=-1, keepdims=True)


def normalize(v):
    centered = v - mean(v)
    rstd = lax.rsqrt(mean(centered * centered) + EPSILON)
    return centered * rstd, rstd


def norm_back(n, rstd, r):
    return (r - mean(r) - n * mean(r * n)) * rstd


def column_sum(v):
    return jnp.sum(v, axis=0, keepdims=True)


def roll_half(v):
    return pltpu.roll(v, 64, 1)


def place(x, y, z, c):
    return (y * 4 + (z // 2) * 2 + c, lax.rem(z, 2) * 4 + x)


def remote(src, dst, send, recv, device):
    return pltpu.make_async_remote_copy(
        src_ref=src, dst_ref=dst, send_sem=send, recv_sem=recv, device_id=device, device_id_type=MESH
    )


def arrived(ref, sem):
    pltpu.make_async_copy(ref, ref, sem).wait()


def block_kernel(
    tok, cot, lens, smi, wq_s, wp_s, wf_s, wo_s,
    bo, ig, gq_o, gf_o, go_t, sgo, fbo,
    wq, wp, wf, wo, gall, r0, r2, r3, pmat, qh, kh, vh, goh, turned, msg, msg2, rcv, rcv2, osnd, orcv, grcv, tmp,
    yv, acc1, acc2, smr, sm, fbs, fbg, sg, sgr, a1v, a2v, gmv, lt1, lt2, ov, g3, hv,
    ag_s, ag_r, ag_l, sm_s, sm_r, aa_s, aa_r, c_s, c_r, d_s, d_r, fin_s, fin_r, t_s, t_r,
):
    rep, sh = lax.axis_index("rep"), lax.axis_index("shard")
    me = rep * 8 + sh
    x, zl, y, c = lax.rem(sh, 4), sh // 4, rep // 4, lax.rem(rep, 2)
    z = lax.rem(rep // 2, 2) * 2 + zl
    sibling = place(x, y, z, 1 - c)

    def ring(v, k):
        return lax.rem(v + k + 4, 4)

    def along(dim, value):
        return place(*[value if d == dim else v for d, v in enumerate((x, y, z))], c)

    own = (x, y, z)

    barrier = pltpu.get_barrier_semaphore()

    def greet(step, carry):
        peer = lax.rem(me + step, 128)
        pl.semaphore_signal(
            barrier, inc=1, device_id=(peer // 8, lax.rem(peer, 8)), device_id_type=MESH
        )
        return carry

    lax.fori_loop(1, 128, greet, 0)
    pl.semaphore_wait(barrier, 127)

    def rows16(start, size):
        return pl.ds(pl.multiple_of(start, 16), size)

    def gathered(m, s, core, h):
        if m == 0:
            return wq.at[rows16(s * 96 + core * 48, 48), pl.ds(h * 1152, 1152)]
        if m == 1:
            return wp.at[rows16(s * 96 + core * 48, 48), pl.ds(h * 384, 384)]
        if m == 2:
            return wf.at[pl.ds(h * 4, 4), pl.ds(s * 6 + core * 3, 3)]
        return wo.at[s, pl.ds(h * 24 + core * 12, 12)]

    def shard_of(m, core, h):
        if m == 0:
            return wq_s.at[rows16(core * 48, 48), pl.ds(h * 1152, 1152)]
        if m == 1:
            return wp_s.at[rows16(core * 48, 48), pl.ds(h * 384, 384)]
        return gathered(m, sh, core, h)

    def from_x(k):
        return zl * 4 + ring(x, -k)

    def from_z(j):
        return (1 - zl) * 4 + ring(x, -j)

    def own_copies(m):
        if m == 2:
            return [
                pltpu.make_async_copy(
                    wf_s.at[:, :, pl.ds(q * 384, 384)], wf.at[q, pl.ds(sh * 6, 6)], ag_l.at[m, q]
                )
                for q in range(8)
            ]
        if m == 3:
            return [
                pltpu.make_async_copy(
                    wo_s.at[:, :, pl.ds(h * 384, 384)], wo.at[sh, pl.ds(h * 24, 24)], ag_l.at[m, h]
                )
                for h in (0, 1)
            ]
        return [
            pltpu.make_async_copy(
                shard_of(m, core, h), gathered(m, sh, core, h), ag_l.at[m, core * 2 + h]
            )
            for core in (0, 1)
            for h in (0, 1)
        ]

    def beside(h):
        return along(2, ring(z, 1 - 2 * h))

    def gather_start(m):
        for copy in own_copies(m):
            copy.start()
        if m >= 2:
            for copy in own_copies(m):
                copy.wait()
        for h in (0, 1):
            remote(
                shard_of(m, c, h), gathered(m, sh, c, h), ag_s.at[m, 6 + h], ag_r.at[m, 6 + h], beside(h)
            ).start()
            for k in (1, 3):
                i = (k - 1) * 2 + h
                remote(
                    shard_of(m, c, h), gathered(m, sh, c, h), ag_s.at[m, i], ag_r.at[m, i],
                    along(0, ring(x, k)),
                ).start()

    def gather_relay_x(m):
        for k, h in ((1, 0), (3, 1), (1, 1), (3, 0), (2, 0), (2, 1)):
            i = (k - 1) * 2 + h
            piece = gathered(m, from_x(k), c, h)
            arrived(piece, ag_r.at[m, i])
            if (k, h) in ((1, 0), (3, 1)):
                remote(
                    piece, piece, ag_s.at[m, 2 + h], ag_r.at[m, 2 + h], along(0, ring(x, 1 - 2 * h))
                ).start()
            i = 6 + 2 * k + h
            remote(piece, piece, ag_s.at[m, i], ag_r.at[m, i], beside(h)).start()
            i = 14 + (k - 1) * 2 + h
            remote(piece, piece, ag_s.at[m, i], ag_r.at[m, i], sibling).start()

    def gather_relay_z(m):
        for j in (0, 1, 3, 2):
            for h in (0, 1):
                piece = gathered(m, from_z(j), c, h)
                arrived(piece, ag_r.at[m, 6 + 2 * j + h])
                i = 20 + 2 * j + h
                remote(piece, piece, ag_s.at[m, i], ag_r.at[m, i], sibling).start()

    def gather_finish(m):
        if m < 2:
            for copy in own_copies(m):
                copy.wait()
        for h in (0, 1):
            for k in (1, 2, 3):
                arrived(gathered(m, from_x(k), 1 - c, h), ag_r.at[m, 14 + (k - 1) * 2 + h])
            for j in range(4):
                arrived(gathered(m, from_z(j), 1 - c, h), ag_r.at[m, 20 + 2 * j + h])

    def gather_drain(m):
        for h in (0, 1):
            for i in range(0, 28, 2):
                arrived(gathered(m, 0, 0, h), ag_s.at[m, i + h])

    def exchange_start(src, dst, i):
        def send(step, carry):
            peer = lax.rem(me + step, 128)
            remote(
                src.at[peer], dst.at[me], aa_s.at[i], aa_r.at[i], (peer // 8, lax.rem(peer, 8))
            ).start()
            return carry

        lax.fori_loop(1, 128, send, 0)
        dst[pl.ds(me, 1)] = src[pl.ds(me, 1)]

    def exchange_wait(dst, i):
        most = dst.at[pl.ds(0, 127)]
        arrived(most, aa_r.at[i])

    def exchange_drain(src, i):
        most = src.at[pl.ds(0, 127)]
        arrived(most, aa_s.at[i])

    lane = lax.broadcasted_iota(jnp.int32, (1, 128), 1)
    low = lane < 64
    half = lax.rem(me, 2)
    here = (lane >= half * 64) & (lane < half * 64 + 64)

    def lanes(i, count=1):
        return pl.ds(i * 128, count * 128)

    def put_groups(dst, b, per_group):
        stacked = jnp.stack([g.reshape(32, 8, 128) for g in per_group], axis=1)
        dst[:, :, b * 128 : (b + 1) * 128] = stacked.reshape(128, 8, 128).astype(BF)

    def get_groups(src, b):
        v = src[:, :, b * 128 : (b + 1) * 128].astype(F32).reshape(32, 4, 8, 128)
        return [v[:, g].reshape(256, 128) for g in range(4)]

    def put_positions(dst, b, v):
        dst[:, :, b * 128 : (b + 1) * 128] = v.reshape(128, 8, 128).astype(BF)

    def get_positions(src, b):
        return src[:, :, b * 128 : (b + 1) * 128].astype(F32).reshape(1024, 128)

    def block0(m, k, a):
        if m == 0:
            i = k * 4 + a
            return wo.at[i // 3, pl.ds(lax.rem(i, 3) * 16, 16)]
        return r0.at[(m - 1) * 12 + k * 4 + a]

    def block1(m, k, off):
        i = k * 3 + off - 1
        if m == 0:
            return wo.at[4 + i // 3, pl.ds((i % 3) * 16, 16)]
        return wf.at[(m - 1) * 4 + i // 3, pl.ds((i % 3) * 16, 16)]

    def core_start(m):
        for off in (1, 2, 3, 0):
            for k in range(3):
                a = ring(own[k], off)
                i = (m * 3 + k) * 4 + off
                remote(
                    gall.at[1 - c, m * 12 + k * 4 + a], block0(m, k, a), c_s.at[i], c_r.at[i], sibling
                ).start()

    def stage1_start(m):
        for off in (1, 2, 3):
            for k in range(3):
                a = ring(own[k], off)
                i = (m * 3 + k) * 4 + off
                arrived(block0(m, k, a), c_r.at[i])
                mine = gall.at[c, m * 12 + k * 4 + a]
                mine[...] = mine[...] + block0(m, k, a)[...]
                i = (m * 3 + k) * 3 + off - 1
                remote(
                    mine, block1(m, k, off), d_s.at[0, i], d_r.at[0, i], along(k, a)
                ).start()

    def stage2_start(m):
        for k in range(3):
            a = own[k]
            arrived(block0(m, k, a), c_r.at[(m * 3 + k) * 4])
            mine = gall.at[c, m * 12 + k * 4 + a]
            total = mine[...].astype(F32) + block0(m, k, a)[...].astype(F32)
            for off in (1, 2, 3):
                i = (m * 3 + k) * 3 + off - 1
                arrived(block1(m, k, off), d_r.at[0, i])
                total = total + block1(m, k, off)[...].astype(F32)
            mine[...] = total.astype(BF)
            dim = (k + 1) % 3
            for off in (1, 2, 3):
                i = (m * 3 + k) * 3 + off - 1
                b = ring(own[dim], off)
                remote(
                    mine.at[pl.ds(b * 4, 4)], r2.at[i], d_s.at[1, i], d_r.at[1, i], along(dim, b)
                ).start()

    def stage3_start(m):
        for k in range(3):
            mine = gall.at[c, m * 12 + k * 4 + own[k], pl.ds(own[(k + 1) % 3] * 4, 4)]
            total = mine[...].astype(F32)
            for off in (1, 2, 3):
                i = (m * 3 + k) * 3 + off - 1
                arrived(r2.at[i], d_r.at[1, i])
                total = total + r2[i].astype(F32)
            mine[...] = total.astype(BF)
            dim = (k + 2) % 3
            for off in (1, 2, 3):
                i = (m * 3 + k) * 3 + off - 1
                e = ring(own[dim], off)
                remote(mine.at[e], r3.at[i], d_s.at[2, i], d_r.at[2, i], along(dim, e)).start()

    def region(m, r):
        part, core = lax.rem(r // 2, 2) * 4 + r // 4, lax.rem(r, 2)
        if m == 2:
            return go_t.at[rows16(core * 384 + part * 48, 48)]
        out = gf_o if m == 1 else gq_o
        return out.at[rows16(core * 48, 48), pl.ds(pl.multiple_of(part * 384, 128), 384)]

    def share_start(m):
        for k in range(3):
            u = own[(k + 1) % 3] * 4 + own[(k + 2) % 3]
            total = gall[c, m * 12 + k * 4 + own[k], u].astype(F32)
            for off in (1, 2, 3):
                i = (m * 3 + k) * 3 + off - 1
                arrived(r3.at[i], d_r.at[2, i])
                total = total + r3[i].astype(F32)
            region(m, rep).at[pl.ds(k * 16, 16), :][...] = total.astype(BF)
        mine = region(m, rep)
        for k in range(1, 8):
            peer = lax.rem(rep // 2 + k, 8) * 2 + c
            remote(mine, mine, fin_s.at[m, k - 1], fin_r.at[m, k - 1], (peer, sh)).start()

    def strip(m, core):
        if m == 2:
            return go_t.at[rows16(core * 384, 384)]
        return (gf_o if m == 1 else gq_o).at[rows16(core * 48, 48)]

    def share_relay(m):
        for k in range(1, 8):
            peer = lax.rem(rep // 2 + 8 - k, 8) * 2 + c
            arrived(region(m, peer), fin_r.at[m, k - 1])
        remote(strip(m, c), strip(m, c), fin_s.at[m, 7], fin_r.at[m, 7], sibling).start()

    def share_finish(m):
        arrived(strip(m, 1 - c), fin_r.at[m, 7])

    def sums_drain(m):
        for k in range(3):
            for off in range(4):
                arrived(r0.at[0], c_s.at[(m * 3 + k) * 4 + off])
            for off in range(3):
                i = (m * 3 + k) * 3 + off
                arrived(r0.at[0], d_s.at[0, i])
                arrived(r2.at[0], d_s.at[1, i])
                arrived(r3.at[0], d_s.at[2, i])
        for k in range(7):
            arrived(region(m, rep), fin_s.at[m, k])
        arrived(strip(m, c), fin_s.at[m, 7])

    def vectors_start(stage):
        if stage == 0:
            remote(sg, sgr.at[12], t_s.at[9], t_r.at[9], sibling).start()
            return
        dim = stage - 1
        slot = dim * 4 + own[dim]
        sgr[pl.ds(slot, 1)] = sg[...].reshape(1, 16, 768)
        for off in (1, 2, 3):
            i = dim * 3 + off - 1
            remote(
                sgr.at[slot], sgr.at[slot], t_s.at[i], t_r.at[i], along(dim, ring(own[dim], off))
            ).start()

    def vectors_finish(stage):
        if stage == 0:
            arrived(sgr.at[12], t_r.at[9])
            arrived(sg, t_s.at[9])
            sg[...] = sg[...] + sgr[12]
            return
        dim = stage - 1
        for off in (1, 2, 3):
            i = dim * 3 + off - 1
            arrived(sgr.at[dim * 4 + ring(own[dim], -off)], t_r.at[i])
        sg[...] = (sgr[dim * 4] + sgr[dim * 4 + 1]) + (sgr[dim * 4 + 2] + sgr[dim * 4 + 3])

    gather_start(0)
    for k in range(1, 8):
        remote(
            smi, smr.at[sh], sm_s.at[k - 1], sm_r.at[k - 1], (rep, lax.rem(sh + k, 8))
        ).start()
    smr[pl.ds(sh, 1)] = smi[...].reshape(1, 16, 768)
    for k in range(1, 8):
        arrived(smr.at[lax.rem(sh + 8 - k, 8)], sm_r.at[k - 1])
    sm[...] = jnp.sum(smr[...].astype(F32), axis=0)
    for q in range(4):
        fbs[q] = jnp.broadcast_to(sm[8 + q : 9 + q, :], (8, 768))
    x_in = tok[...].astype(F32).reshape(256, 768)
    n1, rstd1 = normalize(x_in)
    a1 = n1 * sm[0:1, :] + sm[1:2, :]
    a1v[...] = a1.astype(BF)
    gather_relay_x(0)
    for m in range(1, 4):
        gather_start(m)
    gather_relay_z(0)
    gather_finish(0)
    gather_relay_x(1)

    for b in range(9):
        v = mm(a1v[...], wq[:, b * 256 : (b + 1) * 256])
        if b < 3:
            v = v + sm[2:3, b * 256 : (b + 1) * 256]
        if b >= 6:
            v = v + sm[3:4, (b - 6) * 256 : (b - 5) * 256]
        tmp[pl.ds(b * 512, 256)] = v[:, :128]
        tmp[pl.ds(b * 512 + 256, 256)] = v[:, 128:]

    def natural(which, b):
        return tmp[pl.ds((which * 6 + b) * 256, 256)]

    for which in range(3):
        put_groups(msg, which, [natural(which, PAIR[g]) for g in range(4)])
    exchange_start(msg, rcv, 0)
    packed = []
    for g in range(4):
        qb, kb = natural(0, SINGLE[g]), natural(1, SINGLE[g])
        packed.append(
            jnp.where(low, qb, roll_half(kb)) if g % 2 == 0 else jnp.where(low, roll_half(qb), kb)
        )
    put_groups(msg2, 0, packed)
    put_groups(msg2, 1, [natural(2, SINGLE[g]) for g in range(4)])
    exchange_start(msg2, rcv2, 4)
    gather_relay_x(2)
    exchange_wait(rcv, 0)

    zero = jnp.zeros((1024, 128), F32)

    def load_head(h, qq, kk, vv, mask, vmask):
        qh[h] = jnp.where(mask, qq * 0.125, zero).astype(BF)
        kh[h] = jnp.where(mask, kk, zero).astype(BF)
        vv = jnp.where(vmask, vv, zero)
        vh[h] = vv.astype(BF)
        turned[h] = jnp.transpose(vv).astype(BF)

    q01, k01, v01 = [get_positions(rcv, b) for b in range(3)]
    load_head(0, q01, k01, v01, low, low)
    load_head(1, q01, k01, v01, ~low, ~low)
    length = lens[me // 4]
    offsets = (0, 256, 768, 1536)
    tmp[pl.ds(0, 2048)] = jnp.zeros((2048, 128), F32)

    def attend(h, carry):
        for i in range(4):
            n = (i + 1) * 256
            s = mm_nt(kh[h, :n, :], qh[h, i * 256 : n, :])
            key = lax.broadcasted_iota(jnp.int32, (n, 256), 0)
            limit = lax.broadcasted_iota(jnp.int32, (1, 256), 1) + (i * 256 + 1)
            s = jnp.where(key < jnp.minimum(limit, length), s, MASKED)
            e = jnp.exp(s - jnp.max(s, axis=0, keepdims=True))
            p = (e * (1.0 / jnp.sum(e, axis=0, keepdims=True))).astype(BF)
            pmat[h, offsets[i] : offsets[i] + n, :] = p
            o = jnp.transpose(mm(turned[h, :, :n], p))
            tmp[pl.ds((h // 2) * 1024 + i * 256, 256)] += o
        return carry

    lax.fori_loop(0, 2, attend, 0)
    gather_relay_x(3)
    exchange_wait(rcv2, 4)
    qks, vs = [get_positions(rcv2, b) for b in range(2)]
    load_head(2, qks, roll_half(qks), vs, low, here)
    lax.fori_loop(2, 3, attend, 0)
    put_positions(osnd, 0, tmp[pl.ds(0, 1024)])
    put_positions(osnd, 1, tmp[pl.ds(1024, 1024)])
    exchange_start(osnd, orcv, 1)
    for h in range(3):
        turned[h] = jnp.transpose(kh[h].astype(F32)).astype(BF)
    for m in range(1, 4):
        gather_relay_z(m)
    for m in range(1, 4):
        gather_finish(m)
    exchange_wait(orcv, 1)

    pairs, singles = get_groups(orcv, 0), get_groups(orcv, 1)
    blocks = [None] * 6
    for g in range(4):
        blocks[PAIR[g]] = pairs[g]
    blocks[1], blocks[4] = singles[0] + singles[1], singles[2] + singles[3]
    for b in range(6):
        ov[:, b * 128 : (b + 1) * 128] = blocks[b].astype(BF)
    x_in = tok[...].astype(F32).reshape(256, 768)
    g_in = cot[...].astype(F32).reshape(256, 768)
    y_mid = x_in + ALPHA * (mm(ov[...], wp[...]) + sm[4:5, :])
    yv[...] = y_mid
    n2, rstd2 = normalize(y_mid)
    a2 = n2 * sm[5:6, :] + sm[6:7, :]
    a2v[...] = a2.astype(BF)
    gm = (ALPHA * g_in).astype(BF)
    gmv[...] = gm
    gm = gm.astype(F32)
    sg[7:8, :] = column_sum(gm)
    lt1[...] = jnp.transpose(a2v[...].astype(F32)).astype(BF)
    lt2[...] = jnp.transpose(gm).astype(BF)
    acc1[...] = jnp.zeros((256, 768), F32)
    acc2[...] = jnp.zeros((256, 768), F32)

    def color(k, ux, uy, uz):
        order = ((ux, uy, uz), (uy, uz, ux), (uz, ux, uy))[k]
        return order[0], order[1] * 4 + order[2]

    def put_columns(m, q, v, first, shards):
        uy, zq = lax.rem(q, 4), q // 4
        for s in range(first, first + shards):
            for core in range(2):
                for k in range(3):
                    r = (s - first) * 96 + core * 48 + k * 16
                    a, u = color(k, s % 4, uy, zq * 2 + s // 4)
                    gall[core, m * 12 + k * 4 + a, u] = v[r : r + 16]

    def put_rows(m, q, v, core):
        ux, zq = lax.rem(q, 4), q // 4
        for e in range(8):
            for k in range(3):
                r = e * 48 + k * 16
                a, u = color(k, ux, e % 4, (e // 4) * 2 + zq)
                gall[core, m * 12 + k * 4 + a, u] = v[r : r + 16]

    def feed(p, carry):
        left, right = 2 * p, 2 * p + 1
        w1 = jnp.concatenate([wf[q].reshape(768, 384) for q in (left, right)], axis=1)
        w2 = jnp.concatenate(
            [
                jnp.concatenate([wo[q, h * 24 : h * 24 + 24].reshape(384, 384) for h in (0, 1)], axis=1)
                for q in (left, right)
            ],
            axis=0,
        )
        u = mm(a2v[...], w1) + fbs[p, 0:1, :]
        uu = u * u
        t = jnp.tanh(ROOT * (u + CUBE * (u * uu)))
        hv[0] = (0.5 * u * (1.0 + t)).astype(BF)
        slope = 0.5 * (1.0 + t) + 0.5 * u * (1.0 - t * t) * (ROOT * (1.0 + (3.0 * CUBE) * uu))
        gu = (mm_nt(gmv[...], w2) * slope).astype(BF)
        hv[1] = gu
        fbg[p] = jnp.broadcast_to(column_sum(gu.astype(F32)), (8, 768))
        acc1[...] += mm(hv[0], w2)
        acc2[...] += mm_nt(hv[1], w1)
        for half in (0, 1):
            v = mm(lt1[half * 384 : half * 384 + 384, :], hv[1]).astype(BF)
            put_columns(1, left, v[:, 0:384], half * 4, 4)
            put_columns(1, right, v[:, 384:768], half * 4, 4)
            v = mm(lt2[half * 384 : half * 384 + 384, :], hv[0]).astype(BF)
            put_rows(2, left, v[:, 0:384], half)
            put_rows(2, right, v[:, 384:768], half)
        return carry

    lax.fori_loop(0, 4, feed, 0)
    core_start(1)
    core_start(2)
    block = yv[...] + ALPHA * (acc1[...] + sm[7:8, :])
    bo[...] = block.reshape(32, 8, 768).astype(BF)
    for q in range(4):
        sg[8 + q : 9 + q, :] = fbg[q, 0:1, :]
    sg[12:16, :] = jnp.zeros((4, 768), F32)
    n2, rstd2 = normalize(yv[...])
    ga2 = acc2[...]
    sg[5:6, :] = column_sum(ga2 * n2)
    sg[6:7, :] = column_sum(ga2)
    gyy = cot[...].astype(F32).reshape(256, 768) + norm_back(n2, rstd2, ga2 * sm[5:6, :])
    acc1[...] = gyy
    ga = (ALPHA * gyy).astype(BF)
    a2v[...] = ga
    sg[4:5, :] = column_sum(ga.astype(F32))
    lt1[...] = jnp.transpose(ov[...].astype(F32)).astype(BF)
    for half in (0, 1):
        v = mm(lt1[half * 384 : half * 384 + 384, :], a2v[...]).astype(BF)
        put_columns(0, 6, v[:, 0:384], half * 4, 4)
        put_columns(0, 7, v[:, 384:768], half * 4, 4)
    go = mm_nt(a2v[...], wp[...])
    exchange_drain(osnd, 1)
    for m in range(4):
        gather_drain(m)
    put_groups(osnd, 0, [go[:, PAIR[g] * 128 : PAIR[g] * 128 + 128] for g in range(4)])
    put_groups(osnd, 1, [go[:, SINGLE[g] * 128 : SINGLE[g] * 128 + 128] for g in range(4)])
    exchange_start(osnd, grcv, 2)
    lt1[...] = jnp.transpose(a1v[...].astype(F32)).astype(BF)
    exchange_wait(grcv, 2)

    for m in (1, 2):
        stage1_start(m)
    go01, gos = get_positions(grcv, 0), get_positions(grcv, 1)
    goh[0] = jnp.where(low, go01, zero).astype(BF)
    goh[1] = jnp.where(low, zero, go01).astype(BF)
    goh[2] = jnp.where(here, gos, zero).astype(BF)
    tmp[...] = jnp.zeros((6144, 128), F32)

    def attend_back(h, carry):
        base = (h // 2) * 1024
        for i in range(4):
            n = (i + 1) * 256
            g_rows = goh[h, i * 256 : n, :]
            p = pmat[h, offsets[i] : offsets[i] + n, :]
            pf = p.astype(F32)
            gp = mm_nt(vh[h, :n, :], g_rows)
            inner = jnp.sum(pf * gp, axis=0, keepdims=True)
            gs = (pf * (gp - inner)).astype(BF)
            tmp[pl.ds(base + i * 256, 256)] += jnp.transpose(mm(turned[h, :, :n], gs)) * 0.125
            tmp[pl.ds(2048 + base, n)] += mm(gs, qh[h, i * 256 : n, :])
            tmp[pl.ds(4096 + base, n)] += mm(p, g_rows)
        return carry

    lax.fori_loop(0, 2, attend_back, 0)
    exchange_drain(msg, 0)
    for b in range(3):
        put_positions(msg, b, tmp[pl.ds(b * 2048, 1024)])
    exchange_start(msg, rcv, 3)
    lax.fori_loop(2, 3, attend_back, 0)
    exchange_drain(msg2, 4)
    put_positions(msg2, 0, tmp[pl.ds(1024, 1024)] + roll_half(tmp[pl.ds(3072, 1024)]))
    put_positions(msg2, 1, tmp[pl.ds(5120, 1024)])
    exchange_start(msg2, rcv2, 5)
    exchange_wait(rcv, 3)
    exchange_wait(rcv2, 5)

    got = [get_groups(rcv, b) for b in range(3)] + [get_groups(rcv2, b) for b in range(2)]
    for which in range(3):
        blocks = [None] * 6
        for g in range(4):
            blocks[PAIR[g]] = got[which][g]
        for b, e, o in ((1, 0, 1), (4, 2, 3)):
            if which == 0:
                blocks[b] = jnp.where(low, got[3][e], roll_half(got[3][o]))
            elif which == 1:
                blocks[b] = jnp.where(low, roll_half(got[3][e]), got[3][o])
            else:
                blocks[b] = got[4][e] + got[4][o]
        for b in range(6):
            at = which * 768 + b * 128
            g3[:, at : at + 128] = blocks[b].astype(BF)
            if which != 1:
                row = 2 if which == 0 else 3
                sg[row : row + 1, b * 128 : b * 128 + 128] = column_sum(blocks[b])

    def qkv_grad(p, carry):
        cols = g3[:, pl.ds(pl.multiple_of(p * 768, 128), 768)]
        for half in (0, 1):
            v = mm(lt1[half * 384 : half * 384 + 384, :], cols).astype(BF)
            put_columns(0, 2 * p, v[:, 0:384], half * 4, 4)
            put_columns(0, 2 * p + 1, v[:, 384:768], half * 4, 4)
        return carry

    lax.fori_loop(0, 3, qkv_grad, 0)
    core_start(0)
    for m in (1, 2):
        stage2_start(m)
    ga1 = mm_nt(g3[...], wq[...])
    n1, rstd1 = normalize(tok[...].astype(F32).reshape(256, 768))
    sg[0:1, :] = column_sum(ga1 * n1)
    sg[1:2, :] = column_sum(ga1)
    gx = acc1[...] + norm_back(n1, rstd1, ga1 * sm[0:1, :])
    ig[...] = gx.reshape(32, 8, 768).astype(BF)

    vectors_start(0)
    for m in (1, 2):
        stage3_start(m)
    stage1_start(0)
    vectors_finish(0)
    vectors_start(1)
    for m in (1, 2):
        share_start(m)
    stage2_start(0)
    vectors_finish(1)
    vectors_start(2)
    for m in (1, 2):
        share_relay(m)
    stage3_start(0)
    vectors_finish(2)
    vectors_start(3)
    share_start(0)
    vectors_finish(3)
    lead = pltpu.roll(sg[0:8, :], lax.rem(8 - sh, 8) * 96, 1)
    sgo[...] = lead[:, 0:128]
    wide = column_sum(
        jnp.where(lax.broadcasted_iota(jnp.int32, (4, 768), 0) == sh // 2, sg[8:12, :], 0.0)
    )
    fbo[...] = jnp.where(lax.rem(sh, 2) == 0, wide[:, 0:384], wide[:, 384:768])
    share_relay(0)
    for m in range(3):
        share_finish(m)

    for k in range(7):
        arrived(smi, sm_s.at[k])
    exchange_drain(osnd, 2)
    exchange_drain(msg, 3)
    exchange_drain(msg2, 5)
    for m in range(3):
        sums_drain(m)
    for i in range(9):
        arrived(sgr.at[0], t_s.at[i])


def block_step(tok, cot, lens, smi, wq_s, wp_s, wf_s, wo_s):
    vmem = pl.BlockSpec(memory_space=pltpu.VMEM)
    smem = pl.BlockSpec(memory_space=pltpu.SMEM)
    anywhere = pl.BlockSpec(memory_space=pl.ANY)
    V, D = pltpu.VMEM, pltpu.SemaphoreType.DMA
    return pl.pallas_call(
        block_kernel,
        name="block",
        out_shape=(
            jax.ShapeDtypeStruct((32, 8, 768), BF),
            jax.ShapeDtypeStruct((32, 8, 768), BF),
            jax.ShapeDtypeStruct((96, 3072), BF),
            jax.ShapeDtypeStruct((96, 3072), BF),
            jax.ShapeDtypeStruct((768, 384), BF),
            jax.ShapeDtypeStruct((8, 128), F32),
            jax.ShapeDtypeStruct((1, 384), F32),
        ),
        in_specs=[vmem, vmem, smem, vmem, anywhere, anywhere, anywhere, anywhere],
        out_specs=(vmem,) * 7,
        scratch_shapes=[
            V((768, 2304), BF),
            V((768, 768), BF),
            V((8, 48, 16, 384), BF),
            V((8, 48, 16, 384), BF),
            V((2, 36, 16, 16, 384), BF),
            V((24, 16, 16, 384), BF),
            V((27, 4, 16, 384), BF),
            V((27, 16, 384), BF),
            V((3, 2560, 256), BF),
            V((3, 1024, 128), BF),
            V((3, 1024, 128), BF),
            V((3, 1024, 128), BF),
            V((3, 1024, 128), BF),
            V((3, 128, 1024), BF),
            V((128, 8, 384), BF),
            V((128, 8, 256), BF),
            V((128, 8, 384), BF),
            V((128, 8, 256), BF),
            V((128, 8, 256), BF),
            V((128, 8, 256), BF),
            V((128, 8, 256), BF),
            V((6144, 128), F32),
            V((256, 768), F32),
            V((256, 768), F32),
            V((256, 768), F32),
            V((8, 16, 768), BF),
            V((16, 768), F32),
            V((4, 8, 768), F32),
            V((4, 8, 768), F32),
            V((16, 768), F32),
            V((13, 16, 768), F32),
            V((256, 768), BF),
            V((256, 768), BF),
            V((256, 768), BF),
            V((768, 256), BF),
            V((768, 256), BF),
            V((256, 768), BF),
            V((256, 2304), BF),
            V((2, 256, 768), BF),
            D((4, 28)), D((4, 28)), D((4, 8)),
            D((7,)), D((7,)),
            D((6,)), D((6,)),
            D((36,)), D((36,)),
            D((3, 27)), D((3, 27)),
            D((3, 8)), D((3, 8)),
            D((10,)), D((10,)),
        ],
        compiler_params=pltpu.CompilerParams(
            collective_id=0, has_side_effects=True, vmem_limit_bytes=64 * 2**20
        ),
    )(tok, cot, lens, smi, wq_s, wp_s, wf_s, wo_s)


def per_device(
    tokens,
    out_grad,
    lengths,
    ln1_gain,
    ln1_bias,
    w_qkv,
    q_bias,
    v_bias,
    w_proj,
    proj_bias,
    ln2_gain,
    ln2_bias,
    w_fc,
    fc_bias,
    w_out,
    out_bias,
):
    sh = lax.axis_index("shard")
    vectors = jnp.stack(
        [ln1_gain, ln1_bias, q_bias, v_bias, proj_bias, ln2_gain, ln2_bias, out_bias]
    )
    column = lax.broadcasted_iota(jnp.int32, (8, 768), 1)
    vectors = jnp.where(column // 96 == sh, jnp.tile(vectors, (1, 8)), jnp.zeros((), BF))
    place384 = lax.broadcasted_iota(jnp.int32, (8, 768), 0) * 2 + column // 384
    wide = jnp.where(place384 == sh, jnp.tile(fc_bias[None, :], (8, 2)), jnp.zeros((), BF))
    smi = jnp.concatenate([vectors, wide], axis=0)
    wf_s = w_fc.reshape(6, 16, 3072)
    wo_s = w_out.reshape(24, 16, 768)
    block, in_grad, gq, gf, gt, rows, d_fb = block_step(
        tokens, out_grad, lengths, smi, w_qkv, w_proj, wf_s, wo_s
    )
    rows = rows[:, :96]
    return (
        block,
        in_grad,
        rows[0],
        rows[1],
        gq[:, :2304].astype(F32),
        rows[2],
        rows[3],
        gq[:, 2304:].astype(F32),
        rows[4],
        rows[5],
        rows[6],
        gf.astype(F32),
        d_fb[0],
        gt.astype(F32).T,
        rows[7],
    )


def solution(mesh):
    pieces = P(None, ("rep", "shard"), None)
    row, table = P("shard"), P("shard", None)
    kinds = (row, row, table, row, row, table, row, row, row, table, row, table, row)
    return jax.shard_map(
        per_device,
        mesh=mesh,
        in_specs=(pieces, pieces, P(), *kinds),
        out_specs=(pieces, pieces, *kinds),
        check_vma=False,
    )
```

```python
import functools
import math

import jax
import jax.numpy as jnp
from jax import lax
from jax.experimental import pallas as pl
from jax.experimental.pallas import tpu as pltpu
from jax.sharding import PartitionSpec as P

HEADS = 12
LAYERS = 12
EPSILON = 1e-05
MASKED = -1e30
MESH = pl.DeviceIdType.MESH
BF = jnp.bfloat16
F32 = jnp.float32
ALPHA = 1.0 / math.sqrt(LAYERS)
ROOT = math.sqrt(2.0 / math.pi)
CUBE = 0.044715
NT = (((1,), (1,)), ((), ()))
PAIR = (0, 2, 3, 5)
SINGLE = (1, 1, 4, 4)


def mm(a, b):
    return jnp.dot(a, b, preferred_element_type=F32)


def mm_nt(a, b):
    return lax.dot_general(a, b, NT, preferred_element_type=F32)


def mean(v):
    return jnp.mean(v, axis=-1, keepdims=True)


def normalize(v):
    centered = v - mean(v)
    rstd = lax.rsqrt(mean(centered * centered) + EPSILON)
    return centered * rstd, rstd


def norm_back(n, rstd, r):
    return (r - mean(r) - n * mean(r * n)) * rstd


def column_sum(v):
    return jnp.sum(v, axis=0, keepdims=True)


def roll_half(v):
    return pltpu.roll(v, 64, 1)


def place(x, y, z, c):
    return (y * 4 + (z // 2) * 2 + c, lax.rem(z, 2) * 4 + x)


def remote(src, dst, send, recv, device):
    return pltpu.make_async_remote_copy(
        src_ref=src, dst_ref=dst, send_sem=send, recv_sem=recv, device_id=device, device_id_type=MESH
    )


def arrived(ref, sem):
    pltpu.make_async_copy(ref, ref, sem).wait()


def block_kernel(
    tok, cot, lens, smi, wq_s, wp_s, wf_s, wo_s,
    bo, ig, gq_o, gf_o, go_t, sgo, fbo,
    wq, wp, wf, wo, gall, r0, r2, r3, pmat, qh, kh, vh, goh, turned, msg, msg2, rcv, rcv2, osnd, orcv, grcv, tmp,
    yv, acc1, acc2, smr, sm, fbs, fbg, sg, sgr, a1v, a2v, gmv, lt1, lt2, ov, g3, hv,
    ag_s, ag_r, ag_l, y_s, y_r, sm_s, sm_r, aa_s, aa_r, c_s, c_r, d_s, d_r, fin_s, fin_r, t_s, t_r,
):
    rep, sh = lax.axis_index("rep"), lax.axis_index("shard")
    me = rep * 8 + sh
    x, zl, y, c = lax.rem(sh, 4), sh // 4, rep // 4, lax.rem(rep, 2)
    z = lax.rem(rep // 2, 2) * 2 + zl
    sibling = place(x, y, z, 1 - c)

    def ring(v, k):
        return lax.rem(v + k + 4, 4)

    def along(dim, value):
        return place(*[value if d == dim else v for d, v in enumerate((x, y, z))], c)

    own = (x, y, z)

    barrier = pltpu.get_barrier_semaphore()

    def greet(step, carry):
        peer = lax.rem(me + step, 128)
        pl.semaphore_signal(
            barrier, inc=1, device_id=(peer // 8, lax.rem(peer, 8)), device_id_type=MESH
        )
        return carry

    lax.fori_loop(1, 128, greet, 0)
    pl.semaphore_wait(barrier, 127)

    def rows16(start, size):
        return pl.ds(pl.multiple_of(start, 16), size)

    def gathered(m, s, core, h):
        if m == 0:
            return wq.at[rows16(s * 96 + core * 48, 48), pl.ds(h * 1152, 1152)]
        if m == 1:
            return wp.at[rows16(s * 96 + core * 48, 48), pl.ds(h * 384, 384)]
        if m == 2:
            return wf.at[pl.ds(h * 4, 4), pl.ds(s * 6 + core * 3, 3)]
        return wo.at[s, pl.ds(h * 24 + core * 12, 12)]

    def shard_of(m, core, h):
        if m == 0:
            return wq_s.at[rows16(core * 48, 48), pl.ds(h * 1152, 1152)]
        if m == 1:
            return wp_s.at[rows16(core * 48, 48), pl.ds(h * 384, 384)]
        return gathered(m, sh, core, h)

    def sideways(m, s, core, h):
        return quarter(s, core, h, y) if m == 3 else gathered(m, s, core, h)

    def quarter(s, core, h, part):
        return wo.at[s, pl.ds(h * 24 + core * 12 + part * 3, 3)]

    def from_x(k):
        return zl * 4 + ring(x, -k)

    def from_z(j):
        return (1 - zl) * 4 + ring(x, -j)

    def own_copies(m):
        if m == 2:
            return [
                pltpu.make_async_copy(
                    wf_s.at[:, :, pl.ds(q * 384, 384)], wf.at[q, pl.ds(sh * 6, 6)], ag_l.at[m, q]
                )
                for q in range(8)
            ]
        if m == 3:
            return [
                pltpu.make_async_copy(
                    wo_s.at[:, :, pl.ds(h * 384, 384)], wo.at[sh, pl.ds(h * 24, 24)], ag_l.at[m, h]
                )
                for h in (0, 1)
            ]
        return [
            pltpu.make_async_copy(
                shard_of(m, core, h), gathered(m, sh, core, h), ag_l.at[m, core * 2 + h]
            )
            for core in (0, 1)
            for h in (0, 1)
        ]

    def beside(h):
        return along(2, ring(z, 1 - 2 * h))

    def gather_start(m):
        for copy in own_copies(m):
            copy.start()
        if m >= 2:
            for copy in own_copies(m):
                copy.wait()
        for h in (0, 1):
            for k in (1, 3):
                i = (k - 1) * 2 + h
                remote(
                    shard_of(m, c, h), gathered(m, sh, c, h), ag_s.at[m, i], ag_r.at[m, i],
                    along(0, ring(x, k)),
                ).start()

    def gather_beside(m):
        for h in (0, 1):
            src = shard_of(m, c, h) if m < 2 else sideways(m, sh, c, h)
            remote(
                src, sideways(m, sh, c, h), ag_s.at[m, 6 + h], ag_r.at[m, 6 + h], beside(h)
            ).start()

    def gather_relay_x(m):
        for k, h in ((1, 0), (3, 1), (1, 1), (3, 0), (2, 0), (2, 1)):
            i = (k - 1) * 2 + h
            piece = gathered(m, from_x(k), c, h)
            arrived(piece, ag_r.at[m, i])
            if (k, h) in ((1, 0), (3, 1)):
                remote(
                    piece, piece, ag_s.at[m, 2 + h], ag_r.at[m, 2 + h], along(0, ring(x, 1 - 2 * h))
                ).start()
            i = 6 + 2 * k + h
            part = sideways(m, from_x(k), c, h)
            remote(part, part, ag_s.at[m, i], ag_r.at[m, i], beside(h)).start()
            i = 14 + (k - 1) * 2 + h
            remote(piece, piece, ag_s.at[m, i], ag_r.at[m, i], sibling).start()

    def gather_relay_z(m):
        for j in (0, 1, 3, 2):
            for h in (0, 1):
                part = sideways(m, from_z(j), c, h)
                arrived(part, ag_r.at[m, 6 + 2 * j + h])
                if m == 3:
                    for off in (1, 2, 3):
                        i = (j * 2 + h) * 3 + off - 1
                        remote(part, part, y_s.at[i], y_r.at[i], along(1, ring(y, off))).start()
                    continue
                i = 20 + 2 * j + h
                remote(part, part, ag_s.at[m, i], ag_r.at[m, i], sibling).start()

    def gather_relay_y(m):
        for j in (0, 1, 3, 2):
            for h in (0, 1):
                for off in (1, 2, 3):
                    arrived(
                        quarter(from_z(j), c, h, ring(y, -off)), y_r.at[(j * 2 + h) * 3 + off - 1]
                    )
                piece = gathered(m, from_z(j), c, h)
                i = 20 + 2 * j + h
                remote(piece, piece, ag_s.at[m, i], ag_r.at[m, i], sibling).start()

    def gather_finish(m):
        if m < 2:
            for copy in own_copies(m):
                copy.wait()
        for h in (0, 1):
            for k in (1, 2, 3):
                arrived(gathered(m, from_x(k), 1 - c, h), ag_r.at[m, 14 + (k - 1) * 2 + h])
            for j in range(4):
                arrived(gathered(m, from_z(j), 1 - c, h), ag_r.at[m, 20 + 2 * j + h])

    def gather_drain(m):
        for h in (0, 1):
            for i in range(0, 28, 2):
                part = sideways if 6 <= i < 14 else gathered
                arrived(part(m, 0, 0, h), ag_s.at[m, i + h])
        if m == 3:
            for i in range(24):
                arrived(quarter(0, 0, 0, 0), y_s.at[i])

    def exchange_start(src, dst, i):
        def send(step, carry):
            peer = lax.rem(me + step, 128)
            remote(
                src.at[peer], dst.at[me], aa_s.at[i], aa_r.at[i], (peer // 8, lax.rem(peer, 8))
            ).start()
            return carry

        lax.fori_loop(1, 128, send, 0)
        dst[pl.ds(me, 1)] = src[pl.ds(me, 1)]

    def exchange_wait(dst, i):
        most = dst.at[pl.ds(0, 127)]
        arrived(most, aa_r.at[i])

    def exchange_drain(src, i):
        most = src.at[pl.ds(0, 127)]
        arrived(most, aa_s.at[i])

    lane = lax.broadcasted_iota(jnp.int32, (1, 128), 1)
    low = lane < 64
    half = lax.rem(me, 2)
    here = (lane >= half * 64) & (lane < half * 64 + 64)

    def lanes(i, count=1):
        return pl.ds(i * 128, count * 128)

    def put_groups(dst, b, per_group):
        stacked = jnp.stack([g.reshape(32, 8, 128) for g in per_group], axis=1)
        dst[:, :, b * 128 : (b + 1) * 128] = stacked.reshape(128, 8, 128).astype(BF)

    def get_groups(src, b):
        v = src[:, :, b * 128 : (b + 1) * 128].astype(F32).reshape(32, 4, 8, 128)
        return [v[:, g].reshape(256, 128) for g in range(4)]

    def put_positions(dst, b, v):
        dst[:, :, b * 128 : (b + 1) * 128] = v.reshape(128, 8, 128).astype(BF)

    def get_positions(src, b):
        return src[:, :, b * 128 : (b + 1) * 128].astype(F32).reshape(1024, 128)

    def block0(m, k, a):
        if m == 0:
            i = k * 4 + a
            return wo.at[i // 3, pl.ds(lax.rem(i, 3) * 16, 16)]
        return r0.at[(m - 1) * 12 + k * 4 + a]

    def block1(m, k, off):
        i = k * 3 + off - 1
        if m == 0:
            return wo.at[4 + i // 3, pl.ds((i % 3) * 16, 16)]
        return wf.at[(m - 1) * 4 + i // 3, pl.ds((i % 3) * 16, 16)]

    def core_start(m):
        for off in (1, 2, 3, 0):
            for k in range(3):
                a = ring(own[k], off)
                i = (m * 3 + k) * 4 + off
                remote(
                    gall.at[1 - c, m * 12 + k * 4 + a], block0(m, k, a), c_s.at[i], c_r.at[i], sibling
                ).start()

    def stage1_start(m):
        for off in (1, 2, 3):
            for k in range(3):
                a = ring(own[k], off)
                i = (m * 3 + k) * 4 + off
                arrived(block0(m, k, a), c_r.at[i])
                mine = gall.at[c, m * 12 + k * 4 + a]
                mine[...] = mine[...] + block0(m, k, a)[...]
                i = (m * 3 + k) * 3 + off - 1
                remote(
                    mine, block1(m, k, off), d_s.at[0, i], d_r.at[0, i], along(k, a)
                ).start()

    def stage2_start(m):
        for k in range(3):
            a = own[k]
            arrived(block0(m, k, a), c_r.at[(m * 3 + k) * 4])
            mine = gall.at[c, m * 12 + k * 4 + a]
            total = mine[...].astype(F32) + block0(m, k, a)[...].astype(F32)
            for off in (1, 2, 3):
                i = (m * 3 + k) * 3 + off - 1
                arrived(block1(m, k, off), d_r.at[0, i])
                total = total + block1(m, k, off)[...].astype(F32)
            mine[...] = total.astype(BF)
            dim = (k + 1) % 3
            for off in (1, 2, 3):
                i = (m * 3 + k) * 3 + off - 1
                b = ring(own[dim], off)
                remote(
                    mine.at[pl.ds(b * 4, 4)], r2.at[i], d_s.at[1, i], d_r.at[1, i], along(dim, b)
                ).start()

    def stage3_start(m):
        for k in range(3):
            mine = gall.at[c, m * 12 + k * 4 + own[k], pl.ds(own[(k + 1) % 3] * 4, 4)]
            total = mine[...].astype(F32)
            for off in (1, 2, 3):
                i = (m * 3 + k) * 3 + off - 1
                arrived(r2.at[i], d_r.at[1, i])
                total = total + r2[i].astype(F32)
            mine[...] = total.astype(BF)
            dim = (k + 2) % 3
            for off in (1, 2, 3):
                i = (m * 3 + k) * 3 + off - 1
                e = ring(own[dim], off)
                remote(mine.at[e], r3.at[i], d_s.at[2, i], d_r.at[2, i], along(dim, e)).start()

    def region(m, r):
        part, core = lax.rem(r // 2, 2) * 4 + r // 4, lax.rem(r, 2)
        if m == 2:
            return go_t.at[rows16(core * 384 + part * 48, 48)]
        out = gf_o if m == 1 else gq_o
        return out.at[rows16(core * 48, 48), pl.ds(pl.multiple_of(part * 384, 128), 384)]

    def share_start(m):
        for k in range(3):
            u = own[(k + 1) % 3] * 4 + own[(k + 2) % 3]
            total = gall[c, m * 12 + k * 4 + own[k], u].astype(F32)
            for off in (1, 2, 3):
                i = (m * 3 + k) * 3 + off - 1
                arrived(r3.at[i], d_r.at[2, i])
                total = total + r3[i].astype(F32)
            region(m, rep).at[pl.ds(k * 16, 16), :][...] = total.astype(BF)
        mine = region(m, rep)
        for k in range(1, 8):
            peer = lax.rem(rep // 2 + k, 8) * 2 + c
            remote(mine, mine, fin_s.at[m, k - 1], fin_r.at[m, k - 1], (peer, sh)).start()

    def strip(m, core):
        if m == 2:
            return go_t.at[rows16(core * 384, 384)]
        return (gf_o if m == 1 else gq_o).at[rows16(core * 48, 48)]

    def share_relay(m):
        for k in range(1, 8):
            peer = lax.rem(rep // 2 + 8 - k, 8) * 2 + c
            arrived(region(m, peer), fin_r.at[m, k - 1])
        remote(strip(m, c), strip(m, c), fin_s.at[m, 7], fin_r.at[m, 7], sibling).start()

    def share_finish(m):
        arrived(strip(m, 1 - c), fin_r.at[m, 7])

    def sums_drain(m):
        for k in range(3):
            for off in range(4):
                arrived(r0.at[0], c_s.at[(m * 3 + k) * 4 + off])
            for off in range(3):
                i = (m * 3 + k) * 3 + off
                arrived(r0.at[0], d_s.at[0, i])
                arrived(r2.at[0], d_s.at[1, i])
                arrived(r3.at[0], d_s.at[2, i])
        for k in range(7):
            arrived(region(m, rep), fin_s.at[m, k])
        arrived(strip(m, c), fin_s.at[m, 7])

    def vectors_start(stage):
        if stage == 0:
            remote(sg, sgr.at[12], t_s.at[9], t_r.at[9], sibling).start()
            return
        dim = stage - 1
        slot = dim * 4 + own[dim]
        sgr[pl.ds(slot, 1)] = sg[...].reshape(1, 16, 768)
        for off in (1, 2, 3):
            i = dim * 3 + off - 1
            remote(
                sgr.at[slot], sgr.at[slot], t_s.at[i], t_r.at[i], along(dim, ring(own[dim], off))
            ).start()

    def vectors_finish(stage):
        if stage == 0:
            arrived(sgr.at[12], t_r.at[9])
            arrived(sg, t_s.at[9])
            sg[...] = sg[...] + sgr[12]
            return
        dim = stage - 1
        for off in (1, 2, 3):
            i = dim * 3 + off - 1
            arrived(sgr.at[dim * 4 + ring(own[dim], -off)], t_r.at[i])
        sg[...] = (sgr[dim * 4] + sgr[dim * 4 + 1]) + (sgr[dim * 4 + 2] + sgr[dim * 4 + 3])

    gather_start(0)
    gather_beside(0)
    for k in range(1, 8):
        remote(
            smi, smr.at[sh], sm_s.at[k - 1], sm_r.at[k - 1], (rep, lax.rem(sh + k, 8))
        ).start()
    smr[pl.ds(sh, 1)] = smi[...].reshape(1, 16, 768)
    for k in range(1, 8):
        arrived(smr.at[lax.rem(sh + 8 - k, 8)], sm_r.at[k - 1])
    sm[...] = jnp.sum(smr[...].astype(F32), axis=0)
    for q in range(4):
        fbs[q] = jnp.broadcast_to(sm[8 + q : 9 + q, :], (8, 768))
    x_in = tok[...].astype(F32).reshape(256, 768)
    n1, rstd1 = normalize(x_in)
    a1 = n1 * sm[0:1, :] + sm[1:2, :]
    a1v[...] = a1.astype(BF)
    gather_relay_x(0)
    for m in range(1, 4):
        gather_start(m)
    gather_relay_z(0)
    for m in range(1, 4):
        gather_beside(m)
    gather_finish(0)
    gather_relay_x(1)

    for b in range(9):
        v = mm(a1v[...], wq[:, b * 256 : (b + 1) * 256])
        if b < 3:
            v = v + sm[2:3, b * 256 : (b + 1) * 256]
        if b >= 6:
            v = v + sm[3:4, (b - 6) * 256 : (b - 5) * 256]
        tmp[pl.ds(b * 512, 256)] = v[:, :128]
        tmp[pl.ds(b * 512 + 256, 256)] = v[:, 128:]

    def natural(which, b):
        return tmp[pl.ds((which * 6 + b) * 256, 256)]

    for which in range(3):
        put_groups(msg, which, [natural(which, PAIR[g]) for g in range(4)])
    exchange_start(msg, rcv, 0)
    packed = []
    for g in range(4):
        qb, kb = natural(0, SINGLE[g]), natural(1, SINGLE[g])
        packed.append(
            jnp.where(low, qb, roll_half(kb)) if g % 2 == 0 else jnp.where(low, roll_half(qb), kb)
        )
    put_groups(msg2, 0, packed)
    put_groups(msg2, 1, [natural(2, SINGLE[g]) for g in range(4)])
    exchange_start(msg2, rcv2, 4)
    for m in (2, 3):
        gather_relay_x(m)
    exchange_wait(rcv, 0)

    zero = jnp.zeros((1024, 128), F32)

    def load_head(h, qq, kk, vv, mask, vmask):
        qh[h] = jnp.where(mask, qq * 0.125, zero).astype(BF)
        kh[h] = jnp.where(mask, kk, zero).astype(BF)
        vv = jnp.where(vmask, vv, zero)
        vh[h] = vv.astype(BF)
        turned[h] = jnp.transpose(vv).astype(BF)

    q01, k01, v01 = [get_positions(rcv, b) for b in range(3)]
    load_head(0, q01, k01, v01, low, low)
    load_head(1, q01, k01, v01, ~low, ~low)
    length = lens[me // 4]
    offsets = (0, 256, 768, 1536)
    tmp[pl.ds(0, 2048)] = jnp.zeros((2048, 128), F32)

    def attend(h, carry):
        for i in range(4):
            n = (i + 1) * 256
            s = mm_nt(kh[h, :n, :], qh[h, i * 256 : n, :])
            key = lax.broadcasted_iota(jnp.int32, (n, 256), 0)
            limit = lax.broadcasted_iota(jnp.int32, (1, 256), 1) + (i * 256 + 1)
            s = jnp.where(key < jnp.minimum(limit, length), s, MASKED)
            e = jnp.exp(s - jnp.max(s, axis=0, keepdims=True))
            p = (e * (1.0 / jnp.sum(e, axis=0, keepdims=True))).astype(BF)
            pmat[h, offsets[i] : offsets[i] + n, :] = p
            o = jnp.transpose(mm(turned[h, :, :n], p))
            tmp[pl.ds((h // 2) * 1024 + i * 256, 256)] += o
        return carry

    lax.fori_loop(0, 2, attend, 0)
    gather_relay_z(3)
    exchange_wait(rcv2, 4)
    qks, vs = [get_positions(rcv2, b) for b in range(2)]
    load_head(2, qks, roll_half(qks), vs, low, here)
    lax.fori_loop(2, 3, attend, 0)
    put_positions(osnd, 0, tmp[pl.ds(0, 1024)])
    put_positions(osnd, 1, tmp[pl.ds(1024, 1024)])
    exchange_start(osnd, orcv, 1)
    for h in range(3):
        turned[h] = jnp.transpose(kh[h].astype(F32)).astype(BF)
    for m in (1, 2):
        gather_relay_z(m)
    gather_relay_y(3)
    for m in range(1, 4):
        gather_finish(m)
    exchange_wait(orcv, 1)

    pairs, singles = get_groups(orcv, 0), get_groups(orcv, 1)
    blocks = [None] * 6
    for g in range(4):
        blocks[PAIR[g]] = pairs[g]
    blocks[1], blocks[4] = singles[0] + singles[1], singles[2] + singles[3]
    for b in range(6):
        ov[:, b * 128 : (b + 1) * 128] = blocks[b].astype(BF)
    x_in = tok[...].astype(F32).reshape(256, 768)
    g_in = cot[...].astype(F32).reshape(256, 768)
    y_mid = x_in + ALPHA * (mm(ov[...], wp[...]) + sm[4:5, :])
    yv[...] = y_mid
    n2, rstd2 = normalize(y_mid)
    a2 = n2 * sm[5:6, :] + sm[6:7, :]
    a2v[...] = a2.astype(BF)
    gm = (ALPHA * g_in).astype(BF)
    gmv[...] = gm
    gm = gm.astype(F32)
    sg[7:8, :] = column_sum(gm)
    lt1[...] = jnp.transpose(a2v[...].astype(F32)).astype(BF)
    lt2[...] = jnp.transpose(gm).astype(BF)
    acc1[...] = jnp.zeros((256, 768), F32)
    acc2[...] = jnp.zeros((256, 768), F32)

    def color(k, ux, uy, uz):
        order = ((ux, uy, uz), (uy, uz, ux), (uz, ux, uy))[k]
        return order[0], order[1] * 4 + order[2]

    def put_columns(m, q, v, first, shards):
        uy, zq = lax.rem(q, 4), q // 4
        for s in range(first, first + shards):
            for core in range(2):
                for k in range(3):
                    r = (s - first) * 96 + core * 48 + k * 16
                    a, u = color(k, s % 4, uy, zq * 2 + s // 4)
                    gall[core, m * 12 + k * 4 + a, u] = v[r : r + 16]

    def put_rows(m, q, v, core):
        ux, zq = lax.rem(q, 4), q // 4
        for e in range(8):
            for k in range(3):
                r = e * 48 + k * 16
                a, u = color(k, ux, e % 4, (e // 4) * 2 + zq)
                gall[core, m * 12 + k * 4 + a, u] = v[r : r + 16]

    def feed(p, carry):
        left, right = 2 * p, 2 * p + 1
        w1 = jnp.concatenate([wf[q].reshape(768, 384) for q in (left, right)], axis=1)
        w2 = jnp.concatenate(
            [
                jnp.concatenate([wo[q, h * 24 : h * 24 + 24].reshape(384, 384) for h in (0, 1)], axis=1)
                for q in (left, right)
            ],
            axis=0,
        )
        u = mm(a2v[...], w1) + fbs[p, 0:1, :]
        uu = u * u
        t = jnp.tanh(ROOT * (u + CUBE * (u * uu)))
        hv[0] = (0.5 * u * (1.0 + t)).astype(BF)
        slope = 0.5 * (1.0 + t) + 0.5 * u * (1.0 - t * t) * (ROOT * (1.0 + (3.0 * CUBE) * uu))
        gu = (mm_nt(gmv[...], w2) * slope).astype(BF)
        hv[1] = gu
        fbg[p] = jnp.broadcast_to(column_sum(gu.astype(F32)), (8, 768))
        acc1[...] += mm(hv[0], w2)
        acc2[...] += mm_nt(hv[1], w1)
        for half in (0, 1):
            v = mm(lt1[half * 384 : half * 384 + 384, :], hv[1]).astype(BF)
            put_columns(1, left, v[:, 0:384], half * 4, 4)
            put_columns(1, right, v[:, 384:768], half * 4, 4)
            v = mm(lt2[half * 384 : half * 384 + 384, :], hv[0]).astype(BF)
            put_rows(2, left, v[:, 0:384], half)
            put_rows(2, right, v[:, 384:768], half)
        return carry

    lax.fori_loop(0, 4, feed, 0)
    core_start(1)
    core_start(2)
    block = yv[...] + ALPHA * (acc1[...] + sm[7:8, :])
    bo[...] = block.reshape(32, 8, 768).astype(BF)
    for q in range(4):
        sg[8 + q : 9 + q, :] = fbg[q, 0:1, :]
    sg[12:16, :] = jnp.zeros((4, 768), F32)
    n2, rstd2 = normalize(yv[...])
    ga2 = acc2[...]
    sg[5:6, :] = column_sum(ga2 * n2)
    sg[6:7, :] = column_sum(ga2)
    gyy = cot[...].astype(F32).reshape(256, 768) + norm_back(n2, rstd2, ga2 * sm[5:6, :])
    acc1[...] = gyy
    ga = (ALPHA * gyy).astype(BF)
    a2v[...] = ga
    sg[4:5, :] = column_sum(ga.astype(F32))
    lt1[...] = jnp.transpose(ov[...].astype(F32)).astype(BF)
    for half in (0, 1):
        v = mm(lt1[half * 384 : half * 384 + 384, :], a2v[...]).astype(BF)
        put_columns(0, 6, v[:, 0:384], half * 4, 4)
        put_columns(0, 7, v[:, 384:768], half * 4, 4)
    go = mm_nt(a2v[...], wp[...])
    exchange_drain(osnd, 1)
    for m in range(4):
        gather_drain(m)
    put_groups(osnd, 0, [go[:, PAIR[g] * 128 : PAIR[g] * 128 + 128] for g in range(4)])
    put_groups(osnd, 1, [go[:, SINGLE[g] * 128 : SINGLE[g] * 128 + 128] for g in range(4)])
    exchange_start(osnd, grcv, 2)
    lt1[...] = jnp.transpose(a1v[...].astype(F32)).astype(BF)
    exchange_wait(grcv, 2)

    for m in (1, 2):
        stage1_start(m)
    go01, gos = get_positions(grcv, 0), get_positions(grcv, 1)
    goh[0] = jnp.where(low, go01, zero).astype(BF)
    goh[1] = jnp.where(low, zero, go01).astype(BF)
    goh[2] = jnp.where(here, gos, zero).astype(BF)
    tmp[...] = jnp.zeros((6144, 128), F32)

    def attend_back(h, carry):
        base = (h // 2) * 1024
        for i in range(4):
            n = (i + 1) * 256
            g_rows = goh[h, i * 256 : n, :]
            p = pmat[h, offsets[i] : offsets[i] + n, :]
            pf = p.astype(F32)
            gp = mm_nt(vh[h, :n, :], g_rows)
            inner = jnp.sum(pf * gp, axis=0, keepdims=True)
            gs = (pf * (gp - inner)).astype(BF)
            tmp[pl.ds(base + i * 256, 256)] += jnp.transpose(mm(turned[h, :, :n], gs)) * 0.125
            tmp[pl.ds(2048 + base, n)] += mm(gs, qh[h, i * 256 : n, :])
            tmp[pl.ds(4096 + base, n)] += mm(p, g_rows)
        return carry

    lax.fori_loop(0, 2, attend_back, 0)
    exchange_drain(msg, 0)
    for b in range(3):
        put_positions(msg, b, tmp[pl.ds(b * 2048, 1024)])
    exchange_start(msg, rcv, 3)
    lax.fori_loop(2, 3, attend_back, 0)
    exchange_drain(msg2, 4)
    put_positions(msg2, 0, tmp[pl.ds(1024, 1024)] + roll_half(tmp[pl.ds(3072, 1024)]))
    put_positions(msg2, 1, tmp[pl.ds(5120, 1024)])
    exchange_start(msg2, rcv2, 5)
    exchange_wait(rcv, 3)
    exchange_wait(rcv2, 5)

    got = [get_groups(rcv, b) for b in range(3)] + [get_groups(rcv2, b) for b in range(2)]
    for which in range(3):
        blocks = [None] * 6
        for g in range(4):
            blocks[PAIR[g]] = got[which][g]
        for b, e, o in ((1, 0, 1), (4, 2, 3)):
            if which == 0:
                blocks[b] = jnp.where(low, got[3][e], roll_half(got[3][o]))
            elif which == 1:
                blocks[b] = jnp.where(low, roll_half(got[3][e]), got[3][o])
            else:
                blocks[b] = got[4][e] + got[4][o]
        for b in range(6):
            at = which * 768 + b * 128
            g3[:, at : at + 128] = blocks[b].astype(BF)
            if which != 1:
                row = 2 if which == 0 else 3
                sg[row : row + 1, b * 128 : b * 128 + 128] = column_sum(blocks[b])

    def qkv_grad(p, carry):
        cols = g3[:, pl.ds(pl.multiple_of(p * 768, 128), 768)]
        for half in (0, 1):
            v = mm(lt1[half * 384 : half * 384 + 384, :], cols).astype(BF)
            put_columns(0, 2 * p, v[:, 0:384], half * 4, 4)
            put_columns(0, 2 * p + 1, v[:, 384:768], half * 4, 4)
        return carry

    lax.fori_loop(0, 3, qkv_grad, 0)
    core_start(0)
    for m in (1, 2):
        stage2_start(m)
    ga1 = mm_nt(g3[...], wq[...])
    n1, rstd1 = normalize(tok[...].astype(F32).reshape(256, 768))
    sg[0:1, :] = column_sum(ga1 * n1)
    sg[1:2, :] = column_sum(ga1)
    gx = acc1[...] + norm_back(n1, rstd1, ga1 * sm[0:1, :])
    ig[...] = gx.reshape(32, 8, 768).astype(BF)

    vectors_start(0)
    for m in (1, 2):
        stage3_start(m)
    stage1_start(0)
    vectors_finish(0)
    vectors_start(1)
    for m in (1, 2):
        share_start(m)
    stage2_start(0)
    vectors_finish(1)
    vectors_start(2)
    for m in (1, 2):
        share_relay(m)
    stage3_start(0)
    vectors_finish(2)
    vectors_start(3)
    share_start(0)
    vectors_finish(3)
    lead = pltpu.roll(sg[0:8, :], lax.rem(8 - sh, 8) * 96, 1)
    sgo[...] = lead[:, 0:128]
    wide = column_sum(
        jnp.where(lax.broadcasted_iota(jnp.int32, (4, 768), 0) == sh // 2, sg[8:12, :], 0.0)
    )
    fbo[...] = jnp.where(lax.rem(sh, 2) == 0, wide[:, 0:384], wide[:, 384:768])
    share_relay(0)
    for m in range(3):
        share_finish(m)

    for k in range(7):
        arrived(smi, sm_s.at[k])
    exchange_drain(osnd, 2)
    exchange_drain(msg, 3)
    exchange_drain(msg2, 5)
    for m in range(3):
        sums_drain(m)
    for i in range(9):
        arrived(sgr.at[0], t_s.at[i])


def block_step(tok, cot, lens, smi, wq_s, wp_s, wf_s, wo_s):
    vmem = pl.BlockSpec(memory_space=pltpu.VMEM)
    smem = pl.BlockSpec(memory_space=pltpu.SMEM)
    anywhere = pl.BlockSpec(memory_space=pl.ANY)
    V, D = pltpu.VMEM, pltpu.SemaphoreType.DMA
    return pl.pallas_call(
        block_kernel,
        name="block",
        out_shape=(
            jax.ShapeDtypeStruct((32, 8, 768), BF),
            jax.ShapeDtypeStruct((32, 8, 768), BF),
            jax.ShapeDtypeStruct((96, 3072), BF),
            jax.ShapeDtypeStruct((96, 3072), BF),
            jax.ShapeDtypeStruct((768, 384), BF),
            jax.ShapeDtypeStruct((8, 128), F32),
            jax.ShapeDtypeStruct((1, 384), F32),
        ),
        in_specs=[vmem, vmem, smem, vmem, anywhere, anywhere, anywhere, anywhere],
        out_specs=(vmem,) * 7,
        scratch_shapes=[
            V((768, 2304), BF),
            V((768, 768), BF),
            V((8, 48, 16, 384), BF),
            V((8, 48, 16, 384), BF),
            V((2, 36, 16, 16, 384), BF),
            V((24, 16, 16, 384), BF),
            V((27, 4, 16, 384), BF),
            V((27, 16, 384), BF),
            V((3, 2560, 256), BF),
            V((3, 1024, 128), BF),
            V((3, 1024, 128), BF),
            V((3, 1024, 128), BF),
            V((3, 1024, 128), BF),
            V((3, 128, 1024), BF),
            V((128, 8, 384), BF),
            V((128, 8, 256), BF),
            V((128, 8, 384), BF),
            V((128, 8, 256), BF),
            V((128, 8, 256), BF),
            V((128, 8, 256), BF),
            V((128, 8, 256), BF),
            V((6144, 128), F32),
            V((256, 768), F32),
            V((256, 768), F32),
            V((256, 768), F32),
            V((8, 16, 768), BF),
            V((16, 768), F32),
            V((4, 8, 768), F32),
            V((4, 8, 768), F32),
            V((16, 768), F32),
            V((13, 16, 768), F32),
            V((256, 768), BF),
            V((256, 768), BF),
            V((256, 768), BF),
            V((768, 256), BF),
            V((768, 256), BF),
            V((256, 768), BF),
            V((256, 2304), BF),
            V((2, 256, 768), BF),
            D((4, 28)), D((4, 28)), D((4, 8)), D((24,)), D((24,)),
            D((7,)), D((7,)),
            D((6,)), D((6,)),
            D((36,)), D((36,)),
            D((3, 27)), D((3, 27)),
            D((3, 8)), D((3, 8)),
            D((10,)), D((10,)),
        ],
        compiler_params=pltpu.CompilerParams(
            collective_id=0, has_side_effects=True, vmem_limit_bytes=64 * 2**20
        ),
    )(tok, cot, lens, smi, wq_s, wp_s, wf_s, wo_s)


def per_device(
    tokens,
    out_grad,
    lengths,
    ln1_gain,
    ln1_bias,
    w_qkv,
    q_bias,
    v_bias,
    w_proj,
    proj_bias,
    ln2_gain,
    ln2_bias,
    w_fc,
    fc_bias,
    w_out,
    out_bias,
):
    sh = lax.axis_index("shard")
    vectors = jnp.stack(
        [ln1_gain, ln1_bias, q_bias, v_bias, proj_bias, ln2_gain, ln2_bias, out_bias]
    )
    column = lax.broadcasted_iota(jnp.int32, (8, 768), 1)
    vectors = jnp.where(column // 96 == sh, jnp.tile(vectors, (1, 8)), jnp.zeros((), BF))
    place384 = lax.broadcasted_iota(jnp.int32, (8, 768), 0) * 2 + column // 384
    wide = jnp.where(place384 == sh, jnp.tile(fc_bias[None, :], (8, 2)), jnp.zeros((), BF))
    smi = jnp.concatenate([vectors, wide], axis=0)
    wf_s = w_fc.reshape(6, 16, 3072)
    wo_s = w_out.reshape(24, 16, 768)
    block, in_grad, gq, gf, gt, rows, d_fb = block_step(
        tokens, out_grad, lengths, smi, w_qkv, w_proj, wf_s, wo_s
    )
    rows = rows[:, :96]
    return (
        block,
        in_grad,
        rows[0],
        rows[1],
        gq[:, :2304].astype(F32),
        rows[2],
        rows[3],
        gq[:, 2304:].astype(F32),
        rows[4],
        rows[5],
        rows[6],
        gf.astype(F32),
        d_fb[0],
        gt.astype(F32).T,
        rows[7],
    )


def solution(mesh):
    pieces = P(None, ("rep", "shard"), None)
    row, table = P("shard"), P("shard", None)
    kinds = (row, row, table, row, row, table, row, row, row, table, row, table, row)
    return jax.shard_map(
        per_device,
        mesh=mesh,
        in_specs=(pieces, pieces, P(), *kinds),
        out_specs=(pieces, pieces, *kinds),
        check_vma=False,
    )
```

```python
import functools
import math

import jax
import jax.numpy as jnp
from jax import lax
from jax.experimental import pallas as pl
from jax.experimental.pallas import tpu as pltpu
from jax.sharding import PartitionSpec as P

HEADS = 12
LAYERS = 12
EPSILON = 1e-05
MASKED = -1e30
MESH = pl.DeviceIdType.MESH
BF = jnp.bfloat16
F32 = jnp.float32
ALPHA = 1.0 / math.sqrt(LAYERS)
ROOT = math.sqrt(2.0 / math.pi)
CUBE = 0.044715
NT = (((1,), (1,)), ((), ()))
PAIR = (0, 2, 3, 5)
SINGLE = (1, 1, 4, 4)


def mm(a, b):
    return jnp.dot(a, b, preferred_element_type=F32)


def mm_nt(a, b):
    return lax.dot_general(a, b, NT, preferred_element_type=F32)


def mean(v):
    return jnp.mean(v, axis=-1, keepdims=True)


def normalize(v):
    centered = v - mean(v)
    rstd = lax.rsqrt(mean(centered * centered) + EPSILON)
    return centered * rstd, rstd


def norm_back(n, rstd, r):
    return (r - mean(r) - n * mean(r * n)) * rstd


def column_sum(v):
    return jnp.sum(v, axis=0, keepdims=True)


def roll_half(v):
    return pltpu.roll(v, 64, 1)


def place(x, y, z, c):
    return (y * 4 + (z // 2) * 2 + c, lax.rem(z, 2) * 4 + x)


def remote(src, dst, send, recv, device):
    return pltpu.make_async_remote_copy(
        src_ref=src, dst_ref=dst, send_sem=send, recv_sem=recv, device_id=device, device_id_type=MESH
    )


def arrived(ref, sem):
    pltpu.make_async_copy(ref, ref, sem).wait()


def block_kernel(
    tok, cot, lens, smi, wq_s, wp_s, wf_s, wo_s,
    bo, ig, gq_o, gf_o, go_t, sgo, fbo,
    wq, wp, wf, wo, gall, r0, r2, r3, pmat, qh, kh, vh, goh, turned, msg, msg2, rcv, rcv2, osnd, orcv, grcv, tmp,
    yv, acc1, acc2, smr, sm, fbs, fbg, sg, sgr, a1v, a2v, gmv, lt1, lt2, ov, g3, hv,
    ag_s, ag_r, ag_l, sm_s, sm_r, aa_s, aa_r, c_s, c_r, d_s, d_r, fin_s, fin_r, t_s, t_r,
):
    rep, sh = lax.axis_index("rep"), lax.axis_index("shard")
    me = rep * 8 + sh
    x, zl, y, c = lax.rem(sh, 4), sh // 4, rep // 4, lax.rem(rep, 2)
    z = lax.rem(rep // 2, 2) * 2 + zl
    sibling = place(x, y, z, 1 - c)

    def ring(v, k):
        return lax.rem(v + k + 4, 4)

    def along(dim, value):
        return place(*[value if d == dim else v for d, v in enumerate((x, y, z))], c)

    own = (x, y, z)

    barrier = pltpu.get_barrier_semaphore()

    def greet(step, carry):
        peer = lax.rem(me + step, 128)
        pl.semaphore_signal(
            barrier, inc=1, device_id=(peer // 8, lax.rem(peer, 8)), device_id_type=MESH
        )
        return carry

    lax.fori_loop(1, 128, greet, 0)
    pl.semaphore_wait(barrier, 127)

    def rows16(start, size):
        return pl.ds(pl.multiple_of(start, 16), size)

    def gathered(m, s, core, h):
        if m == 0:
            return wq.at[rows16(s * 96 + core * 48, 48), pl.ds(h * 1152, 1152)]
        if m == 1:
            return wp.at[rows16(s * 96 + core * 48, 48), pl.ds(h * 384, 384)]
        if m == 2:
            return wf.at[pl.ds(h * 4, 4), pl.ds(s * 6 + core * 3, 3)]
        return wo.at[s, pl.ds(h * 24 + core * 12, 12)]

    def shard_of(m, core, h):
        if m == 0:
            return wq_s.at[rows16(core * 48, 48), pl.ds(h * 1152, 1152)]
        if m == 1:
            return wp_s.at[rows16(core * 48, 48), pl.ds(h * 384, 384)]
        return gathered(m, sh, core, h)

    def from_x(k):
        return zl * 4 + ring(x, -k)

    def from_z(j):
        return (1 - zl) * 4 + ring(x, -j)

    def own_copies(m):
        if m == 2:
            return [
                pltpu.make_async_copy(
                    wf_s.at[:, :, pl.ds(q * 384, 384)], wf.at[q, pl.ds(sh * 6, 6)], ag_l.at[m, q]
                )
                for q in range(8)
            ]
        if m == 3:
            return [
                pltpu.make_async_copy(
                    wo_s.at[:, :, pl.ds(h * 384, 384)], wo.at[sh, pl.ds(h * 24, 24)], ag_l.at[m, h]
                )
                for h in (0, 1)
            ]
        return [
            pltpu.make_async_copy(
                shard_of(m, core, h), gathered(m, sh, core, h), ag_l.at[m, core * 2 + h]
            )
            for core in (0, 1)
            for h in (0, 1)
        ]

    def beside(h):
        return along(2, ring(z, 1 - 2 * h))

    def gather_start(m):
        for copy in own_copies(m):
            copy.start()
        if m >= 2:
            for copy in own_copies(m):
                copy.wait()
        for h in (0, 1):
            remote(
                shard_of(m, c, h), gathered(m, sh, c, h), ag_s.at[m, 6 + h], ag_r.at[m, 6 + h], beside(h)
            ).start()
            for k in (1, 3):
                i = (k - 1) * 2 + h
                remote(
                    shard_of(m, c, h), gathered(m, sh, c, h), ag_s.at[m, i], ag_r.at[m, i],
                    along(0, ring(x, k)),
                ).start()

    def gather_relay_x(m):
        for k, h in ((1, 0), (3, 1), (1, 1), (3, 0), (2, 0), (2, 1)):
            i = (k - 1) * 2 + h
            piece = gathered(m, from_x(k), c, h)
            arrived(piece, ag_r.at[m, i])
            if (k, h) in ((1, 0), (3, 1)):
                remote(
                    piece, piece, ag_s.at[m, 2 + h], ag_r.at[m, 2 + h], along(0, ring(x, 1 - 2 * h))
                ).start()
            i = 6 + 2 * k + h
            remote(piece, piece, ag_s.at[m, i], ag_r.at[m, i], beside(h)).start()
            i = 14 + (k - 1) * 2 + h
            remote(piece, piece, ag_s.at[m, i], ag_r.at[m, i], sibling).start()

    def gather_relay_z(m):
        for j in (0, 1, 3, 2):
            for h in (0, 1):
                piece = gathered(m, from_z(j), c, h)
                arrived(piece, ag_r.at[m, 6 + 2 * j + h])
                i = 20 + 2 * j + h
                remote(piece, piece, ag_s.at[m, i], ag_r.at[m, i], sibling).start()

    def gather_finish(m):
        if m < 2:
            for copy in own_copies(m):
                copy.wait()
        for h in (0, 1):
            for k in (1, 2, 3):
                arrived(gathered(m, from_x(k), 1 - c, h), ag_r.at[m, 14 + (k - 1) * 2 + h])
            for j in range(4):
                arrived(gathered(m, from_z(j), 1 - c, h), ag_r.at[m, 20 + 2 * j + h])

    def gather_drain(m):
        for h in (0, 1):
            for i in range(0, 28, 2):
                arrived(gathered(m, 0, 0, h), ag_s.at[m, i + h])

    def exchange_start(src, dst, i):
        def send(step, carry):
            peer = lax.rem(me + step, 128)
            remote(
                src.at[peer], dst.at[me], aa_s.at[i], aa_r.at[i], (peer // 8, lax.rem(peer, 8))
            ).start()
            return carry

        lax.fori_loop(1, 128, send, 0)
        dst[pl.ds(me, 1)] = src[pl.ds(me, 1)]

    def exchange_wait(dst, i):
        most = dst.at[pl.ds(0, 127)]
        arrived(most, aa_r.at[i])

    def exchange_drain(src, i):
        most = src.at[pl.ds(0, 127)]
        arrived(most, aa_s.at[i])

    lane = lax.broadcasted_iota(jnp.int32, (1, 128), 1)
    low = lane < 64
    half = lax.rem(me, 2)
    here = (lane >= half * 64) & (lane < half * 64 + 64)

    def lanes(i, count=1):
        return pl.ds(i * 128, count * 128)

    def put_groups(dst, b, per_group):
        stacked = jnp.stack([g.reshape(32, 8, 128) for g in per_group], axis=1)
        dst[:, :, b * 128 : (b + 1) * 128] = stacked.reshape(128, 8, 128).astype(BF)

    def get_groups(src, b):
        v = src[:, :, b * 128 : (b + 1) * 128].astype(F32).reshape(32, 4, 8, 128)
        return [v[:, g].reshape(256, 128) for g in range(4)]

    def put_positions(dst, b, v):
        dst[:, :, b * 128 : (b + 1) * 128] = v.reshape(128, 8, 128).astype(BF)

    def get_positions(src, b):
        return src[:, :, b * 128 : (b + 1) * 128].astype(F32).reshape(1024, 128)

    def block0(m, k, a):
        if m == 0:
            i = k * 4 + a
            return wo.at[i // 3, pl.ds(lax.rem(i, 3) * 16, 16)]
        return r0.at[(m - 1) * 12 + k * 4 + a]

    def block1(m, k, off):
        i = k * 3 + off - 1
        if m == 0:
            return wo.at[4 + i // 3, pl.ds((i % 3) * 16, 16)]
        return wf.at[(m - 1) * 4 + i // 3, pl.ds((i % 3) * 16, 16)]

    def core_start(m):
        for off in (1, 2, 3, 0):
            for k in range(3):
                a = ring(own[k], off)
                i = (m * 3 + k) * 4 + off
                remote(
                    gall.at[1 - c, m * 12 + k * 4 + a], block0(m, k, a), c_s.at[i], c_r.at[i], sibling
                ).start()

    def stage1_start(m):
        for off in (1, 2, 3):
            for k in range(3):
                a = ring(own[k], off)
                i = (m * 3 + k) * 4 + off
                arrived(block0(m, k, a), c_r.at[i])
                mine = gall.at[c, m * 12 + k * 4 + a]
                mine[...] = mine[...] + block0(m, k, a)[...]
                i = (m * 3 + k) * 3 + off - 1
                remote(
                    mine, block1(m, k, off), d_s.at[0, i], d_r.at[0, i], along(k, a)
                ).start()

    def stage2_start(m):
        for k in range(3):
            a = own[k]
            arrived(block0(m, k, a), c_r.at[(m * 3 + k) * 4])
            mine = gall.at[c, m * 12 + k * 4 + a]
            total = mine[...].astype(F32) + block0(m, k, a)[...].astype(F32)
            for off in (1, 2, 3):
                i = (m * 3 + k) * 3 + off - 1
                arrived(block1(m, k, off), d_r.at[0, i])
                total = total + block1(m, k, off)[...].astype(F32)
            mine[...] = total.astype(BF)
            dim = (k + 1) % 3
            for off in (1, 2, 3):
                i = (m * 3 + k) * 3 + off - 1
                b = ring(own[dim], off)
                remote(
                    mine.at[pl.ds(b * 4, 4)], r2.at[i], d_s.at[1, i], d_r.at[1, i], along(dim, b)
                ).start()

    def stage3_start(m):
        for k in range(3):
            mine = gall.at[c, m * 12 + k * 4 + own[k], pl.ds(own[(k + 1) % 3] * 4, 4)]
            total = mine[...].astype(F32)
            for off in (1, 2, 3):
                i = (m * 3 + k) * 3 + off - 1
                arrived(r2.at[i], d_r.at[1, i])
                total = total + r2[i].astype(F32)
            mine[...] = total.astype(BF)
            dim = (k + 2) % 3
            for off in (1, 2, 3):
                i = (m * 3 + k) * 3 + off - 1
                e = ring(own[dim], off)
                remote(mine.at[e], r3.at[i], d_s.at[2, i], d_r.at[2, i], along(dim, e)).start()

    def region(m, r):
        part, core = lax.rem(r // 2, 2) * 4 + r // 4, lax.rem(r, 2)
        if m == 2:
            return go_t.at[rows16(core * 384 + part * 48, 48)]
        out = gf_o if m == 1 else gq_o
        return out.at[rows16(core * 48, 48), pl.ds(pl.multiple_of(part * 384, 128), 384)]

    def share_start(m):
        for k in range(3):
            u = own[(k + 1) % 3] * 4 + own[(k + 2) % 3]
            total = gall[c, m * 12 + k * 4 + own[k], u].astype(F32)
            for off in (1, 2, 3):
                i = (m * 3 + k) * 3 + off - 1
                arrived(r3.at[i], d_r.at[2, i])
                total = total + r3[i].astype(F32)
            region(m, rep).at[pl.ds(k * 16, 16), :][...] = total.astype(BF)
        mine = region(m, rep)
        for k in range(1, 8):
            peer = lax.rem(rep // 2 + k, 8) * 2 + c
            remote(mine, mine, fin_s.at[m, k - 1], fin_r.at[m, k - 1], (peer, sh)).start()

    def strip(m, core):
        if m == 2:
            return go_t.at[rows16(core * 384, 384)]
        return (gf_o if m == 1 else gq_o).at[rows16(core * 48, 48)]

    def share_relay(m):
        for k in range(1, 8):
            peer = lax.rem(rep // 2 + 8 - k, 8) * 2 + c
            arrived(region(m, peer), fin_r.at[m, k - 1])
        remote(strip(m, c), strip(m, c), fin_s.at[m, 7], fin_r.at[m, 7], sibling).start()

    def share_finish(m):
        arrived(strip(m, 1 - c), fin_r.at[m, 7])

    def sums_drain(m):
        for k in range(3):
            for off in range(4):
                arrived(r0.at[0], c_s.at[(m * 3 + k) * 4 + off])
            for off in range(3):
                i = (m * 3 + k) * 3 + off
                arrived(r0.at[0], d_s.at[0, i])
                arrived(r2.at[0], d_s.at[1, i])
                arrived(r3.at[0], d_s.at[2, i])
        for k in range(7):
            arrived(region(m, rep), fin_s.at[m, k])
        arrived(strip(m, c), fin_s.at[m, 7])

    def vectors_start(stage):
        if stage == 0:
            remote(sg, sgr.at[12], t_s.at[9], t_r.at[9], sibling).start()
            return
        dim = stage - 1
        slot = dim * 4 + own[dim]
        sgr[pl.ds(slot, 1)] = sg[...].reshape(1, 16, 768)
        for off in (1, 2, 3):
            i = dim * 3 + off - 1
            remote(
                sgr.at[slot], sgr.at[slot], t_s.at[i], t_r.at[i], along(dim, ring(own[dim], off))
            ).start()

    def vectors_finish(stage):
        if stage == 0:
            arrived(sgr.at[12], t_r.at[9])
            arrived(sg, t_s.at[9])
            sg[...] = sg[...] + sgr[12]
            return
        dim = stage - 1
        for off in (1, 2, 3):
            i = dim * 3 + off - 1
            arrived(sgr.at[dim * 4 + ring(own[dim], -off)], t_r.at[i])
        sg[...] = (sgr[dim * 4] + sgr[dim * 4 + 1]) + (sgr[dim * 4 + 2] + sgr[dim * 4 + 3])

    gather_start(0)
    for k in range(1, 8):
        remote(
            smi, smr.at[sh], sm_s.at[k - 1], sm_r.at[k - 1], (rep, lax.rem(sh + k, 8))
        ).start()
    smr[pl.ds(sh, 1)] = smi[...].reshape(1, 16, 768)
    for k in range(1, 8):
        arrived(smr.at[lax.rem(sh + 8 - k, 8)], sm_r.at[k - 1])
    sm[...] = jnp.sum(smr[...].astype(F32), axis=0)
    for q in range(4):
        fbs[q] = jnp.broadcast_to(sm[8 + q : 9 + q, :], (8, 768))
    x_in = tok[...].astype(F32).reshape(256, 768)
    n1, rstd1 = normalize(x_in)
    a1 = n1 * sm[0:1, :] + sm[1:2, :]
    a1v[...] = a1.astype(BF)
    gather_relay_x(0)
    for m in range(1, 4):
        gather_start(m)
    gather_relay_z(0)
    gather_finish(0)
    gather_relay_x(1)

    for b in range(9):
        v = mm(a1v[...], wq[:, b * 256 : (b + 1) * 256])
        if b < 3:
            v = v + sm[2:3, b * 256 : (b + 1) * 256]
        if b >= 6:
            v = v + sm[3:4, (b - 6) * 256 : (b - 5) * 256]
        tmp[pl.ds(b * 512, 256)] = v[:, :128]
        tmp[pl.ds(b * 512 + 256, 256)] = v[:, 128:]

    def natural(which, b):
        return tmp[pl.ds((which * 6 + b) * 256, 256)]

    for which in range(3):
        put_groups(msg, which, [natural(which, PAIR[g]) for g in range(4)])
    exchange_start(msg, rcv, 0)
    packed = []
    for g in range(4):
        qb, kb = natural(0, SINGLE[g]), natural(1, SINGLE[g])
        packed.append(
            jnp.where(low, qb, roll_half(kb)) if g % 2 == 0 else jnp.where(low, roll_half(qb), kb)
        )
    put_groups(msg2, 0, packed)
    put_groups(msg2, 1, [natural(2, SINGLE[g]) for g in range(4)])
    exchange_start(msg2, rcv2, 4)
    gather_relay_x(2)
    exchange_wait(rcv, 0)
    gather_relay_x(3)

    zero = jnp.zeros((1024, 128), F32)

    def load_head(h, qq, kk, vv, mask, vmask):
        qh[h] = jnp.where(mask, qq * 0.125, zero).astype(BF)
        kh[h] = jnp.where(mask, kk, zero).astype(BF)
        vv = jnp.where(vmask, vv, zero)
        vh[h] = vv.astype(BF)
        turned[h] = jnp.transpose(vv).astype(BF)

    q01, k01, v01 = [get_positions(rcv, b) for b in range(3)]
    load_head(0, q01, k01, v01, low, low)
    load_head(1, q01, k01, v01, ~low, ~low)
    length = lens[me // 4]
    offsets = (0, 256, 768, 1536)
    tmp[pl.ds(0, 2048)] = jnp.zeros((2048, 128), F32)

    def attend(h, carry):
        for i in range(4):
            n = (i + 1) * 256
            s = mm_nt(kh[h, :n, :], qh[h, i * 256 : n, :])
            key = lax.broadcasted_iota(jnp.int32, (n, 256), 0)
            limit = lax.broadcasted_iota(jnp.int32, (1, 256), 1) + (i * 256 + 1)
            s = jnp.where(key < jnp.minimum(limit, length), s, MASKED)
            e = jnp.exp(s - jnp.max(s, axis=0, keepdims=True))
            p = (e * (1.0 / jnp.sum(e, axis=0, keepdims=True))).astype(BF)
            pmat[h, offsets[i] : offsets[i] + n, :] = p
            o = jnp.transpose(mm(turned[h, :, :n], p))
            tmp[pl.ds((h // 2) * 1024 + i * 256, 256)] += o
        return carry

    lax.fori_loop(0, 2, attend, 0)
    for m in (1, 2):
        gather_relay_z(m)
    exchange_wait(rcv2, 4)
    qks, vs = [get_positions(rcv2, b) for b in range(2)]
    load_head(2, qks, roll_half(qks), vs, low, here)
    lax.fori_loop(2, 3, attend, 0)
    put_positions(osnd, 0, tmp[pl.ds(0, 1024)])
    put_positions(osnd, 1, tmp[pl.ds(1024, 1024)])
    exchange_start(osnd, orcv, 1)
    for h in range(3):
        turned[h] = jnp.transpose(kh[h].astype(F32)).astype(BF)
    gather_relay_z(3)
    for m in range(1, 4):
        gather_finish(m)
    exchange_wait(orcv, 1)

    pairs, singles = get_groups(orcv, 0), get_groups(orcv, 1)
    blocks = [None] * 6
    for g in range(4):
        blocks[PAIR[g]] = pairs[g]
    blocks[1], blocks[4] = singles[0] + singles[1], singles[2] + singles[3]
    for b in range(6):
        ov[:, b * 128 : (b + 1) * 128] = blocks[b].astype(BF)
    x_in = tok[...].astype(F32).reshape(256, 768)
    g_in = cot[...].astype(F32).reshape(256, 768)
    y_mid = x_in + ALPHA * (mm(ov[...], wp[...]) + sm[4:5, :])
    yv[...] = y_mid
    n2, rstd2 = normalize(y_mid)
    a2 = n2 * sm[5:6, :] + sm[6:7, :]
    a2v[...] = a2.astype(BF)
    gm = (ALPHA * g_in).astype(BF)
    gmv[...] = gm
    gm = gm.astype(F32)
    sg[7:8, :] = column_sum(gm)
    lt1[...] = jnp.transpose(a2v[...].astype(F32)).astype(BF)
    lt2[...] = jnp.transpose(gm).astype(BF)
    acc1[...] = jnp.zeros((256, 768), F32)
    acc2[...] = jnp.zeros((256, 768), F32)

    def color(k, ux, uy, uz):
        order = ((ux, uy, uz), (uy, uz, ux), (uz, ux, uy))[k]
        return order[0], order[1] * 4 + order[2]

    def put_columns(m, q, v, first, shards):
        uy, zq = lax.rem(q, 4), q // 4
        for s in range(first, first + shards):
            for core in range(2):
                for k in range(3):
                    r = (s - first) * 96 + core * 48 + k * 16
                    a, u = color(k, s % 4, uy, zq * 2 + s // 4)
                    gall[core, m * 12 + k * 4 + a, u] = v[r : r + 16]

    def put_rows(m, q, v, core):
        ux, zq = lax.rem(q, 4), q // 4
        for e in range(8):
            for k in range(3):
                r = e * 48 + k * 16
                a, u = color(k, ux, e % 4, (e // 4) * 2 + zq)
                gall[core, m * 12 + k * 4 + a, u] = v[r : r + 16]

    def feed(p, carry):
        left, right = 2 * p, 2 * p + 1
        w1 = jnp.concatenate([wf[q].reshape(768, 384) for q in (left, right)], axis=1)
        w2 = jnp.concatenate(
            [
                jnp.concatenate([wo[q, h * 24 : h * 24 + 24].reshape(384, 384) for h in (0, 1)], axis=1)
                for q in (left, right)
            ],
            axis=0,
        )
        u = mm(a2v[...], w1) + fbs[p, 0:1, :]
        uu = u * u
        t = jnp.tanh(ROOT * (u + CUBE * (u * uu)))
        hv[0] = (0.5 * u * (1.0 + t)).astype(BF)
        slope = 0.5 * (1.0 + t) + 0.5 * u * (1.0 - t * t) * (ROOT * (1.0 + (3.0 * CUBE) * uu))
        gu = (mm_nt(gmv[...], w2) * slope).astype(BF)
        hv[1] = gu
        fbg[p] = jnp.broadcast_to(column_sum(gu.astype(F32)), (8, 768))
        acc1[...] += mm(hv[0], w2)
        acc2[...] += mm_nt(hv[1], w1)
        for half in (0, 1):
            v = mm(lt1[half * 384 : half * 384 + 384, :], hv[1]).astype(BF)
            put_columns(1, left, v[:, 0:384], half * 4, 4)
            put_columns(1, right, v[:, 384:768], half * 4, 4)
            v = mm(lt2[half * 384 : half * 384 + 384, :], hv[0]).astype(BF)
            put_rows(2, left, v[:, 0:384], half)
            put_rows(2, right, v[:, 384:768], half)
        return carry

    lax.fori_loop(0, 4, feed, 0)
    core_start(1)
    core_start(2)
    block = yv[...] + ALPHA * (acc1[...] + sm[7:8, :])
    bo[...] = block.reshape(32, 8, 768).astype(BF)
    for q in range(4):
        sg[8 + q : 9 + q, :] = fbg[q, 0:1, :]
    sg[12:16, :] = jnp.zeros((4, 768), F32)
    n2, rstd2 = normalize(yv[...])
    ga2 = acc2[...]
    sg[5:6, :] = column_sum(ga2 * n2)
    sg[6:7, :] = column_sum(ga2)
    gyy = cot[...].astype(F32).reshape(256, 768) + norm_back(n2, rstd2, ga2 * sm[5:6, :])
    acc1[...] = gyy
    ga = (ALPHA * gyy).astype(BF)
    a2v[...] = ga
    sg[4:5, :] = column_sum(ga.astype(F32))
    lt1[...] = jnp.transpose(ov[...].astype(F32)).astype(BF)
    for half in (0, 1):
        v = mm(lt1[half * 384 : half * 384 + 384, :], a2v[...]).astype(BF)
        put_columns(0, 6, v[:, 0:384], half * 4, 4)
        put_columns(0, 7, v[:, 384:768], half * 4, 4)
    go = mm_nt(a2v[...], wp[...])
    exchange_drain(osnd, 1)
    for m in range(4):
        gather_drain(m)
    put_groups(osnd, 0, [go[:, PAIR[g] * 128 : PAIR[g] * 128 + 128] for g in range(4)])
    put_groups(osnd, 1, [go[:, SINGLE[g] * 128 : SINGLE[g] * 128 + 128] for g in range(4)])
    exchange_start(osnd, grcv, 2)
    lt1[...] = jnp.transpose(a1v[...].astype(F32)).astype(BF)
    exchange_wait(grcv, 2)

    stage1_start(1)
    go01, gos = get_positions(grcv, 0), get_positions(grcv, 1)
    goh[0] = jnp.where(low, go01, zero).astype(BF)
    goh[1] = jnp.where(low, zero, go01).astype(BF)
    goh[2] = jnp.where(here, gos, zero).astype(BF)
    tmp[...] = jnp.zeros((6144, 128), F32)

    def attend_back(h, carry):
        base = (h // 2) * 1024
        for i in range(4):
            n = (i + 1) * 256
            g_rows = goh[h, i * 256 : n, :]
            p = pmat[h, offsets[i] : offsets[i] + n, :]
            pf = p.astype(F32)
            gp = mm_nt(vh[h, :n, :], g_rows)
            inner = jnp.sum(pf * gp, axis=0, keepdims=True)
            gs = (pf * (gp - inner)).astype(BF)
            tmp[pl.ds(base + i * 256, 256)] += jnp.transpose(mm(turned[h, :, :n], gs)) * 0.125
            tmp[pl.ds(2048 + base, n)] += mm(gs, qh[h, i * 256 : n, :])
            tmp[pl.ds(4096 + base, n)] += mm(p, g_rows)
        return carry

    lax.fori_loop(0, 2, attend_back, 0)
    exchange_drain(msg, 0)
    for b in range(3):
        put_positions(msg, b, tmp[pl.ds(b * 2048, 1024)])
    exchange_start(msg, rcv, 3)
    lax.fori_loop(2, 3, attend_back, 0)
    exchange_drain(msg2, 4)
    put_positions(msg2, 0, tmp[pl.ds(1024, 1024)] + roll_half(tmp[pl.ds(3072, 1024)]))
    put_positions(msg2, 1, tmp[pl.ds(5120, 1024)])
    exchange_start(msg2, rcv2, 5)
    stage2_start(1)
    exchange_wait(rcv, 3)
    exchange_wait(rcv2, 5)
    stage1_start(2)

    got = [get_groups(rcv, b) for b in range(3)] + [get_groups(rcv2, b) for b in range(2)]
    for which in range(3):
        blocks = [None] * 6
        for g in range(4):
            blocks[PAIR[g]] = got[which][g]
        for b, e, o in ((1, 0, 1), (4, 2, 3)):
            if which == 0:
                blocks[b] = jnp.where(low, got[3][e], roll_half(got[3][o]))
            elif which == 1:
                blocks[b] = jnp.where(low, roll_half(got[3][e]), got[3][o])
            else:
                blocks[b] = got[4][e] + got[4][o]
        for b in range(6):
            at = which * 768 + b * 128
            g3[:, at : at + 128] = blocks[b].astype(BF)
            if which != 1:
                row = 2 if which == 0 else 3
                sg[row : row + 1, b * 128 : b * 128 + 128] = column_sum(blocks[b])

    def qkv_grad(p, carry):
        cols = g3[:, pl.ds(pl.multiple_of(p * 768, 128), 768)]
        for half in (0, 1):
            v = mm(lt1[half * 384 : half * 384 + 384, :], cols).astype(BF)
            put_columns(0, 2 * p, v[:, 0:384], half * 4, 4)
            put_columns(0, 2 * p + 1, v[:, 384:768], half * 4, 4)
        return carry

    lax.fori_loop(0, 3, qkv_grad, 0)
    core_start(0)
    ga1 = mm_nt(g3[...], wq[...])
    n1, rstd1 = normalize(tok[...].astype(F32).reshape(256, 768))
    sg[0:1, :] = column_sum(ga1 * n1)
    sg[1:2, :] = column_sum(ga1)
    gx = acc1[...] + norm_back(n1, rstd1, ga1 * sm[0:1, :])
    ig[...] = gx.reshape(32, 8, 768).astype(BF)

    vectors_start(0)
    stage3_start(1)
    stage2_start(2)
    stage1_start(0)
    vectors_finish(0)
    vectors_start(1)
    stage3_start(2)
    share_start(1)
    stage2_start(0)
    vectors_finish(1)
    vectors_start(2)
    share_start(2)
    share_relay(1)
    stage3_start(0)
    vectors_finish(2)
    vectors_start(3)
    share_relay(2)
    share_start(0)
    vectors_finish(3)
    lead = pltpu.roll(sg[0:8, :], lax.rem(8 - sh, 8) * 96, 1)
    sgo[...] = lead[:, 0:128]
    wide = column_sum(
        jnp.where(lax.broadcasted_iota(jnp.int32, (4, 768), 0) == sh // 2, sg[8:12, :], 0.0)
    )
    fbo[...] = jnp.where(lax.rem(sh, 2) == 0, wide[:, 0:384], wide[:, 384:768])
    share_relay(0)
    for m in range(3):
        share_finish(m)

    for k in range(7):
        arrived(smi, sm_s.at[k])
    exchange_drain(osnd, 2)
    exchange_drain(msg, 3)
    exchange_drain(msg2, 5)
    for m in range(3):
        sums_drain(m)
    for i in range(9):
        arrived(sgr.at[0], t_s.at[i])


def block_step(tok, cot, lens, smi, wq_s, wp_s, wf_s, wo_s):
    vmem = pl.BlockSpec(memory_space=pltpu.VMEM)
    smem = pl.BlockSpec(memory_space=pltpu.SMEM)
    anywhere = pl.BlockSpec(memory_space=pl.ANY)
    V, D = pltpu.VMEM, pltpu.SemaphoreType.DMA
    return pl.pallas_call(
        block_kernel,
        name="block",
        out_shape=(
            jax.ShapeDtypeStruct((32, 8, 768), BF),
            jax.ShapeDtypeStruct((32, 8, 768), BF),
            jax.ShapeDtypeStruct((96, 3072), BF),
            jax.ShapeDtypeStruct((96, 3072), BF),
            jax.ShapeDtypeStruct((768, 384), BF),
            jax.ShapeDtypeStruct((8, 128), F32),
            jax.ShapeDtypeStruct((1, 384), F32),
        ),
        in_specs=[vmem, vmem, smem, vmem, anywhere, anywhere, anywhere, anywhere],
        out_specs=(vmem,) * 7,
        scratch_shapes=[
            V((768, 2304), BF),
            V((768, 768), BF),
            V((8, 48, 16, 384), BF),
            V((8, 48, 16, 384), BF),
            V((2, 36, 16, 16, 384), BF),
            V((24, 16, 16, 384), BF),
            V((27, 4, 16, 384), BF),
            V((27, 16, 384), BF),
            V((3, 2560, 256), BF),
            V((3, 1024, 128), BF),
            V((3, 1024, 128), BF),
            V((3, 1024, 128), BF),
            V((3, 1024, 128), BF),
            V((3, 128, 1024), BF),
            V((128, 8, 384), BF),
            V((128, 8, 256), BF),
            V((128, 8, 384), BF),
            V((128, 8, 256), BF),
            V((128, 8, 256), BF),
            V((128, 8, 256), BF),
            V((128, 8, 256), BF),
            V((6144, 128), F32),
            V((256, 768), F32),
            V((256, 768), F32),
            V((256, 768), F32),
            V((8, 16, 768), BF),
            V((16, 768), F32),
            V((4, 8, 768), F32),
            V((4, 8, 768), F32),
            V((16, 768), F32),
            V((13, 16, 768), F32),
            V((256, 768), BF),
            V((256, 768), BF),
            V((256, 768), BF),
            V((768, 256), BF),
            V((768, 256), BF),
            V((256, 768), BF),
            V((256, 2304), BF),
            V((2, 256, 768), BF),
            D((4, 28)), D((4, 28)), D((4, 8)),
            D((7,)), D((7,)),
            D((6,)), D((6,)),
            D((36,)), D((36,)),
            D((3, 27)), D((3, 27)),
            D((3, 8)), D((3, 8)),
            D((10,)), D((10,)),
        ],
        compiler_params=pltpu.CompilerParams(
            collective_id=0, has_side_effects=True, vmem_limit_bytes=64 * 2**20
        ),
    )(tok, cot, lens, smi, wq_s, wp_s, wf_s, wo_s)


def per_device(
    tokens,
    out_grad,
    lengths,
    ln1_gain,
    ln1_bias,
    w_qkv,
    q_bias,
    v_bias,
    w_proj,
    proj_bias,
    ln2_gain,
    ln2_bias,
    w_fc,
    fc_bias,
    w_out,
    out_bias,
):
    sh = lax.axis_index("shard")
    vectors = jnp.stack(
        [ln1_gain, ln1_bias, q_bias, v_bias, proj_bias, ln2_gain, ln2_bias, out_bias]
    )
    column = lax.broadcasted_iota(jnp.int32, (8, 768), 1)
    vectors = jnp.where(column // 96 == sh, jnp.tile(vectors, (1, 8)), jnp.zeros((), BF))
    place384 = lax.broadcasted_iota(jnp.int32, (8, 768), 0) * 2 + column // 384
    wide = jnp.where(place384 == sh, jnp.tile(fc_bias[None, :], (8, 2)), jnp.zeros((), BF))
    smi = jnp.concatenate([vectors, wide], axis=0)
    wf_s = w_fc.reshape(6, 16, 3072)
    wo_s = w_out.reshape(24, 16, 768)
    block, in_grad, gq, gf, gt, rows, d_fb = block_step(
        tokens, out_grad, lengths, smi, w_qkv, w_proj, wf_s, wo_s
    )
    rows = rows[:, :96]
    return (
        block,
        in_grad,
        rows[0],
        rows[1],
        gq[:, :2304].astype(F32),
        rows[2],
        rows[3],
        gq[:, 2304:].astype(F32),
        rows[4],
        rows[5],
        rows[6],
        gf.astype(F32),
        d_fb[0],
        gt.astype(F32).T,
        rows[7],
    )


def solution(mesh):
    pieces = P(None, ("rep", "shard"), None)
    row, table = P("shard"), P("shard", None)
    kinds = (row, row, table, row, row, table, row, row, row, table, row, table, row)
    return jax.shard_map(
        per_device,
        mesh=mesh,
        in_specs=(pieces, pieces, P(), *kinds),
        out_specs=(pieces, pieces, *kinds),
        check_vma=False,
    )
```

```python
import functools
import math

import jax
import jax.numpy as jnp
from jax import lax
from jax.experimental import pallas as pl
from jax.experimental.pallas import tpu as pltpu
from jax.sharding import PartitionSpec as P

HEADS = 12
LAYERS = 12
EPSILON = 1e-05
MASKED = -1e30
MESH = pl.DeviceIdType.MESH
BF = jnp.bfloat16
F32 = jnp.float32
ALPHA = 1.0 / math.sqrt(LAYERS)
ROOT = math.sqrt(2.0 / math.pi)
CUBE = 0.044715
NT = (((1,), (1,)), ((), ()))
PAIR = (0, 2, 3, 5)
SINGLE = (1, 1, 4, 4)


def mm(a, b):
    return jnp.dot(a, b, preferred_element_type=F32)


def mm_nt(a, b):
    return lax.dot_general(a, b, NT, preferred_element_type=F32)


def mean(v):
    return jnp.mean(v, axis=-1, keepdims=True)


def normalize(v):
    centered = v - mean(v)
    rstd = lax.rsqrt(mean(centered * centered) + EPSILON)
    return centered * rstd, rstd


def norm_back(n, rstd, r):
    return (r - mean(r) - n * mean(r * n)) * rstd


def column_sum(v):
    return jnp.sum(v, axis=0, keepdims=True)


def roll_half(v):
    return pltpu.roll(v, 64, 1)


def place(x, y, z, c):
    return (y * 4 + (z // 2) * 2 + c, lax.rem(z, 2) * 4 + x)


def remote(src, dst, send, recv, device):
    return pltpu.make_async_remote_copy(
        src_ref=src, dst_ref=dst, send_sem=send, recv_sem=recv, device_id=device, device_id_type=MESH
    )


def arrived(ref, sem):
    pltpu.make_async_copy(ref, ref, sem).wait()


def block_kernel(
    tok, cot, lens, smi, wq_s, wp_s, wf_s, wo_s,
    bo, ig, gq_o, gf_o, go_t, sgo, fbo,
    wq, wp, wf, wo, gall, r0, r2, r3, pmat, qh, kh, vh, goh, turned, msg, msg2, rcv, rcv2, osnd, orcv, grcv, tmp,
    yv, acc1, acc2, smr, sm, fbs, fbg, sg, sgr, a1v, a2v, gmv, lt1, lt2, ov, g3, hv,
    ag_s, ag_r, ag_l, sm_s, sm_r, aa_s, aa_r, c_s, c_r, d_s, d_r, fin_s, fin_r, t_s, t_r,
):
    rep, sh = lax.axis_index("rep"), lax.axis_index("shard")
    me = rep * 8 + sh
    x, zl, y, c = lax.rem(sh, 4), sh // 4, rep // 4, lax.rem(rep, 2)
    z = lax.rem(rep // 2, 2) * 2 + zl
    sibling = place(x, y, z, 1 - c)

    def ring(v, k):
        return lax.rem(v + k + 4, 4)

    def along(dim, value):
        return place(*[value if d == dim else v for d, v in enumerate((x, y, z))], c)

    own = (x, y, z)

    barrier = pltpu.get_barrier_semaphore()

    def greet(step, carry):
        peer = lax.rem(me + step, 128)
        pl.semaphore_signal(
            barrier, inc=1, device_id=(peer // 8, lax.rem(peer, 8)), device_id_type=MESH
        )
        return carry

    lax.fori_loop(1, 128, greet, 0)
    pl.semaphore_wait(barrier, 127)

    def rows16(start, size):
        return pl.ds(pl.multiple_of(start, 16), size)

    def gathered(m, s, core, h):
        if m == 0:
            return wq.at[rows16(s * 96 + core * 48, 48), pl.ds(h * 1152, 1152)]
        if m == 1:
            return wp.at[rows16(s * 96 + core * 48, 48), pl.ds(h * 384, 384)]
        if m == 2:
            return wf.at[pl.ds(h * 4, 4), pl.ds(s * 6 + core * 3, 3)]
        return wo.at[s, pl.ds(h * 24 + core * 12, 12)]

    def shard_of(m, core, h):
        if m == 0:
            return wq_s.at[rows16(core * 48, 48), pl.ds(h * 1152, 1152)]
        if m == 1:
            return wp_s.at[rows16(core * 48, 48), pl.ds(h * 384, 384)]
        return gathered(m, sh, core, h)

    def from_x(k):
        return zl * 4 + ring(x, -k)

    def from_z(j):
        return (1 - zl) * 4 + ring(x, -j)

    def own_copies(m):
        if m == 2:
            return [
                pltpu.make_async_copy(
                    wf_s.at[:, :, pl.ds(q * 384, 384)], wf.at[q, pl.ds(sh * 6, 6)], ag_l.at[m, q]
                )
                for q in range(8)
            ]
        if m == 3:
            return [
                pltpu.make_async_copy(
                    wo_s.at[:, :, pl.ds(h * 384, 384)], wo.at[sh, pl.ds(h * 24, 24)], ag_l.at[m, h]
                )
                for h in (0, 1)
            ]
        return [
            pltpu.make_async_copy(
                shard_of(m, core, h), gathered(m, sh, core, h), ag_l.at[m, core * 2 + h]
            )
            for core in (0, 1)
            for h in (0, 1)
        ]

    def beside(h):
        return along(2, ring(z, 1 - 2 * h))

    def gather_start(m):
        for copy in own_copies(m):
            copy.start()
        if m >= 2:
            for copy in own_copies(m):
                copy.wait()
        for h in (0, 1):
            remote(
                shard_of(m, c, h), gathered(m, sh, c, h), ag_s.at[m, 6 + h], ag_r.at[m, 6 + h], beside(h)
            ).start()
            for k in (1, 3):
                i = (k - 1) * 2 + h
                remote(
                    shard_of(m, c, h), gathered(m, sh, c, h), ag_s.at[m, i], ag_r.at[m, i],
                    along(0, ring(x, k)),
                ).start()

    def gather_relay_x(m, pieces=((1, 0), (3, 1), (1, 1), (3, 0), (2, 0), (2, 1))):
        for k, h in pieces:
            i = (k - 1) * 2 + h
            piece = gathered(m, from_x(k), c, h)
            arrived(piece, ag_r.at[m, i])
            if (k, h) in ((1, 0), (3, 1)):
                remote(
                    piece, piece, ag_s.at[m, 2 + h], ag_r.at[m, 2 + h], along(0, ring(x, 1 - 2 * h))
                ).start()
            i = 6 + 2 * k + h
            remote(piece, piece, ag_s.at[m, i], ag_r.at[m, i], beside(h)).start()
            i = 14 + (k - 1) * 2 + h
            remote(piece, piece, ag_s.at[m, i], ag_r.at[m, i], sibling).start()

    def gather_relay_z(m):
        for j in (0, 1, 3, 2):
            for h in (0, 1):
                piece = gathered(m, from_z(j), c, h)
                arrived(piece, ag_r.at[m, 6 + 2 * j + h])
                i = 20 + 2 * j + h
                remote(piece, piece, ag_s.at[m, i], ag_r.at[m, i], sibling).start()

    def gather_finish(m):
        if m < 2:
            for copy in own_copies(m):
                copy.wait()
        for h in (0, 1):
            for k in (1, 2, 3):
                arrived(gathered(m, from_x(k), 1 - c, h), ag_r.at[m, 14 + (k - 1) * 2 + h])
            for j in range(4):
                arrived(gathered(m, from_z(j), 1 - c, h), ag_r.at[m, 20 + 2 * j + h])

    def gather_drain(m):
        for h in (0, 1):
            for i in range(0, 28, 2):
                arrived(gathered(m, 0, 0, h), ag_s.at[m, i + h])

    def exchange_start(src, dst, i):
        def send(step, carry):
            peer = lax.rem(me + step, 128)
            remote(
                src.at[peer], dst.at[me], aa_s.at[i], aa_r.at[i], (peer // 8, lax.rem(peer, 8))
            ).start()
            return carry

        lax.fori_loop(1, 128, send, 0)
        dst[pl.ds(me, 1)] = src[pl.ds(me, 1)]

    def exchange_wait(dst, i):
        most = dst.at[pl.ds(0, 127)]
        arrived(most, aa_r.at[i])

    def exchange_drain(src, i):
        most = src.at[pl.ds(0, 127)]
        arrived(most, aa_s.at[i])

    lane = lax.broadcasted_iota(jnp.int32, (1, 128), 1)
    low = lane < 64
    half = lax.rem(me, 2)
    here = (lane >= half * 64) & (lane < half * 64 + 64)

    def lanes(i, count=1):
        return pl.ds(i * 128, count * 128)

    def put_groups(dst, b, per_group):
        stacked = jnp.stack([g.reshape(32, 8, 128) for g in per_group], axis=1)
        dst[:, :, b * 128 : (b + 1) * 128] = stacked.reshape(128, 8, 128).astype(BF)

    def get_groups(src, b):
        v = src[:, :, b * 128 : (b + 1) * 128].astype(F32).reshape(32, 4, 8, 128)
        return [v[:, g].reshape(256, 128) for g in range(4)]

    def put_positions(dst, b, v):
        dst[:, :, b * 128 : (b + 1) * 128] = v.reshape(128, 8, 128).astype(BF)

    def get_positions(src, b):
        return src[:, :, b * 128 : (b + 1) * 128].astype(F32).reshape(1024, 128)

    def block0(m, k, a):
        if m == 0:
            i = k * 4 + a
            return wo.at[i // 3, pl.ds(lax.rem(i, 3) * 16, 16)]
        return r0.at[(m - 1) * 12 + k * 4 + a]

    def block1(m, k, off):
        i = k * 3 + off - 1
        if m == 0:
            return wo.at[4 + i // 3, pl.ds((i % 3) * 16, 16)]
        return wf.at[(m - 1) * 4 + i // 3, pl.ds((i % 3) * 16, 16)]

    def core_start(m):
        for off in (1, 2, 3, 0):
            for k in range(3):
                a = ring(own[k], off)
                i = (m * 3 + k) * 4 + off
                remote(
                    gall.at[1 - c, m * 12 + k * 4 + a], block0(m, k, a), c_s.at[i], c_r.at[i], sibling
                ).start()

    def stage1_start(m):
        for off in (1, 2, 3):
            for k in range(3):
                a = ring(own[k], off)
                i = (m * 3 + k) * 4 + off
                arrived(block0(m, k, a), c_r.at[i])
                mine = gall.at[c, m * 12 + k * 4 + a]
                mine[...] = mine[...] + block0(m, k, a)[...]
                i = (m * 3 + k) * 3 + off - 1
                remote(
                    mine, block1(m, k, off), d_s.at[0, i], d_r.at[0, i], along(k, a)
                ).start()

    def stage2_start(m):
        for k in range(3):
            a = own[k]
            arrived(block0(m, k, a), c_r.at[(m * 3 + k) * 4])
            mine = gall.at[c, m * 12 + k * 4 + a]
            total = mine[...].astype(F32) + block0(m, k, a)[...].astype(F32)
            for off in (1, 2, 3):
                i = (m * 3 + k) * 3 + off - 1
                arrived(block1(m, k, off), d_r.at[0, i])
                total = total + block1(m, k, off)[...].astype(F32)
            mine[...] = total.astype(BF)
            dim = (k + 1) % 3
            for off in (1, 2, 3):
                i = (m * 3 + k) * 3 + off - 1
                b = ring(own[dim], off)
                remote(
                    mine.at[pl.ds(b * 4, 4)], r2.at[i], d_s.at[1, i], d_r.at[1, i], along(dim, b)
                ).start()

    def stage3_start(m):
        for k in range(3):
            mine = gall.at[c, m * 12 + k * 4 + own[k], pl.ds(own[(k + 1) % 3] * 4, 4)]
            total = mine[...].astype(F32)
            for off in (1, 2, 3):
                i = (m * 3 + k) * 3 + off - 1
                arrived(r2.at[i], d_r.at[1, i])
                total = total + r2[i].astype(F32)
            mine[...] = total.astype(BF)
            dim = (k + 2) % 3
            for off in (1, 2, 3):
                i = (m * 3 + k) * 3 + off - 1
                e = ring(own[dim], off)
                remote(mine.at[e], r3.at[i], d_s.at[2, i], d_r.at[2, i], along(dim, e)).start()

    def region(m, r):
        part, core = lax.rem(r // 2, 2) * 4 + r // 4, lax.rem(r, 2)
        if m == 2:
            return go_t.at[rows16(core * 384 + part * 48, 48)]
        out = gf_o if m == 1 else gq_o
        return out.at[rows16(core * 48, 48), pl.ds(pl.multiple_of(part * 384, 128), 384)]

    def share_start(m):
        for k in range(3):
            u = own[(k + 1) % 3] * 4 + own[(k + 2) % 3]
            total = gall[c, m * 12 + k * 4 + own[k], u].astype(F32)
            for off in (1, 2, 3):
                i = (m * 3 + k) * 3 + off - 1
                arrived(r3.at[i], d_r.at[2, i])
                total = total + r3[i].astype(F32)
            region(m, rep).at[pl.ds(k * 16, 16), :][...] = total.astype(BF)
        mine = region(m, rep)
        for k in range(1, 8):
            peer = lax.rem(rep // 2 + k, 8) * 2 + c
            remote(mine, mine, fin_s.at[m, k - 1], fin_r.at[m, k - 1], (peer, sh)).start()

    def strip(m, core):
        if m == 2:
            return go_t.at[rows16(core * 384, 384)]
        return (gf_o if m == 1 else gq_o).at[rows16(core * 48, 48)]

    def share_relay(m):
        for k in range(1, 8):
            peer = lax.rem(rep // 2 + 8 - k, 8) * 2 + c
            arrived(region(m, peer), fin_r.at[m, k - 1])
        remote(strip(m, c), strip(m, c), fin_s.at[m, 7], fin_r.at[m, 7], sibling).start()

    def share_finish(m):
        arrived(strip(m, 1 - c), fin_r.at[m, 7])

    def sums_drain(m):
        for k in range(3):
            for off in range(4):
                arrived(r0.at[0], c_s.at[(m * 3 + k) * 4 + off])
            for off in range(3):
                i = (m * 3 + k) * 3 + off
                arrived(r0.at[0], d_s.at[0, i])
                arrived(r2.at[0], d_s.at[1, i])
                arrived(r3.at[0], d_s.at[2, i])
        for k in range(7):
            arrived(region(m, rep), fin_s.at[m, k])
        arrived(strip(m, c), fin_s.at[m, 7])

    def vectors_start(stage):
        if stage == 0:
            remote(sg, sgr.at[12], t_s.at[9], t_r.at[9], sibling).start()
            return
        dim = stage - 1
        slot = dim * 4 + own[dim]
        sgr[pl.ds(slot, 1)] = sg[...].reshape(1, 16, 768)
        for off in (1, 2, 3):
            i = dim * 3 + off - 1
            remote(
                sgr.at[slot], sgr.at[slot], t_s.at[i], t_r.at[i], along(dim, ring(own[dim], off))
            ).start()

    def vectors_finish(stage):
        if stage == 0:
            arrived(sgr.at[12], t_r.at[9])
            arrived(sg, t_s.at[9])
            sg[...] = sg[...] + sgr[12]
            return
        dim = stage - 1
        for off in (1, 2, 3):
            i = dim * 3 + off - 1
            arrived(sgr.at[dim * 4 + ring(own[dim], -off)], t_r.at[i])
        sg[...] = (sgr[dim * 4] + sgr[dim * 4 + 1]) + (sgr[dim * 4 + 2] + sgr[dim * 4 + 3])

    near, far = ((1, 0), (3, 1), (1, 1), (3, 0)), ((2, 0), (2, 1))

    gather_start(0)
    for k in range(1, 8):
        remote(
            smi, smr.at[sh], sm_s.at[k - 1], sm_r.at[k - 1], (rep, lax.rem(sh + k, 8))
        ).start()
    smr[pl.ds(sh, 1)] = smi[...].reshape(1, 16, 768)
    for k in range(1, 8):
        arrived(smr.at[lax.rem(sh + 8 - k, 8)], sm_r.at[k - 1])
    sm[...] = jnp.sum(smr[...].astype(F32), axis=0)
    for q in range(4):
        fbs[q] = jnp.broadcast_to(sm[8 + q : 9 + q, :], (8, 768))
    x_in = tok[...].astype(F32).reshape(256, 768)
    n1, rstd1 = normalize(x_in)
    a1 = n1 * sm[0:1, :] + sm[1:2, :]
    a1v[...] = a1.astype(BF)
    gather_relay_x(0)
    for m in range(1, 4):
        gather_start(m)
    gather_relay_z(0)
    gather_finish(0)
    gather_relay_x(1, near)

    for b in range(9):
        v = mm(a1v[...], wq[:, b * 256 : (b + 1) * 256])
        if b < 3:
            v = v + sm[2:3, b * 256 : (b + 1) * 256]
        if b >= 6:
            v = v + sm[3:4, (b - 6) * 256 : (b - 5) * 256]
        tmp[pl.ds(b * 512, 256)] = v[:, :128]
        tmp[pl.ds(b * 512 + 256, 256)] = v[:, 128:]

    def natural(which, b):
        return tmp[pl.ds((which * 6 + b) * 256, 256)]

    for which in range(3):
        put_groups(msg, which, [natural(which, PAIR[g]) for g in range(4)])
    exchange_start(msg, rcv, 0)
    gather_relay_x(1, far)
    gather_relay_x(2, near)
    packed = []
    for g in range(4):
        qb, kb = natural(0, SINGLE[g]), natural(1, SINGLE[g])
        packed.append(
            jnp.where(low, qb, roll_half(kb)) if g % 2 == 0 else jnp.where(low, roll_half(qb), kb)
        )
    put_groups(msg2, 0, packed)
    put_groups(msg2, 1, [natural(2, SINGLE[g]) for g in range(4)])
    exchange_start(msg2, rcv2, 4)
    gather_relay_x(2, far)
    gather_relay_x(3, near)
    exchange_wait(rcv, 0)
    gather_relay_x(3, far)

    zero = jnp.zeros((1024, 128), F32)

    def load_head(h, qq, kk, vv, mask, vmask):
        qh[h] = jnp.where(mask, qq * 0.125, zero).astype(BF)
        kh[h] = jnp.where(mask, kk, zero).astype(BF)
        vv = jnp.where(vmask, vv, zero)
        vh[h] = vv.astype(BF)
        turned[h] = jnp.transpose(vv).astype(BF)

    q01, k01, v01 = [get_positions(rcv, b) for b in range(3)]
    load_head(0, q01, k01, v01, low, low)
    load_head(1, q01, k01, v01, ~low, ~low)
    length = lens[me // 4]
    offsets = (0, 256, 768, 1536)
    tmp[pl.ds(0, 2048)] = jnp.zeros((2048, 128), F32)

    def attend(h, carry):
        for i in range(4):
            n = (i + 1) * 256
            s = mm_nt(kh[h, :n, :], qh[h, i * 256 : n, :])
            key = lax.broadcasted_iota(jnp.int32, (n, 256), 0)
            limit = lax.broadcasted_iota(jnp.int32, (1, 256), 1) + (i * 256 + 1)
            s = jnp.where(key < jnp.minimum(limit, length), s, MASKED)
            e = jnp.exp(s - jnp.max(s, axis=0, keepdims=True))
            p = (e * (1.0 / jnp.sum(e, axis=0, keepdims=True))).astype(BF)
            pmat[h, offsets[i] : offsets[i] + n, :] = p
            o = jnp.transpose(mm(turned[h, :, :n], p))
            tmp[pl.ds((h // 2) * 1024 + i * 256, 256)] += o
        return carry

    lax.fori_loop(0, 2, attend, 0)
    for m in (1, 2):
        gather_relay_z(m)
    exchange_wait(rcv2, 4)
    qks, vs = [get_positions(rcv2, b) for b in range(2)]
    load_head(2, qks, roll_half(qks), vs, low, here)
    lax.fori_loop(2, 3, attend, 0)
    put_positions(osnd, 0, tmp[pl.ds(0, 1024)])
    put_positions(osnd, 1, tmp[pl.ds(1024, 1024)])
    exchange_start(osnd, orcv, 1)
    for h in range(3):
        turned[h] = jnp.transpose(kh[h].astype(F32)).astype(BF)
    gather_relay_z(3)
    for m in range(1, 4):
        gather_finish(m)
    exchange_wait(orcv, 1)

    pairs, singles = get_groups(orcv, 0), get_groups(orcv, 1)
    blocks = [None] * 6
    for g in range(4):
        blocks[PAIR[g]] = pairs[g]
    blocks[1], blocks[4] = singles[0] + singles[1], singles[2] + singles[3]
    for b in range(6):
        ov[:, b * 128 : (b + 1) * 128] = blocks[b].astype(BF)
    x_in = tok[...].astype(F32).reshape(256, 768)
    g_in = cot[...].astype(F32).reshape(256, 768)
    y_mid = x_in + ALPHA * (mm(ov[...], wp[...]) + sm[4:5, :])
    yv[...] = y_mid
    n2, rstd2 = normalize(y_mid)
    a2 = n2 * sm[5:6, :] + sm[6:7, :]
    a2v[...] = a2.astype(BF)
    gm = (ALPHA * g_in).astype(BF)
    gmv[...] = gm
    gm = gm.astype(F32)
    sg[7:8, :] = column_sum(gm)
    lt1[...] = jnp.transpose(a2v[...].astype(F32)).astype(BF)
    lt2[...] = jnp.transpose(gm).astype(BF)
    acc1[...] = jnp.zeros((256, 768), F32)
    acc2[...] = jnp.zeros((256, 768), F32)

    def color(k, ux, uy, uz):
        order = ((ux, uy, uz), (uy, uz, ux), (uz, ux, uy))[k]
        return order[0], order[1] * 4 + order[2]

    def put_columns(m, q, v, first, shards):
        uy, zq = lax.rem(q, 4), q // 4
        for s in range(first, first + shards):
            for core in range(2):
                for k in range(3):
                    r = (s - first) * 96 + core * 48 + k * 16
                    a, u = color(k, s % 4, uy, zq * 2 + s // 4)
                    gall[core, m * 12 + k * 4 + a, u] = v[r : r + 16]

    def put_rows(m, q, v, core):
        ux, zq = lax.rem(q, 4), q // 4
        for e in range(8):
            for k in range(3):
                r = e * 48 + k * 16
                a, u = color(k, ux, e % 4, (e // 4) * 2 + zq)
                gall[core, m * 12 + k * 4 + a, u] = v[r : r + 16]

    def feed(p, carry):
        left, right = 2 * p, 2 * p + 1
        w1 = jnp.concatenate([wf[q].reshape(768, 384) for q in (left, right)], axis=1)
        w2 = jnp.concatenate(
            [
                jnp.concatenate([wo[q, h * 24 : h * 24 + 24].reshape(384, 384) for h in (0, 1)], axis=1)
                for q in (left, right)
            ],
            axis=0,
        )
        u = mm(a2v[...], w1) + fbs[p, 0:1, :]
        uu = u * u
        t = jnp.tanh(ROOT * (u + CUBE * (u * uu)))
        hv[0] = (0.5 * u * (1.0 + t)).astype(BF)
        slope = 0.5 * (1.0 + t) + 0.5 * u * (1.0 - t * t) * (ROOT * (1.0 + (3.0 * CUBE) * uu))
        gu = (mm_nt(gmv[...], w2) * slope).astype(BF)
        hv[1] = gu
        fbg[p] = jnp.broadcast_to(column_sum(gu.astype(F32)), (8, 768))
        acc1[...] += mm(hv[0], w2)
        acc2[...] += mm_nt(hv[1], w1)
        for half in (0, 1):
            v = mm(lt1[half * 384 : half * 384 + 384, :], hv[1]).astype(BF)
            put_columns(1, left, v[:, 0:384], half * 4, 4)
            put_columns(1, right, v[:, 384:768], half * 4, 4)
            v = mm(lt2[half * 384 : half * 384 + 384, :], hv[0]).astype(BF)
            put_rows(2, left, v[:, 0:384], half)
            put_rows(2, right, v[:, 384:768], half)
        return carry

    lax.fori_loop(0, 4, feed, 0)
    core_start(1)
    core_start(2)
    block = yv[...] + ALPHA * (acc1[...] + sm[7:8, :])
    bo[...] = block.reshape(32, 8, 768).astype(BF)
    for q in range(4):
        sg[8 + q : 9 + q, :] = fbg[q, 0:1, :]
    sg[12:16, :] = jnp.zeros((4, 768), F32)
    n2, rstd2 = normalize(yv[...])
    ga2 = acc2[...]
    sg[5:6, :] = column_sum(ga2 * n2)
    sg[6:7, :] = column_sum(ga2)
    gyy = cot[...].astype(F32).reshape(256, 768) + norm_back(n2, rstd2, ga2 * sm[5:6, :])
    acc1[...] = gyy
    ga = (ALPHA * gyy).astype(BF)
    a2v[...] = ga
    sg[4:5, :] = column_sum(ga.astype(F32))
    lt1[...] = jnp.transpose(ov[...].astype(F32)).astype(BF)
    for half in (0, 1):
        v = mm(lt1[half * 384 : half * 384 + 384, :], a2v[...]).astype(BF)
        put_columns(0, 6, v[:, 0:384], half * 4, 4)
        put_columns(0, 7, v[:, 384:768], half * 4, 4)
    go = mm_nt(a2v[...], wp[...])
    exchange_drain(osnd, 1)
    for m in range(4):
        gather_drain(m)
    put_groups(osnd, 0, [go[:, PAIR[g] * 128 : PAIR[g] * 128 + 128] for g in range(4)])
    put_groups(osnd, 1, [go[:, SINGLE[g] * 128 : SINGLE[g] * 128 + 128] for g in range(4)])
    exchange_start(osnd, grcv, 2)
    lt1[...] = jnp.transpose(a1v[...].astype(F32)).astype(BF)
    exchange_wait(grcv, 2)

    stage1_start(1)
    go01, gos = get_positions(grcv, 0), get_positions(grcv, 1)
    goh[0] = jnp.where(low, go01, zero).astype(BF)
    goh[1] = jnp.where(low, zero, go01).astype(BF)
    goh[2] = jnp.where(here, gos, zero).astype(BF)
    tmp[...] = jnp.zeros((6144, 128), F32)

    def attend_back(h, carry):
        base = (h // 2) * 1024
        for i in range(4):
            n = (i + 1) * 256
            g_rows = goh[h, i * 256 : n, :]
            p = pmat[h, offsets[i] : offsets[i] + n, :]
            pf = p.astype(F32)
            gp = mm_nt(vh[h, :n, :], g_rows)
            inner = jnp.sum(pf * gp, axis=0, keepdims=True)
            gs = (pf * (gp - inner)).astype(BF)
            tmp[pl.ds(base + i * 256, 256)] += jnp.transpose(mm(turned[h, :, :n], gs)) * 0.125
            tmp[pl.ds(2048 + base, n)] += mm(gs, qh[h, i * 256 : n, :])
            tmp[pl.ds(4096 + base, n)] += mm(p, g_rows)
        return carry

    lax.fori_loop(0, 2, attend_back, 0)
    exchange_drain(msg, 0)
    for b in range(3):
        put_positions(msg, b, tmp[pl.ds(b * 2048, 1024)])
    exchange_start(msg, rcv, 3)
    lax.fori_loop(2, 3, attend_back, 0)
    exchange_drain(msg2, 4)
    put_positions(msg2, 0, tmp[pl.ds(1024, 1024)] + roll_half(tmp[pl.ds(3072, 1024)]))
    put_positions(msg2, 1, tmp[pl.ds(5120, 1024)])
    exchange_start(msg2, rcv2, 5)
    stage2_start(1)
    exchange_wait(rcv, 3)
    exchange_wait(rcv2, 5)
    stage1_start(2)

    got = [get_groups(rcv, b) for b in range(3)] + [get_groups(rcv2, b) for b in range(2)]
    for which in range(3):
        blocks = [None] * 6
        for g in range(4):
            blocks[PAIR[g]] = got[which][g]
        for b, e, o in ((1, 0, 1), (4, 2, 3)):
            if which == 0:
                blocks[b] = jnp.where(low, got[3][e], roll_half(got[3][o]))
            elif which == 1:
                blocks[b] = jnp.where(low, roll_half(got[3][e]), got[3][o])
            else:
                blocks[b] = got[4][e] + got[4][o]
        for b in range(6):
            at = which * 768 + b * 128
            g3[:, at : at + 128] = blocks[b].astype(BF)
            if which != 1:
                row = 2 if which == 0 else 3
                sg[row : row + 1, b * 128 : b * 128 + 128] = column_sum(blocks[b])

    def qkv_grad(p, carry):
        cols = g3[:, pl.ds(pl.multiple_of(p * 768, 128), 768)]
        for half in (0, 1):
            v = mm(lt1[half * 384 : half * 384 + 384, :], cols).astype(BF)
            put_columns(0, 2 * p, v[:, 0:384], half * 4, 4)
            put_columns(0, 2 * p + 1, v[:, 384:768], half * 4, 4)
        return carry

    lax.fori_loop(0, 3, qkv_grad, 0)
    core_start(0)
    ga1 = mm_nt(g3[...], wq[...])
    n1, rstd1 = normalize(tok[...].astype(F32).reshape(256, 768))
    sg[0:1, :] = column_sum(ga1 * n1)
    sg[1:2, :] = column_sum(ga1)
    gx = acc1[...] + norm_back(n1, rstd1, ga1 * sm[0:1, :])
    ig[...] = gx.reshape(32, 8, 768).astype(BF)

    vectors_start(0)
    stage3_start(1)
    stage2_start(2)
    stage1_start(0)
    vectors_finish(0)
    vectors_start(1)
    stage3_start(2)
    share_start(1)
    stage2_start(0)
    vectors_finish(1)
    vectors_start(2)
    share_start(2)
    share_relay(1)
    stage3_start(0)
    vectors_finish(2)
    vectors_start(3)
    share_relay(2)
    share_start(0)
    vectors_finish(3)
    lead = pltpu.roll(sg[0:8, :], lax.rem(8 - sh, 8) * 96, 1)
    sgo[...] = lead[:, 0:128]
    wide = column_sum(
        jnp.where(lax.broadcasted_iota(jnp.int32, (4, 768), 0) == sh // 2, sg[8:12, :], 0.0)
    )
    fbo[...] = jnp.where(lax.rem(sh, 2) == 0, wide[:, 0:384], wide[:, 384:768])
    share_relay(0)
    for m in range(3):
        share_finish(m)

    for k in range(7):
        arrived(smi, sm_s.at[k])
    exchange_drain(osnd, 2)
    exchange_drain(msg, 3)
    exchange_drain(msg2, 5)
    for m in range(3):
        sums_drain(m)
    for i in range(9):
        arrived(sgr.at[0], t_s.at[i])


def block_step(tok, cot, lens, smi, wq_s, wp_s, wf_s, wo_s):
    vmem = pl.BlockSpec(memory_space=pltpu.VMEM)
    smem = pl.BlockSpec(memory_space=pltpu.SMEM)
    anywhere = pl.BlockSpec(memory_space=pl.ANY)
    V, D = pltpu.VMEM, pltpu.SemaphoreType.DMA
    return pl.pallas_call(
        block_kernel,
        name="block",
        out_shape=(
            jax.ShapeDtypeStruct((32, 8, 768), BF),
            jax.ShapeDtypeStruct((32, 8, 768), BF),
            jax.ShapeDtypeStruct((96, 3072), BF),
            jax.ShapeDtypeStruct((96, 3072), BF),
            jax.ShapeDtypeStruct((768, 384), BF),
            jax.ShapeDtypeStruct((8, 128), F32),
            jax.ShapeDtypeStruct((1, 384), F32),
        ),
        in_specs=[vmem, vmem, smem, vmem, anywhere, anywhere, anywhere, anywhere],
        out_specs=(vmem,) * 7,
        scratch_shapes=[
            V((768, 2304), BF),
            V((768, 768), BF),
            V((8, 48, 16, 384), BF),
            V((8, 48, 16, 384), BF),
            V((2, 36, 16, 16, 384), BF),
            V((24, 16, 16, 384), BF),
            V((27, 4, 16, 384), BF),
            V((27, 16, 384), BF),
            V((3, 2560, 256), BF),
            V((3, 1024, 128), BF),
            V((3, 1024, 128), BF),
            V((3, 1024, 128), BF),
            V((3, 1024, 128), BF),
            V((3, 128, 1024), BF),
            V((128, 8, 384), BF),
            V((128, 8, 256), BF),
            V((128, 8, 384), BF),
            V((128, 8, 256), BF),
            V((128, 8, 256), BF),
            V((128, 8, 256), BF),
            V((128, 8, 256), BF),
            V((6144, 128), F32),
            V((256, 768), F32),
            V((256, 768), F32),
            V((256, 768), F32),
            V((8, 16, 768), BF),
            V((16, 768), F32),
            V((4, 8, 768), F32),
            V((4, 8, 768), F32),
            V((16, 768), F32),
            V((13, 16, 768), F32),
            V((256, 768), BF),
            V((256, 768), BF),
            V((256, 768), BF),
            V((768, 256), BF),
            V((768, 256), BF),
            V((256, 768), BF),
            V((256, 2304), BF),
            V((2, 256, 768), BF),
            D((4, 28)), D((4, 28)), D((4, 8)),
            D((7,)), D((7,)),
            D((6,)), D((6,)),
            D((36,)), D((36,)),
            D((3, 27)), D((3, 27)),
            D((3, 8)), D((3, 8)),
            D((10,)), D((10,)),
        ],
        compiler_params=pltpu.CompilerParams(
            collective_id=0, has_side_effects=True, vmem_limit_bytes=64 * 2**20
        ),
    )(tok, cot, lens, smi, wq_s, wp_s, wf_s, wo_s)


def per_device(
    tokens,
    out_grad,
    lengths,
    ln1_gain,
    ln1_bias,
    w_qkv,
    q_bias,
    v_bias,
    w_proj,
    proj_bias,
    ln2_gain,
    ln2_bias,
    w_fc,
    fc_bias,
    w_out,
    out_bias,
):
    sh = lax.axis_index("shard")
    vectors = jnp.stack(
        [ln1_gain, ln1_bias, q_bias, v_bias, proj_bias, ln2_gain, ln2_bias, out_bias]
    )
    column = lax.broadcasted_iota(jnp.int32, (8, 768), 1)
    vectors = jnp.where(column // 96 == sh, jnp.tile(vectors, (1, 8)), jnp.zeros((), BF))
    place384 = lax.broadcasted_iota(jnp.int32, (8, 768), 0) * 2 + column // 384
    wide = jnp.where(place384 == sh, jnp.tile(fc_bias[None, :], (8, 2)), jnp.zeros((), BF))
    smi = jnp.concatenate([vectors, wide], axis=0)
    wf_s = w_fc.reshape(6, 16, 3072)
    wo_s = w_out.reshape(24, 16, 768)
    block, in_grad, gq, gf, gt, rows, d_fb = block_step(
        tokens, out_grad, lengths, smi, w_qkv, w_proj, wf_s, wo_s
    )
    rows = rows[:, :96]
    return (
        block,
        in_grad,
        rows[0],
        rows[1],
        gq[:, :2304].astype(F32),
        rows[2],
        rows[3],
        gq[:, 2304:].astype(F32),
        rows[4],
        rows[5],
        rows[6],
        gf.astype(F32),
        d_fb[0],
        gt.astype(F32).T,
        rows[7],
    )


def solution(mesh):
    pieces = P(None, ("rep", "shard"), None)
    row, table = P("shard"), P("shard", None)
    kinds = (row, row, table, row, row, table, row, row, row, table, row, table, row)
    return jax.shard_map(
        per_device,
        mesh=mesh,
        in_specs=(pieces, pieces, P(), *kinds),
        out_specs=(pieces, pieces, *kinds),
        check_vma=False,
    )
```
